32 devices in a mesh: row: 4 (over y, x), col: 8 (over z, core).
Axes of the slice: x: 2, y: 2, z: 4, core: 2. Of those that a mesh axis runs over, the one named last changes fastest.
Arguments:
- tokens: bfloat16 [9216, 2048], P(('row', 'col')), may hold values from -6 to 6
- cotangent: bfloat16 [9216, 2048], P(('row', 'col')), may hold values from -6 to 6
- segment_numbers: int32 [9216], P('row'), may hold values from 0 to 8, as said below
- positions: int32 [9216], P('row'), may hold values from 0 to 2095, as said below
- attention_norm_gain: float32 [2048], P(('row', 'col')), may hold values from 0.1 to 1.9
- query_matrix: float32 [2048, 2048], P(('row', 'col')), may hold values from -0.1875 to 0.1875
- key_value_matrix: float32 [2048, 512], P(('row', 'col')), may hold values from -0.125 to 0.125
- output_matrix: float32 [2048, 2048], P(('row', 'col')), may hold values from -1 to 1
- output_adapter_first: float32 [2048, 256], P(('row', 'col')), may hold values from -1 to 1
- output_adapter_second: float32 [256, 2048], P(('row', 'col')), may hold values from -0.375 to 0.375
- feedforward_norm_gain: float32 [2048], P(('row', 'col')), may hold values from 0.1 to 1.9
- gate_matrix: float32 [2048, 16384], P('row', 'col'), may hold values from -0.125 to 0.125
- up_matrix: float32 [2048, 16384], P('row', 'col'), may hold values from -0.125 to 0.125
- down_matrix: float32 [2048, 16384], P('row', 'col'), may hold values from -0.046875 to 0.046875
- down_adapter_first: float32 [256, 16384], P('row', 'col'), may hold values from -0.046875 to 0.046875
- down_adapter_second: float32 [256, 2048], P(('row', 'col')), may hold values from -0.375 to 0.375
Outputs:
- layer_out: bfloat16 [9216, 2048], P(('row', 'col'))
- input_grad: bfloat16 [9216, 2048], P(('row', 'col'))
- grad_norm_attn: float32 [2048], P(('row', 'col'))
- grad_w_query: float32 [2048, 2048], P(('row', 'col'))
- grad_w_keyval: float32 [2048, 512], P(('row', 'col'))
- grad_w_out: float32 [2048, 2048], P(('row', 'col'))
- grad_lora_out_a: float32 [2048, 256], P(('row', 'col'))
- grad_lora_out_b: float32 [256, 2048], P(('row', 'col'))
- grad_norm_mlp: float32 [2048], P(('row', 'col'))
- grad_w_gate: float32 [2048, 16384], P('row', 'col')
- grad_w_up: float32 [2048, 16384], P('row', 'col')
- grad_w_down: float32 [2048, 16384], P('row', 'col')
- grad_lora_down_a: float32 [256, 16384], P('row', 'col')
- grad_lora_down_b: float32 [256, 2048], P(('row', 'col'))
The draws below stay inside these ranges and needn't reach their ends.
Inputs may be any that keep to these rules, and one draw needn't show every extreme that they name: `segment_numbers`: in each block of 2304 tokens the first 2048 have id 0, the rest form 8 contiguous continuations with ids 1 to 8 in order, each of 16 to 48 tokens, one of exactly 48. `positions`: A prompt token's position is its index in the prompt; a continuation token's is 2048 plus its index in its continuation.
All inputs are finite; a program needn't handle non-finite values.
Results may differ from the reference program's by a relative error of at most 0.02.
The reference program's roundings to bfloat16 on the way count: a program that leaves them out, or rounds other values in their place, can miss the bound.
Values may be sent and summed in bfloat16 or wider, within the bound.
No kernel may reach another device: no remote copies, remote signals or barrier semaphores. Data moves between devices by JAX's collectives and lax.ppermute only.
A program may use at most 384 MiB of HBM per device.

```python
import jax
import jax.numpy as jnp
from jax import lax

MODEL_WIDTH = 2048
NH = 8
HD = 256
HIDDEN_UNITS = 16384
ADAPTER_RANK = 256
PROMPT = 2048
NBR = 8
BR_LEN = 32
QUERY_FEATURES = 2048
GROUP_LEN = 2304
TOKENS = 9216


def group_layout(key):
    base = jax.random.fold_in(key, 11)
    group_count = TOKENS // GROUP_LEN
    pair_count = NBR // 2
    longer = jax.random.randint(jax.random.fold_in(base, 1), (group_count, pair_count), BR_LEN // 2, 3 * BR_LEN // 2 + 1)
    longer = longer.at[:, 0].set(3 * BR_LEN // 2)
    lengths = jnp.stack([longer, 2 * BR_LEN - longer], axis=-1).reshape(group_count, NBR)
    ranking = jax.random.randint(jax.random.fold_in(base, 2), (group_count, NBR), 0, 1000) * NBR + jnp.arange(NBR)[None, :]
    order = jnp.argsort(ranking, axis=-1)
    lengths = jnp.take_along_axis(lengths, order, axis=-1)
    ends = jnp.cumsum(lengths, axis=-1)
    starts = ends - lengths
    offsets = jnp.arange(NBR * BR_LEN)
    segment = jnp.sum((offsets[None, :, None] >= ends[:, None, :]).astype(jnp.int32), axis=-1)
    begins = jnp.take_along_axis(starts, segment, axis=-1)
    cont_pos = PROMPT + offsets[None, :] - begins
    prompt_pos = jnp.broadcast_to(jnp.arange(PROMPT)[None, :], (group_count, PROMPT))
    seg_out = jnp.concatenate([jnp.zeros((group_count, PROMPT), jnp.int32), (segment + 1).astype(jnp.int32)], axis=-1)
    pos_out = jnp.concatenate([prompt_pos.astype(jnp.int32), cont_pos.astype(jnp.int32)], axis=-1)
    return (seg_out.reshape(TOKENS).astype(jnp.int32), pos_out.reshape(TOKENS).astype(jnp.int32))


def draw_segment_numbers(key, part):
    return group_layout(key)[0]


def draw_positions(key, part):
    return group_layout(key)[1]


def block_scale(stream_key, dims, split, low, high):
    level = 1.0
    for axis_at, blocks in split:
        steps = jax.random.uniform(jax.random.fold_in(jax.random.fold_in(stream_key, 6), axis_at), (blocks,), jnp.float32, low / len(split), high / len(split))
        level = level * jnp.repeat(jnp.exp(steps), dims[axis_at] // blocks).reshape((-1,) + (1,) * (len(dims) - 1 - axis_at))
    return level


def scatter_about(rng, shape, spread, reach, split=(), held_as=jnp.bfloat16):
    level = block_scale(rng, shape, split, -0.22, 0.18) if split else 1.0
    drawn = jax.random.normal(rng, shape, jnp.float32) * spread * level
    return jnp.minimum(jnp.maximum(drawn, -reach), reach).astype(held_as)


def setup_inputs(seed: int = 0) -> dict:
    key_of = jax.random.split(jax.random.key(seed), 17)
    tokens = scatter_about(key_of[0], (TOKENS, MODEL_WIDTH), 1.0, 6.0, ((0, 32),))
    cotangent = scatter_about(key_of[1], (TOKENS, MODEL_WIDTH), 1.0, 6.0, ((0, 32),))
    segment_numbers = draw_segment_numbers(jax.random.fold_in(key_of[16], 71), 0)
    positions = draw_positions(jax.random.fold_in(key_of[16], 71), 0)
    attention_norm_gain = jnp.clip(1.0 + 0.18 * jax.random.normal(key_of[4], (MODEL_WIDTH,), jnp.float32), 0.1, 1.9)
    query_matrix = scatter_about(key_of[5], (MODEL_WIDTH, QUERY_FEATURES), (MODEL_WIDTH // 2) ** -0.5, 0.1875, ((0, 32),), jnp.float32)
    key_value_matrix = scatter_about(key_of[6], (MODEL_WIDTH, 2 * HD), MODEL_WIDTH ** -0.5, 0.125, ((0, 32),), jnp.float32)
    output_matrix = scatter_about(key_of[7], (QUERY_FEATURES, MODEL_WIDTH), (QUERY_FEATURES // 64) ** -0.5, 1.0, ((0, 32),), jnp.float32)
    output_adapter_first = scatter_about(key_of[8], (QUERY_FEATURES, ADAPTER_RANK), (QUERY_FEATURES // 64) ** -0.5, 1.0, ((0, 32),), jnp.float32)
    output_adapter_second = scatter_about(key_of[9], (ADAPTER_RANK, MODEL_WIDTH), ADAPTER_RANK ** -0.5, 0.375, ((0, 32),), jnp.float32)
    feedforward_norm_gain = jnp.clip(1.0 + 0.18 * jax.random.normal(key_of[10], (MODEL_WIDTH,), jnp.float32), 0.1, 1.9)
    gate_matrix = scatter_about(key_of[11], (MODEL_WIDTH, HIDDEN_UNITS), MODEL_WIDTH ** -0.5, 0.125, ((0, 4), (1, 8)), jnp.float32)
    up_matrix = scatter_about(key_of[12], (MODEL_WIDTH, HIDDEN_UNITS), MODEL_WIDTH ** -0.5, 0.125, ((0, 4), (1, 8)), jnp.float32)
    down_matrix = scatter_about(key_of[13], (MODEL_WIDTH, HIDDEN_UNITS), HIDDEN_UNITS ** -0.5, 0.046875, ((0, 4), (1, 8)), jnp.float32)
    down_adapter_first = scatter_about(key_of[14], (ADAPTER_RANK, HIDDEN_UNITS), HIDDEN_UNITS ** -0.5, 0.046875, ((0, 4), (1, 8)), jnp.float32)
    down_adapter_second = scatter_about(key_of[15], (ADAPTER_RANK, MODEL_WIDTH), ADAPTER_RANK ** -0.5, 0.375, ((0, 32),), jnp.float32)
    return dict(tokens=tokens, cotangent=cotangent, segment_numbers=segment_numbers, positions=positions, attention_norm_gain=attention_norm_gain, query_matrix=query_matrix, key_value_matrix=key_value_matrix, output_matrix=output_matrix, output_adapter_first=output_adapter_first, output_adapter_second=output_adapter_second, feedforward_norm_gain=feedforward_norm_gain, gate_matrix=gate_matrix, up_matrix=up_matrix, down_matrix=down_matrix, down_adapter_first=down_adapter_first, down_adapter_second=down_adapter_second)


@jax.custom_vjp
def reduced_copy(v):
    return lax.optimization_barrier(v.astype(jnp.bfloat16)).astype(jnp.float32)

@jax.custom_vjp
def reduced_backward(v):
    return v

def low_keep(v):
    return (reduced_copy(v), None)

def low_pass(kept, grad):
    return (grad,)

def back_keep(v):
    return (v, None)

def back_low(kept, grad):
    return (reduced_copy(grad),)
reduced_copy.defvjp(low_keep, low_pass)
reduced_backward.defvjp(back_keep, back_low)
highest = lax.Precision.HIGHEST
masked_score = -1e+30
epsilon = 1e-06

def round_pair(values):
    return reduced_copy(reduced_backward(values))

def matrix_product(left_side, right_side):
    return jnp.dot(left_side, right_side, precision=highest)

def rms_scale(values, gain):
    return values * lax.rsqrt(lax.optimization_barrier(jnp.mean(values * values, axis=-1, keepdims=True)) + epsilon) * gain

def rotate(tensor, positions):
    full_width = tensor.shape[-1]
    half_width = full_width // 2
    inverse = 10000.0 ** (-jnp.arange(half_width, dtype=jnp.float32) * 2.0 / full_width)
    angles = positions.astype(jnp.float32)[:, None] * inverse[None, :]
    cosine = jnp.cos(angles)
    sine_part = jnp.sin(angles)
    leading = tensor[..., :half_width]
    trailing = tensor[..., half_width:]
    return jnp.concatenate([leading * cosine - trailing * sine_part, trailing * cosine + leading * sine_part], axis=-1)

def attend(query_block, seg_block, index_block, key_rows, value_rows, segments):
    key_index = jnp.arange(GROUP_LEN, dtype=jnp.int32)
    scores = reduced_backward(jnp.einsum('hqd,kd->hqk', query_block, key_rows, precision=highest))
    allowed = (key_index[None, :] <= index_block[:, None]) & ((segments[None, :] == 0) | (segments[None, :] == seg_block[:, None]))
    weights = jax.nn.softmax(jnp.where(allowed[None], scores, masked_score), axis=-1)
    return jnp.einsum('hqk,kd->hqd', reduced_copy(weights), value_rows, precision=highest)

def block_layer(weight_collection, inputs, segments, positions):
    attention_norm_gain, query_matrix, key_value_matrix, output_matrix, output_adapter_first, output_adapter_second, feedforward_norm_gain, gate_matrix, up_matrix, down_matrix, down_adapter_first, down_adapter_second = weight_collection
    normed = reduced_copy(rms_scale(inputs, reduced_copy(attention_norm_gain)))
    query_pre = reduced_backward(matrix_product(normed, reduced_copy(query_matrix)))
    keyval_pre = reduced_backward(matrix_product(normed, reduced_copy(key_value_matrix)))
    head_split = query_pre.reshape(GROUP_LEN, NH, HD).transpose(1, 0, 2)
    queries = reduced_copy(rotate(head_split, positions) * HD ** (-0.5))
    key_rows = reduced_copy(rotate(keyval_pre[:, :HD], positions))
    value_rows = reduced_copy(keyval_pre[:, HD:])
    block_rows = 512 if GROUP_LEN % 512 == 0 else GROUP_LEN
    block_count = GROUP_LEN // block_rows
    query_blocks = queries.reshape(NH, block_count, block_rows, HD).transpose(1, 0, 2, 3)
    seg_blocks = segments.reshape(block_count, block_rows)
    index_blocks = jnp.arange(GROUP_LEN, dtype=jnp.int32).reshape(block_count, block_rows)
    attend_saved = jax.checkpoint(attend)

    def one_block(block_item):
        return attend_saved(block_item[0], block_item[1], block_item[2], key_rows, value_rows, segments)
    mixed_heads = lax.map(one_block, (query_blocks, seg_blocks, index_blocks))
    head_context = round_pair(mixed_heads.transpose(0, 2, 1, 3).reshape(GROUP_LEN, NH * HD))
    output_rank_rows = round_pair(matrix_product(head_context, reduced_copy(output_adapter_first)))
    attention_result = reduced_backward(matrix_product(head_context, reduced_copy(output_matrix)) + matrix_product(output_rank_rows, reduced_copy(output_adapter_second)))
    layer_state = inputs + attention_result
    normed_mlp = reduced_copy(rms_scale(layer_state, reduced_copy(feedforward_norm_gain)))
    gate_values = reduced_backward(matrix_product(normed_mlp, reduced_copy(gate_matrix)))
    up_values = reduced_backward(matrix_product(normed_mlp, reduced_copy(up_matrix)))
    hidden_activated = reduced_copy(jax.nn.gelu(gate_values, approximate=True) * up_values)
    down_rank_rows = round_pair(matrix_product(hidden_activated, reduced_copy(down_adapter_first).T))
    return layer_state + matrix_product(hidden_activated, reduced_copy(down_matrix).T) + matrix_product(down_rank_rows, reduced_copy(down_adapter_second))

def reference(tokens, cotangent, segment_numbers, positions, attention_norm_gain, query_matrix, key_value_matrix, output_matrix, output_adapter_first, output_adapter_second, feedforward_norm_gain, gate_matrix, up_matrix, down_matrix, down_adapter_first, down_adapter_second):
    parameter_tree = jax.tree.map(lambda primary_weights: primary_weights.astype(jnp.float32), (attention_norm_gain, query_matrix, key_value_matrix, output_matrix, output_adapter_first, output_adapter_second, feedforward_norm_gain, gate_matrix, up_matrix, down_matrix, down_adapter_first, down_adapter_second))
    group_count = TOKENS // GROUP_LEN
    inputs_all = tokens.astype(jnp.float32).reshape(group_count, GROUP_LEN, MODEL_WIDTH)
    cot_all = cotangent.astype(jnp.float32).reshape(group_count, GROUP_LEN, MODEL_WIDTH)
    seg_all = segment_numbers.reshape(group_count, GROUP_LEN)
    pos_all = positions.reshape(group_count, GROUP_LEN)

    def one_group(totals, group_item):
        group_in, group_cot, group_seg, group_pos = group_item

        def forward(weight_collection, values_in):
            return block_layer(weight_collection, values_in, group_seg, group_pos)
        result, pull_back = jax.vjp(forward, parameter_tree, group_in)
        weight_grads, input_grads = pull_back(group_cot)
        totals = jax.tree.map(jnp.add, totals, weight_grads)
        return (totals, (result.astype(jnp.bfloat16), input_grads.astype(jnp.bfloat16)))
    zeros_init = jax.tree.map(jnp.zeros_like, parameter_tree)
    totals, (outputs, input_grads) = lax.scan(one_group, zeros_init, (inputs_all, cot_all, seg_all, pos_all))
    return (outputs.reshape(TOKENS, MODEL_WIDTH), input_grads.reshape(TOKENS, MODEL_WIDTH), totals[0], totals[1], totals[2], totals[3], totals[4], totals[5], totals[6], totals[7], totals[8], totals[9], totals[10], totals[11])
```

```python
from functools import partial

import jax
import jax.numpy as jnp
from jax import lax
from jax.sharding import PartitionSpec as P

MODEL_WIDTH = 2048
NH = 8
HD = 256


masked_score = -1e30
epsilon = 1e-06
contract_last = (((1,), (1,)), ((), ()))
contract_first = (((0,), (0,)), ((), ()))


def convert_half(values):
    return values.astype(jnp.bfloat16)


def product(left_side, right_side, dims):
    return lax.dot_general(left_side, right_side, dims, preferred_element_type=jnp.float32)


def matrix_product(left_side, right_side):
    return jnp.dot(left_side, right_side, preferred_element_type=jnp.float32)


def rms_scale(values, gain):
    return values * lax.rsqrt(jnp.mean(values * values, axis=-1, keepdims=True) + epsilon) * gain


def rope_tables(positions):
    half_width = HD // 2
    inverse = 10000.0 ** (-jnp.arange(half_width, dtype=jnp.float32) * 2.0 / HD)
    angles = positions.astype(jnp.float32)[:, None] * inverse[None, :]
    return (jnp.cos(angles), jnp.sin(angles))


def rotate(tensor, cosine, sine_part):
    half_width = tensor.shape[-1] // 2
    leading = tensor[..., :half_width]
    trailing = tensor[..., half_width:]
    return jnp.concatenate(
        [leading * cosine - trailing * sine_part, trailing * cosine + leading * sine_part], axis=-1
    )


def unrotate(tensor, cosine, sine_part):
    half_width = tensor.shape[-1] // 2
    leading = tensor[..., :half_width]
    trailing = tensor[..., half_width:]
    return jnp.concatenate(
        [leading * cosine + trailing * sine_part, trailing * cosine - leading * sine_part], axis=-1
    )


def is_power(count):
    return count & (count - 1) == 0


def swap(values, axis, size, bit):
    return lax.ppermute(values, axis, [(i, i ^ bit) for i in range(size)])


def partner(own, step, size):
    return own ^ step if is_power(size) else (own + step) % size


def source_step(own, block, size):
    return own ^ block if is_power(size) else (block - own) % size


def to_partner(values, axis, step, size):
    return lax.ppermute(values, axis, [(i, partner(i, step, size)) for i in range(size)])


def from_partner(values, axis, step, size):
    return lax.ppermute(values, axis, [(partner(i, step, size), i) for i in range(size)])


def reorder(values, order):
    width = values.shape[-1] // len(order)
    return jnp.concatenate(
        [lax.dynamic_slice_in_dim(values, place * width, width, axis=-1) for place in order], axis=-1
    )


def gather_rows(shard, size):
    if size != 4:
        return [shard] + [from_partner(shard, "row", step, size) for step in range(1, size)]
    half = shard.shape[0] // 2
    upper, lower = shard[:half], shard[half:]
    first_upper_y = swap(upper, "row", size, 2)
    first_lower_x = swap(lower, "row", size, 1)
    upper_x = swap(upper, "row", size, 1)
    lower_y = swap(lower, "row", size, 2)
    far_upper = swap(first_upper_y, "row", size, 1)
    far_lower = swap(first_lower_x, "row", size, 2)
    return [shard, upper_x, first_lower_x, first_upper_y, lower_y, far_upper, far_lower]


def scatter_rows(blocks, size):
    if size != 4:
        total = blocks[0].astype(jnp.float32)
        for step in range(1, size):
            total = total + to_partner(blocks[step], "row", step, size).astype(jnp.float32)
        return total
    own, near_x, near_y, far = blocks
    half = own.shape[0] // 2
    far_upper = swap(far[:half], "row", size, 1)
    far_lower = swap(far[half:], "row", size, 2)
    upper_x = swap(near_x[:half], "row", size, 1)
    lower_y = swap(near_y[half:], "row", size, 2)
    upper_y = swap(add_half(near_y[:half], far_upper), "row", size, 2)
    lower_x = swap(add_half(near_x[half:], far_lower), "row", size, 1)
    return jnp.concatenate(
        [
            add_full(own[:half], upper_x, upper_y),
            add_full(own[half:], lower_x, lower_y),
        ],
        axis=0,
    )


def add_half(first, second):
    return convert_half(first.astype(jnp.float32) + second.astype(jnp.float32))


def add_full(first, second, third):
    return first.astype(jnp.float32) + second.astype(jnp.float32) + third.astype(jnp.float32)


def halve(values, stages, bits, sizes):
    for place, (axis, bit) in enumerate(stages):
        dim = bits.index((axis, bit))
        own = (lax.axis_index(axis) // bit) % 2
        kept = lax.dynamic_slice_in_dim(values, own, 1, axis=dim)
        sent = lax.dynamic_slice_in_dim(values, 1 - own, 1, axis=dim)
        got = swap(sent, axis, sizes[axis], bit)
        values = kept.astype(jnp.float32) + got.astype(jnp.float32)
        if place < len(stages) - 1:
            values = convert_half(values)
    return values.reshape(values.shape[-2:])


def scatter_all(values, row_size, col_size):
    devices, rows, width = values.shape
    if not (is_power(row_size) and is_power(col_size)):
        return lax.psum_scatter(
            values.astype(jnp.float32), ("row", "col"), scatter_dimension=0, tiled=True
        ).reshape(rows, width)
    sizes = {"row": row_size, "col": col_size}
    row_bits = [("row", 1 << k) for k in reversed(range(row_size.bit_length() - 1))]
    col_bits = [("col", 1 << k) for k in reversed(range(col_size.bit_length() - 1))]
    bits = row_bits + col_bits
    shaped = convert_half(values).reshape((2,) * len(bits) + (rows, width))
    half = width // 2
    pieces = []
    for row_order, piece in (
        (row_bits, shaped[..., :half]),
        (row_bits[::-1], shaped[..., half:]),
    ):
        pieces.append(halve(piece, col_bits[-1:] + row_order + col_bits[:-1], bits, sizes))
    return jnp.concatenate(pieces, axis=-1)


def per_device(
    tokens,
    cotangent,
    segment_numbers,
    positions,
    attention_norm_gain,
    query_matrix,
    key_value_matrix,
    output_matrix,
    output_adapter_first,
    output_adapter_second,
    feedforward_norm_gain,
    gate_matrix,
    up_matrix,
    down_matrix,
    down_adapter_first,
    down_adapter_second,
):
    row_size = lax.axis_size("row")
    col_size = lax.axis_size("col")
    devices = row_size * col_size
    row_at = lax.axis_index("row")
    tok_dev, width = tokens.shape
    group_len = segment_numbers.shape[0]
    row_total = tok_dev * NH
    query_width = query_matrix.shape[1]
    adapter_rows = output_adapter_second.shape[0]
    gain_len = attention_norm_gain.shape[0]
    start_row = lax.axis_index("col") * tok_dev
    scale = HD ** (-0.5)
    order = [partner(row_at, step, row_size) for step in range(row_size)]
    back_order = [source_step(row_at, block, row_size) for block in range(row_size)]

    small_rows = 2 * adapter_rows + 1
    small_pad = -small_rows % 8
    small = jnp.concatenate(
        [
            convert_half(output_adapter_second),
            convert_half(down_adapter_second),
            jnp.concatenate(
                [
                    convert_half(attention_norm_gain),
                    convert_half(feedforward_norm_gain),
                    jnp.zeros((width - 2 * gain_len,), jnp.bfloat16),
                ]
            )[None],
            jnp.zeros((small_pad, width), jnp.bfloat16),
        ],
        axis=0,
    )[None]
    small = lax.all_gather(small, ("row", "col"), axis=0, tiled=True)
    out_upper = small[:, :adapter_rows].reshape(-1, width)
    down_upper = small[:, adapter_rows : 2 * adapter_rows].reshape(-1, width)
    gain_attn = small[:, 2 * adapter_rows, :gain_len].reshape(width).astype(jnp.float32)
    gain_mlp = (
        small[:, 2 * adapter_rows, gain_len : 2 * gain_len].reshape(width).astype(jnp.float32)
    )
    in_weight = lax.all_gather(
        jnp.concatenate([convert_half(query_matrix), convert_half(key_value_matrix)], axis=1),
        ("row", "col"),
        axis=0,
        tiled=True,
    )
    out_weight = lax.all_gather(
        jnp.concatenate([convert_half(output_matrix), convert_half(output_adapter_first)], axis=1),
        ("row", "col"),
        axis=0,
        tiled=True,
    )
    gate_weight = jnp.concatenate(gather_rows(convert_half(gate_matrix), row_size), axis=0)
    up_weight = jnp.concatenate(gather_rows(convert_half(up_matrix), row_size), axis=0)
    down_weight = jnp.concatenate(
        gather_rows(convert_half(down_matrix), row_size)
        + gather_rows(convert_half(down_adapter_first), row_size),
        axis=0,
    )

    cot_grad = cotangent.astype(jnp.float32)
    rank_grad = convert_half(product(cotangent, down_upper, contract_last))
    cot_rows = lax.all_gather(
        jnp.concatenate([reorder(cotangent, order), reorder(rank_grad, order)], axis=1),
        "col",
        axis=0,
        tiled=True,
    )

    inputs = tokens.astype(jnp.float32)
    normed = convert_half(rms_scale(inputs, gain_attn))
    own_seg = lax.dynamic_slice_in_dim(segment_numbers, start_row, tok_dev)
    own_pos = lax.dynamic_slice_in_dim(positions, start_row, tok_dev)
    cosine, sine_part = rope_tables(own_pos)
    in_pre = matrix_product(normed, in_weight)
    query_pre = in_pre[:, :query_width]
    keyval_pre = in_pre[:, query_width:]
    query_rows = convert_half(
        rotate(query_pre.reshape(tok_dev, NH, HD), cosine[:, None, :], sine_part[:, None, :])
        * scale
    ).reshape(row_total, HD)
    keyval_rows = lax.all_gather(
        jnp.concatenate(
            [
                convert_half(rotate(keyval_pre[:, :HD], cosine, sine_part)),
                convert_half(keyval_pre[:, HD:]),
            ],
            axis=1,
        ),
        "col",
        axis=0,
        tiled=True,
    )
    key_rows = keyval_rows[:, :HD]
    value_rows = keyval_rows[:, HD:]
    row_index = start_row + jnp.arange(row_total, dtype=jnp.int32) // NH
    row_seg = jnp.repeat(own_seg, NH)
    key_index = jnp.arange(group_len, dtype=jnp.int32)
    allowed = (key_index[None, :] <= row_index[:, None]) & (
        (segment_numbers[None, :] == 0) | (segment_numbers[None, :] == row_seg[:, None])
    )
    scores = jnp.where(allowed, product(query_rows, key_rows, contract_last), masked_score)
    top_value = jnp.max(scores, axis=1)
    total_value = jnp.sum(jnp.exp(scores - top_value[:, None]), axis=1)
    log_norm = top_value + jnp.log(total_value)
    probs = convert_half(jnp.exp(scores - log_norm[:, None]))
    mixed_rows = matrix_product(probs, value_rows)
    head_context = convert_half(mixed_rows.reshape(tok_dev, NH * HD))
    out_pre = matrix_product(head_context, out_weight)
    output_rank_rows = convert_half(out_pre[:, width:])
    layer_state = inputs + out_pre[:, :width] + matrix_product(output_rank_rows, out_upper)
    normed_mlp = convert_half(rms_scale(layer_state, gain_mlp))

    ffn_in = lax.all_gather(reorder(normed_mlp, order), "col", axis=0, tiled=True)
    gate_values = matrix_product(ffn_in, gate_weight)
    up_values = matrix_product(ffn_in, up_weight)
    hidden_activated = convert_half(jax.nn.gelu(gate_values, approximate=True) * up_values)
    summed = lax.psum_scatter(
        convert_half(product(hidden_activated, down_weight, contract_last)),
        "col",
        scatter_dimension=0,
        tiled=True,
    )
    down_rank_rows = reorder(summed[:, width:], back_order)
    layer_out = convert_half(
        layer_state
        + reorder(summed[:, :width], back_order).astype(jnp.float32)
        + matrix_product(down_rank_rows, down_upper)
    )

    grad_down = convert_half(product(cot_rows, hidden_activated, contract_first))
    hidden_grad = matrix_product(cot_rows, down_weight)
    gelu_out, gelu_pull = jax.vjp(partial(jax.nn.gelu, approximate=True), gate_values)
    gate_grad = convert_half(gelu_pull(hidden_grad * up_values)[0])
    up_grad = convert_half(hidden_grad * gelu_out)
    normed_grad = lax.psum_scatter(
        convert_half(
            product(gate_grad, gate_weight, contract_last)
            + product(up_grad, up_weight, contract_last)
        ),
        "col",
        scatter_dimension=0,
        tiled=True,
    )
    grad_gate = convert_half(product(ffn_in, gate_grad, contract_first))
    grad_up = convert_half(product(ffn_in, up_grad, contract_first))

    def blocks_of(values):
        size = values.shape[0] // row_size
        return [values[size * step : size * (step + 1)] for step in range(row_size)]

    down_sum = scatter_rows(blocks_of(grad_down[:width]), row_size)
    rank_sum = scatter_rows(blocks_of(grad_down[width:]), row_size)
    gate_sum = scatter_rows(blocks_of(grad_gate), row_size)
    up_sum = scatter_rows(blocks_of(grad_up), row_size)

    normed_grad = reorder(normed_grad, back_order).astype(jnp.float32)
    state_out, norm_pull = jax.vjp(rms_scale, layer_state, gain_mlp)
    state_part, grad_gain_mlp = norm_pull(normed_grad)
    state_grad = cot_grad + state_part
    attn_grad = convert_half(state_grad)
    rank_out_grad = convert_half(product(attn_grad, out_upper, contract_last))
    out_grad = jnp.concatenate([attn_grad, rank_out_grad], axis=1)
    context_grad = product(out_grad, out_weight, contract_last)
    grad_rows = convert_half(context_grad).reshape(row_total, HD)
    delta = jnp.sum(grad_rows.astype(jnp.float32) * mixed_rows, axis=1)
    weight_grad = product(grad_rows, value_rows, contract_last)
    score_grad = convert_half(probs.astype(jnp.float32) * (weight_grad - delta[:, None]))
    query_acc = matrix_product(score_grad, key_rows)
    key_acc = product(score_grad, query_rows, contract_first)
    value_acc = product(probs, grad_rows, contract_first)
    keyval_sum = lax.psum_scatter(
        jnp.concatenate([convert_half(key_acc), convert_half(value_acc)], axis=1),
        "col",
        scatter_dimension=0,
        tiled=True,
    ).astype(jnp.float32)
    query_grad = convert_half(
        unrotate(
            query_acc.reshape(tok_dev, NH, HD) * scale, cosine[:, None, :], sine_part[:, None, :]
        ).reshape(tok_dev, NH * HD)
    )
    in_grad = jnp.concatenate(
        [
            query_grad,
            convert_half(unrotate(keyval_sum[:, :HD], cosine, sine_part)),
            convert_half(keyval_sum[:, HD:]),
        ],
        axis=1,
    )
    normed_back = product(in_grad, in_weight, contract_last)
    normed_out, first_pull = jax.vjp(rms_scale, inputs, gain_attn)
    input_part, grad_gain_attn = first_pull(normed_back)
    input_grad = convert_half(state_grad + input_part)

    grad_out = product(head_context, out_grad, contract_first)
    grad_in = product(normed, in_grad, contract_first)
    grad_out_upper = product(output_rank_rows, attn_grad, contract_first)
    grad_down_upper = product(down_rank_rows, cotangent, contract_first)
    out_sum = scatter_all(grad_out.reshape(devices, -1, grad_out.shape[1]), row_size, col_size)
    upper_sum = scatter_all(
        jnp.concatenate(
            [
                grad_out_upper.reshape(devices, adapter_rows, width),
                grad_down_upper.reshape(devices, adapter_rows, width),
            ],
            axis=1,
        ),
        row_size,
        col_size,
    )
    in_sum = scatter_all(grad_in.reshape(devices, -1, grad_in.shape[1]), row_size, col_size)
    gain_sum = scatter_all(
        jnp.pad(
            jnp.stack(
                [
                    grad_gain_attn.reshape(devices, gain_len),
                    grad_gain_mlp.reshape(devices, gain_len),
                ],
                axis=1,
            ),
            ((0, 0), (0, 6), (0, 256 - gain_len)),
        ),
        row_size,
        col_size,
    )
    return (
        layer_out,
        input_grad,
        gain_sum[0, :gain_len],
        in_sum[:, :query_width],
        in_sum[:, query_width:],
        out_sum[:, :width],
        out_sum[:, width:],
        upper_sum[:adapter_rows],
        gain_sum[1, :gain_len],
        gate_sum,
        up_sum,
        down_sum,
        rank_sum,
        upper_sum[adapter_rows:],
    )


def solution(mesh):
    return jax.shard_map(
        per_device,
        mesh=mesh,
        in_specs=(
            P(("row", "col"), None),
            P(("row", "col"), None),
            P("row"),
            P("row"),
            P(("row", "col")),
            P(("row", "col"), None),
            P(("row", "col"), None),
            P(("row", "col"), None),
            P(("row", "col"), None),
            P(("row", "col"), None),
            P(("row", "col")),
            P("row", "col"),
            P("row", "col"),
            P("row", "col"),
            P("row", "col"),
            P(("row", "col"), None),
        ),
        out_specs=(
            P(("row", "col"), None),
            P(("row", "col"), None),
            P(("row", "col")),
            P(("row", "col"), None),
            P(("row", "col"), None),
            P(("row", "col"), None),
            P(("row", "col"), None),
            P(("row", "col"), None),
            P(("row", "col")),
            P("row", "col"),
            P("row", "col"),
            P("row", "col"),
            P("row", "col"),
            P(("row", "col"), None),
        ),
        check_vma=False,
    )
```

```python
from functools import partial

import jax
import jax.numpy as jnp
from jax import lax
from jax.sharding import PartitionSpec as P

MODEL_WIDTH = 2048
NH = 8
HD = 256


masked_score = -1e30
epsilon = 1e-06
contract_last = (((1,), (1,)), ((), ()))
contract_first = (((0,), (0,)), ((), ()))


def convert_half(values):
    return values.astype(jnp.bfloat16)


def product(left_side, right_side, dims):
    return lax.dot_general(left_side, right_side, dims, preferred_element_type=jnp.float32)


def matrix_product(left_side, right_side):
    return jnp.dot(left_side, right_side, preferred_element_type=jnp.float32)


def rms_scale(values, gain):
    return values * lax.rsqrt(jnp.mean(values * values, axis=-1, keepdims=True) + epsilon) * gain


def rope_tables(positions):
    half_width = HD // 2
    inverse = 10000.0 ** (-jnp.arange(half_width, dtype=jnp.float32) * 2.0 / HD)
    angles = positions.astype(jnp.float32)[:, None] * inverse[None, :]
    return (jnp.cos(angles), jnp.sin(angles))


def rotate(tensor, cosine, sine_part):
    half_width = tensor.shape[-1] // 2
    leading = tensor[..., :half_width]
    trailing = tensor[..., half_width:]
    return jnp.concatenate(
        [leading * cosine - trailing * sine_part, trailing * cosine + leading * sine_part], axis=-1
    )


def unrotate(tensor, cosine, sine_part):
    half_width = tensor.shape[-1] // 2
    leading = tensor[..., :half_width]
    trailing = tensor[..., half_width:]
    return jnp.concatenate(
        [leading * cosine + trailing * sine_part, trailing * cosine - leading * sine_part], axis=-1
    )


def is_power(count):
    return count & (count - 1) == 0


def swap(values, axis, size, bit):
    return lax.ppermute(values, axis, [(i, i ^ bit) for i in range(size)])


def partner(own, step, size):
    return own ^ step if is_power(size) else (own + step) % size


def source_step(own, block, size):
    return own ^ block if is_power(size) else (block - own) % size


def to_partner(values, axis, step, size):
    return lax.ppermute(values, axis, [(i, partner(i, step, size)) for i in range(size)])


def from_partner(values, axis, step, size):
    return lax.ppermute(values, axis, [(partner(i, step, size), i) for i in range(size)])


def reorder(values, order):
    width = values.shape[-1] // len(order)
    return jnp.concatenate(
        [lax.dynamic_slice_in_dim(values, place * width, width, axis=-1) for place in order], axis=-1
    )


def tie(*values):
    return lax.optimization_barrier(values)


def place_blocks(blocks, places, count):
    rows = blocks[0].shape[0]
    whole = jnp.zeros((rows * count, blocks[0].shape[1]), blocks[0].dtype)
    for block, place in zip(blocks, places):
        whole = lax.dynamic_update_slice_in_dim(whole, block, place * rows, axis=0)
    return whole


def rows_of(pieces, start, stop):
    found = []
    for parts in pieces:
        offset = 0
        for part in parts:
            first, last = max(start - offset, 0), min(stop - offset, part.shape[0])
            if first < last:
                found.append(part[first:last])
            offset += part.shape[0]
    return jnp.concatenate(found, axis=0)


def far_round(blocks, size):
    if size != 4:
        return blocks
    far = blocks[3]
    half = far.shape[0] // 2
    return [
        blocks[0],
        blocks[1],
        blocks[2],
        swap(far[:half], "row", size, 1),
        swap(far[half:], "row", size, 2),
    ]


def near_sums(state, size):
    if size != 4:
        return state
    own, near_x, near_y, far_upper, far_lower = state
    half = own.shape[0] // 2
    near_x = jnp.concatenate([near_x[:half], add_half(near_x[half:], far_lower)], axis=0)
    near_y = jnp.concatenate([add_half(near_y[:half], far_upper), near_y[half:]], axis=0)
    return [own, near_x, near_y]


def near_round(state, size):
    if size != 4:
        return [state[0]] + [
            to_partner(state[step], "row", step, size) for step in range(1, size)
        ]
    own, near_x, near_y = state
    return [own, swap(near_x, "row", size, 1), swap(near_y, "row", size, 2)]


def add_all(state):
    total = state[0].astype(jnp.float32)
    for part in state[1:]:
        total = total + part.astype(jnp.float32)
    return total


def add_half(first, second):
    return convert_half(first.astype(jnp.float32) + second.astype(jnp.float32))


def halve(values, stages, bits, sizes):
    for place, (axis, bit) in enumerate(stages):
        dim = bits.index((axis, bit))
        own = (lax.axis_index(axis) // bit) % 2
        kept = lax.dynamic_slice_in_dim(values, own, 1, axis=dim)
        sent = lax.dynamic_slice_in_dim(values, 1 - own, 1, axis=dim)
        got = swap(sent, axis, sizes[axis], bit)
        values = kept.astype(jnp.float32) + got.astype(jnp.float32)
        if place < len(stages) - 1:
            values = convert_half(values)
    return values.reshape(values.shape[-2:])


def scatter_all(values, row_size, col_size, pieces=2):
    devices, rows, width = values.shape
    if not (is_power(row_size) and is_power(col_size)):
        return lax.psum_scatter(
            values.astype(jnp.float32), ("row", "col"), scatter_dimension=0, tiled=True
        ).reshape(rows, width)
    sizes = {"row": row_size, "col": col_size}
    row_bits = [("row", 1 << k) for k in reversed(range(row_size.bit_length() - 1))]
    col_bits = [("col", 1 << k) for k in reversed(range(col_size.bit_length() - 1))]
    bits = row_bits + col_bits
    shaped = convert_half(values).reshape((2,) * len(bits) + (rows, width))
    part = width // pieces
    sums = []
    for place in range(pieces):
        order = row_bits if place % 2 == 0 else row_bits[::-1]
        piece = shaped[..., part * place : part * (place + 1)]
        sums.append(halve(piece, col_bits[-1:] + order + col_bits[:-1], bits, sizes))
    return jnp.concatenate(sums, axis=-1)


def per_device(
    tokens,
    cotangent,
    segment_numbers,
    positions,
    attention_norm_gain,
    query_matrix,
    key_value_matrix,
    output_matrix,
    output_adapter_first,
    output_adapter_second,
    feedforward_norm_gain,
    gate_matrix,
    up_matrix,
    down_matrix,
    down_adapter_first,
    down_adapter_second,
):
    row_size = lax.axis_size("row")
    col_size = lax.axis_size("col")
    devices = row_size * col_size
    row_at = lax.axis_index("row")
    tok_dev, width = tokens.shape
    group_len = segment_numbers.shape[0]
    row_total = tok_dev * NH
    query_width = query_matrix.shape[1]
    adapter_rows = output_adapter_second.shape[0]
    gain_len = attention_norm_gain.shape[0]
    start_row = lax.axis_index("col") * tok_dev
    scale = HD ** (-0.5)
    order = [partner(row_at, step, row_size) for step in range(row_size)]
    back_order = [source_step(row_at, block, row_size) for block in range(row_size)]

    in_gathered = lax.all_gather(
        jnp.concatenate(
            [
                convert_half(query_matrix),
                convert_half(key_value_matrix),
                convert_half(
                    jnp.pad(
                        jnp.stack([attention_norm_gain, feedforward_norm_gain], axis=1),
                        ((0, 0), (0, 126)),
                    )
                ),
            ],
            axis=1,
        ),
        ("row", "col"),
        axis=0,
        tiled=True,
    )
    shard = jnp.concatenate(
        [
            convert_half(gate_matrix),
            convert_half(up_matrix),
            convert_half(down_matrix),
            convert_half(down_adapter_first),
        ],
        axis=0,
    )
    model_rows = gate_matrix.shape[0]
    by_pairs = row_size == 4 and col_size == 8
    cot_grad = cotangent.astype(jnp.float32)
    cot_mixed = reorder(cotangent, order)
    if by_pairs:
        half = shard.shape[0] // 2
        upper, lower = shard[:half], shard[half:]
        upper_y = swap(upper, "row", 4, 2)
        lower_x = swap(lower, "row", 4, 1)
        cot_two = swap(cot_mixed, "col", 8, 2)
        cot_four = swap(cot_mixed, "col", 8, 4)
        in_gathered, upper_y, lower_x, cot_two, cot_four, upper, lower, cot_last = tie(
            in_gathered, upper_y, lower_x, cot_two, cot_four, upper, lower, cot_mixed
        )
        upper_x = swap(upper, "row", 4, 1)
        lower_y = swap(lower, "row", 4, 2)
        cot_six = swap(cot_last, "col", 8, 6)
    in_width = in_gathered.shape[1] - 128
    in_weight = in_gathered[:, :in_width]
    gains = in_gathered[:, in_width:].astype(jnp.float32)
    gain_attn = gains[:, 0]
    gain_mlp = gains[:, 1]
    own_seg = lax.dynamic_slice_in_dim(segment_numbers, start_row, tok_dev)
    own_pos = lax.dynamic_slice_in_dim(positions, start_row, tok_dev)
    cosine, sine_part = rope_tables(own_pos)
    inputs = tokens.astype(jnp.float32)
    normed = convert_half(rms_scale(inputs, gain_attn))
    in_pre = matrix_product(normed, in_weight)
    query_pre = in_pre[:, :query_width]
    keyval_pre = in_pre[:, query_width:]
    query_rows = convert_half(
        rotate(query_pre.reshape(tok_dev, NH, HD), cosine[:, None, :], sine_part[:, None, :])
        * scale
    ).reshape(row_total, HD)
    keyval_rows = lax.all_gather(
        jnp.concatenate(
            [
                convert_half(rotate(keyval_pre[:, :HD], cosine, sine_part)),
                convert_half(keyval_pre[:, HD:]),
            ],
            axis=1,
        ),
        "col",
        axis=0,
        tiled=True,
    )
    out_packed = jnp.concatenate(
        [
            convert_half(output_matrix),
            convert_half(output_adapter_first),
            convert_half(output_adapter_second).reshape(gain_len, -1),
            convert_half(down_adapter_second).reshape(gain_len, -1),
        ],
        axis=1,
    )
    if by_pairs:
        (
            keyval_rows,
            out_packed,
            upper_x,
            lower_y,
            cot_six,
            upper_y,
            lower_x,
            cot_mixed,
            cot_two,
            cot_four,
        ) = tie(
            keyval_rows,
            out_packed,
            upper_x,
            lower_y,
            cot_six,
            upper_y,
            lower_x,
            cot_mixed,
            cot_two,
            cot_four,
        )
        far_upper = swap(upper_y, "row", 4, 1)
        far_lower = swap(lower_x, "row", 4, 2)
        cot_mine = jnp.concatenate([cot_mixed, cot_two, cot_four, cot_six], axis=0)
        cot_other = swap(cot_mine, "col", 8, 1)
    else:
        keyval_rows, out_packed = tie(keyval_rows, out_packed)
    out_gathered = lax.all_gather(out_packed, ("row", "col"), axis=0, tiled=True)
    key_rows = keyval_rows[:, :HD]
    value_rows = keyval_rows[:, HD:]
    row_index = start_row + jnp.arange(row_total, dtype=jnp.int32) // NH
    row_seg = jnp.repeat(own_seg, NH)
    key_index = jnp.arange(group_len, dtype=jnp.int32)
    allowed = (key_index[None, :] <= row_index[:, None]) & (
        (segment_numbers[None, :] == 0) | (segment_numbers[None, :] == row_seg[:, None])
    )
    scores = jnp.where(allowed, product(query_rows, key_rows, contract_last), masked_score)
    top_value = jnp.max(scores, axis=1)
    total_value = jnp.sum(jnp.exp(scores - top_value[:, None]), axis=1)
    log_norm = top_value + jnp.log(total_value)
    probs = convert_half(jnp.exp(scores - log_norm[:, None]))
    mixed_rows = matrix_product(probs, value_rows)
    head_context = convert_half(mixed_rows.reshape(tok_dev, NH * HD))
    if by_pairs:
        out_gathered, far_upper, far_lower, cot_other, head_context = tie(
            out_gathered, far_upper, far_lower, cot_other, head_context
        )
        pieces = [[shard], [upper_x, lower_x], [upper_y, lower_y], [far_upper, far_lower]]
        places = [lax.axis_index("col") ^ (2 * step) for step in range(4)]
        cot_rows = place_blocks(
            [cot_mine[tok_dev * step : tok_dev * (step + 1)] for step in range(4)]
            + [cot_other[tok_dev * step : tok_dev * (step + 1)] for step in range(4)],
            places + [place ^ 1 for place in places],
            8,
        )
    else:
        pieces = [[shard]] + [
            [from_partner(shard, "row", step, row_size)] for step in range(1, row_size)
        ]
        cot_rows = lax.all_gather(cot_mixed, "col", axis=0, tiled=True)
    gate_weight = rows_of(pieces, 0, model_rows)
    up_weight = rows_of(pieces, model_rows, 2 * model_rows)
    down_weight = jnp.concatenate(
        [
            rows_of(pieces, 2 * model_rows, 3 * model_rows),
            rows_of(pieces, 3 * model_rows, 3 * model_rows + down_adapter_first.shape[0]),
        ],
        axis=0,
    )
    rank_width = output_adapter_first.shape[1]
    out_width = width + rank_width
    upper_width = adapter_rows * width // gain_len
    out_weight = out_gathered[:, :out_width]
    out_upper = out_gathered[:, out_width : out_width + upper_width].reshape(-1, width)
    down_upper = out_gathered[:, out_width + upper_width :].reshape(-1, width)
    out_pre = matrix_product(head_context, out_weight)
    output_rank_rows = convert_half(out_pre[:, width:])
    layer_state = inputs + out_pre[:, :width] + matrix_product(output_rank_rows, out_upper)
    normed_mlp = convert_half(rms_scale(layer_state, gain_mlp))

    ffn_in = lax.all_gather(reorder(normed_mlp, order), "col", axis=0, tiled=True)
    rank_part = rank_width // row_size
    upper_mixed = jnp.concatenate(
        [
            lax.dynamic_slice_in_dim(reorder(down_upper, order), place * rank_part, rank_part)
            for place in order
        ],
        axis=0,
    )
    rank_rows = convert_half(product(cot_rows, upper_mixed, contract_last))
    cot_rows = jnp.concatenate([cot_rows, rank_rows], axis=1)
    hidden_grad = matrix_product(cot_rows, down_weight)
    ffn_in, hidden_grad, gate_weight, up_weight = tie(
        ffn_in, hidden_grad, gate_weight, up_weight
    )
    gate_values = matrix_product(ffn_in, gate_weight)
    up_values = matrix_product(ffn_in, up_weight)
    hidden_activated = convert_half(jax.nn.gelu(gate_values, approximate=True) * up_values)
    gelu_out, gelu_pull = jax.vjp(partial(jax.nn.gelu, approximate=True), gate_values)
    gate_grad = convert_half(gelu_pull(hidden_grad * up_values)[0])
    up_grad = convert_half(hidden_grad * gelu_out)

    def blocks_of(values):
        size = values.shape[0] // row_size
        return [values[size * step : size * (step + 1)] for step in range(row_size)]

    grad_down = convert_half(product(cot_rows, hidden_activated, contract_first))
    grad_down, gate_grad, up_grad = tie(grad_down, gate_grad, up_grad)
    down_state = far_round(
        [
            jnp.concatenate([one, two], axis=0)
            for one, two in zip(blocks_of(grad_down[:width]), blocks_of(grad_down[width:]))
        ],
        row_size,
    )
    normed_sum = convert_half(
        product(gate_grad, gate_weight, contract_last)
        + product(up_grad, up_weight, contract_last)
    )
    *down_state, normed_sum, gate_grad, up_grad = tie(
        *near_sums(down_state, row_size), normed_sum, gate_grad, up_grad
    )
    down_state = near_round(down_state, row_size)
    normed_grad = lax.psum_scatter(normed_sum, "col", scatter_dimension=0, tiled=True)
    grad_gate = convert_half(product(ffn_in, gate_grad, contract_first))
    grad_gate, up_grad = tie(grad_gate, up_grad)
    gate_state = far_round(blocks_of(grad_gate), row_size)
    grad_up = convert_half(product(ffn_in, up_grad, contract_first))
    gate_state = near_sums(gate_state, row_size)
    count = len(down_state)
    *states, grad_up, hidden_activated = tie(*down_state, *gate_state, grad_up, hidden_activated)
    down_total = add_all(states[:count])
    gate_state = near_round(states[count:], row_size)
    up_state = far_round(blocks_of(grad_up), row_size)
    down_partial = convert_half(product(hidden_activated, down_weight, contract_last))
    down_partial, normed_grad = tie(down_partial, normed_grad)

    normed_grad = reorder(normed_grad, back_order).astype(jnp.float32)
    state_out, norm_pull = jax.vjp(rms_scale, layer_state, gain_mlp)
    state_part, grad_gain_mlp = norm_pull(normed_grad)
    state_grad = cot_grad + state_part
    attn_grad = convert_half(state_grad)
    rank_out_grad = convert_half(product(attn_grad, out_upper, contract_last))
    out_grad = jnp.concatenate([attn_grad, rank_out_grad], axis=1)
    context_grad = product(out_grad, out_weight, contract_last)
    grad_rows = convert_half(context_grad).reshape(row_total, HD)
    up_state = near_sums(up_state, row_size)
    count = len(gate_state)
    *states, grad_rows = tie(*gate_state, *up_state, grad_rows)
    gate_sum = add_all(states[:count])
    up_state = near_round(states[count:], row_size)
    delta = jnp.sum(grad_rows.astype(jnp.float32) * mixed_rows, axis=1)
    weight_grad = product(grad_rows, value_rows, contract_last)
    score_grad = convert_half(probs.astype(jnp.float32) * (weight_grad - delta[:, None]))
    query_acc = matrix_product(score_grad, key_rows)
    key_acc = product(score_grad, query_rows, contract_first)
    value_acc = product(probs, grad_rows, contract_first)
    keyval_sum = lax.psum_scatter(
        jnp.concatenate([convert_half(key_acc), convert_half(value_acc)], axis=1),
        "col",
        scatter_dimension=0,
        tiled=True,
    )
    query_grad = convert_half(
        unrotate(
            query_acc.reshape(tok_dev, NH, HD) * scale, cosine[:, None, :], sine_part[:, None, :]
        ).reshape(tok_dev, NH * HD)
    )
    grad_query = convert_half(product(normed, query_grad, contract_first))
    *up_state, keyval_sum, down_partial, grad_query = tie(
        *up_state, keyval_sum, down_partial, grad_query
    )
    up_sum = add_all(up_state)
    keyval_sum = keyval_sum.astype(jnp.float32)
    down_sum, rank_sum = down_total[:model_rows], down_total[model_rows:]
    summed = lax.psum_scatter(down_partial, "col", scatter_dimension=0, tiled=True)
    down_rank_rows = reorder(summed[:, width:], back_order)
    layer_out = convert_half(
        layer_state
        + reorder(summed[:, :width], back_order).astype(jnp.float32)
        + matrix_product(down_rank_rows, down_upper)
    )
    keyval_grad = jnp.concatenate(
        [convert_half(unrotate(keyval_sum[:, :HD], cosine, sine_part)), convert_half(keyval_sum[:, HD:])],
        axis=1,
    )
    in_grad = jnp.concatenate([query_grad, keyval_grad], axis=1)
    normed_back = product(in_grad, in_weight, contract_last)
    normed_out, first_pull = jax.vjp(rms_scale, inputs, gain_attn)
    input_part, grad_gain_attn = first_pull(normed_back)
    input_grad = convert_half(state_grad + input_part)

    grad_out = product(head_context, out_grad, contract_first)
    grad_keyval = product(normed, keyval_grad, contract_first)
    grad_out_upper = product(output_rank_rows, attn_grad, contract_first)
    grad_down_upper = product(down_rank_rows, cotangent, contract_first)

    def shared(values):
        return convert_half(values).reshape(devices, gain_len, -1)

    out_sum = scatter_all(
        jnp.concatenate([shared(grad_out), shared(grad_out_upper)], axis=2),
        row_size,
        col_size,
    )
    query_sum = scatter_all(shared(grad_query), row_size, col_size)
    keyval_total = scatter_all(
        jnp.concatenate(
            [
                shared(grad_keyval),
                shared(grad_down_upper),
                jnp.pad(
                    jnp.stack([shared(grad_gain_attn)[..., 0], shared(grad_gain_mlp)[..., 0]], axis=2),
                    ((0, 0), (0, 0), (0, 126)),
                ),
            ],
            axis=2,
        ),
        row_size,
        col_size,
        pieces=1,
    )
    keyval_width = grad_keyval.shape[1]
    gain_at = keyval_width + upper_width
    return (
        layer_out,
        input_grad,
        keyval_total[:, gain_at],
        query_sum,
        keyval_total[:, :keyval_width],
        out_sum[:, :width],
        out_sum[:, width:out_width],
        out_sum[:, out_width:].reshape(adapter_rows, width),
        keyval_total[:, gain_at + 1],
        gate_sum,
        up_sum,
        down_sum,
        rank_sum,
        keyval_total[:, keyval_width:gain_at].reshape(adapter_rows, width),
    )


def solution(mesh):
    return jax.shard_map(
        per_device,
        mesh=mesh,
        in_specs=(
            P(("row", "col"), None),
            P(("row", "col"), None),
            P("row"),
            P("row"),
            P(("row", "col")),
            P(("row", "col"), None),
            P(("row", "col"), None),
            P(("row", "col"), None),
            P(("row", "col"), None),
            P(("row", "col"), None),
            P(("row", "col")),
            P("row", "col"),
            P("row", "col"),
            P("row", "col"),
            P("row", "col"),
            P(("row", "col"), None),
        ),
        out_specs=(
            P(("row", "col"), None),
            P(("row", "col"), None),
            P(("row", "col")),
            P(("row", "col"), None),
            P(("row", "col"), None),
            P(("row", "col"), None),
            P(("row", "col"), None),
            P(("row", "col"), None),
            P(("row", "col")),
            P("row", "col"),
            P("row", "col"),
            P("row", "col"),
            P("row", "col"),
            P(("row", "col"), None),
        ),
        check_vma=False,
    )
```

```python
from functools import partial

import jax
import jax.numpy as jnp
from jax import lax
from jax.sharding import PartitionSpec as P

MODEL_WIDTH = 2048
NH = 8
HD = 256


masked_score = -1e30
epsilon = 1e-06
contract_last = (((1,), (1,)), ((), ()))
contract_first = (((0,), (0,)), ((), ()))


def convert_half(values):
    return values.astype(jnp.bfloat16)


def product(left_side, right_side, dims):
    return lax.dot_general(left_side, right_side, dims, preferred_element_type=jnp.float32)


def matrix_product(left_side, right_side):
    return jnp.dot(left_side, right_side, preferred_element_type=jnp.float32)


def rms_scale(values, gain):
    return values * lax.rsqrt(jnp.mean(values * values, axis=-1, keepdims=True) + epsilon) * gain


def rope_tables(positions):
    half_width = HD // 2
    inverse = 10000.0 ** (-jnp.arange(half_width, dtype=jnp.float32) * 2.0 / HD)
    angles = positions.astype(jnp.float32)[:, None] * inverse[None, :]
    return (jnp.cos(angles), jnp.sin(angles))


def rotate(tensor, cosine, sine_part):
    half_width = tensor.shape[-1] // 2
    leading = tensor[..., :half_width]
    trailing = tensor[..., half_width:]
    return jnp.concatenate(
        [leading * cosine - trailing * sine_part, trailing * cosine + leading * sine_part], axis=-1
    )


def unrotate(tensor, cosine, sine_part):
    half_width = tensor.shape[-1] // 2
    leading = tensor[..., :half_width]
    trailing = tensor[..., half_width:]
    return jnp.concatenate(
        [leading * cosine + trailing * sine_part, trailing * cosine - leading * sine_part], axis=-1
    )


def swap(values, axis, size, bit):
    return lax.ppermute(values, axis, [(i, i ^ bit) for i in range(size)])


def partner(own, step):
    return own ^ step


def to_partner(values, axis, step, size):
    return lax.ppermute(values, axis, [(i, partner(i, step)) for i in range(size)])


def reorder(values, order):
    width = values.shape[-1] // len(order)
    return jnp.concatenate(
        [lax.dynamic_slice_in_dim(values, place * width, width, axis=-1) for place in order], axis=-1
    )


def tie(*values):
    return lax.optimization_barrier(values)


def place_blocks(blocks, places, count):
    rows = blocks[0].shape[0]
    whole = jnp.zeros((rows * count, blocks[0].shape[1]), blocks[0].dtype)
    for block, place in zip(blocks, places):
        whole = lax.dynamic_update_slice_in_dim(whole, block, place * rows, axis=0)
    return whole


def rows_of(pieces, start, stop):
    found = []
    for parts in pieces:
        offset = 0
        for part in parts:
            first, last = max(start - offset, 0), min(stop - offset, part.shape[0])
            if first < last:
                found.append(part[first:last])
            offset += part.shape[0]
    return jnp.concatenate(found, axis=0)


def split_blocks(blocks):
    own, near_x, near_y, far = blocks
    half = own.shape[0] // 2
    return (
        own,
        (far[:half], far[half:]),
        (near_x[:half], near_y[half:]),
        (near_x[half:], near_y[:half]),
    )


def send_pair(pair):
    return swap(pair[0], "row", 4, 1), swap(pair[1], "row", 4, 2)


def add_pair(pair, got):
    return add_half(pair[0], got[1]), add_half(pair[1], got[0])


def finish_sum(own, free, last):
    half = own.shape[0] // 2
    upper = add_full(own[:half], free[0], last[1])
    lower = add_full(own[half:], last[0], free[1])
    return jnp.concatenate([upper, lower], axis=0)


def row_sum(blocks, size):
    total = blocks[0].astype(jnp.float32)
    for step in range(1, size):
        total = total + to_partner(blocks[step], "row", step, size).astype(jnp.float32)
    return total


def add_full(first, second, third):
    return first.astype(jnp.float32) + second.astype(jnp.float32) + third.astype(jnp.float32)


def add_half(first, second):
    return convert_half(first.astype(jnp.float32) + second.astype(jnp.float32))


def halve(values, dim, axis, size, bit):
    own = (lax.axis_index(axis) // bit) % 2
    kept = lax.dynamic_slice_in_dim(values, own, 1, axis=dim)
    sent = lax.dynamic_slice_in_dim(values, 1 - own, 1, axis=dim)
    return add_half(kept, swap(sent, axis, size, bit))


def scatter_chips(values, row_size, col_size, parts=2):
    chips, rows, width = values.shape
    line = col_size // 2
    bits = [1 << k for k in reversed(range(row_size.bit_length() - 1))]
    shaped = values.reshape((2,) * len(bits) + (line, rows, width))
    part = width // parts
    pieces = []
    for place in range(parts):
        piece = shaped[..., part * place : part * (place + 1)]
        for bit in bits if place % 2 == 0 else bits[::-1]:
            piece = halve(piece, bits.index(bit), "row", row_size, bit)
        pieces.append(piece.reshape(line, rows, part))
    whole = jnp.concatenate(pieces, axis=-1)
    at = lax.axis_index("col") // 2
    total = lax.dynamic_index_in_dim(whole, at, 0, keepdims=False).astype(jnp.float32)
    for step in range(1, line):
        block = lax.dynamic_index_in_dim(whole, at ^ step, 0, keepdims=False)
        total = total + swap(block, "col", col_size, 2 * step).astype(jnp.float32)
    return total


def share_cores(values, col_size):
    core = lax.axis_index("col") % 2
    rows = values.shape[0] // 2
    kept = lax.dynamic_slice_in_dim(values, core * rows, rows)
    got = swap(lax.dynamic_slice_in_dim(values, (1 - core) * rows, rows), "col", col_size, 1)
    first = core == 0
    return jnp.where(first, kept, got), jnp.where(first, got, kept)


def core_half(values, core):
    half = values.shape[-1] // 2
    return lax.dynamic_slice_in_dim(values, core * half, half, axis=-1)


def with_partner(values, col_size):
    got = swap(values, "col", col_size, 1)
    return jnp.concatenate([values, got], axis=0)


def halves_with_partner(values, col_size):
    core = lax.axis_index("col") % 2
    got = swap(core_half(values, 1 - core), "col", col_size, 1)
    return jnp.concatenate([core_half(values, core), got], axis=0)


def per_device(
    tokens,
    cotangent,
    segment_numbers,
    positions,
    attention_norm_gain,
    query_matrix,
    key_value_matrix,
    output_matrix,
    output_adapter_first,
    output_adapter_second,
    feedforward_norm_gain,
    gate_matrix,
    up_matrix,
    down_matrix,
    down_adapter_first,
    down_adapter_second,
):
    row_size = lax.axis_size("row")
    col_size = lax.axis_size("col")
    devices = row_size * col_size
    row_at = lax.axis_index("row")
    tok_dev, width = tokens.shape
    group_len = segment_numbers.shape[0]
    row_total = tok_dev * NH
    query_width = query_matrix.shape[1]
    adapter_rows = output_adapter_second.shape[0]
    gain_len = attention_norm_gain.shape[0]
    start_row = lax.axis_index("col") * tok_dev
    scale = HD ** (-0.5)
    order = [partner(row_at, step) for step in range(row_size)]

    in_gathered = lax.all_gather(
        jnp.concatenate(
            [
                convert_half(query_matrix),
                convert_half(key_value_matrix),
                convert_half(
                    jnp.pad(
                        jnp.stack([attention_norm_gain, feedforward_norm_gain], axis=1),
                        ((0, 0), (0, 126)),
                    )
                ),
            ],
            axis=1,
        ),
        ("row", "col"),
        axis=0,
        tiled=True,
    )
    shard = jnp.concatenate(
        [
            convert_half(gate_matrix),
            convert_half(up_matrix),
            convert_half(down_matrix),
            convert_half(down_adapter_first),
        ],
        axis=0,
    )
    model_rows = gate_matrix.shape[0]
    by_pairs = row_size == 4 and col_size == 8
    cot_grad = cotangent.astype(jnp.float32)
    cot_mixed = reorder(cotangent, order)
    if by_pairs:
        half = shard.shape[0] // 2
        in_gathered, upper, lower, cot_mixed = tie(
            in_gathered, shard[:half], shard[half:], cot_mixed
        )
        upper_y = swap(upper, "row", 4, 2)
        lower_x = swap(lower, "row", 4, 1)
        cot_two = swap(cot_mixed, "col", 8, 2)
        cot_four = swap(cot_mixed, "col", 8, 4)
    in_width = in_gathered.shape[1] - 128
    in_weight = in_gathered[:, :in_width]
    gains = in_gathered[:, in_width:].astype(jnp.float32)
    gain_attn = gains[:, 0]
    gain_mlp = gains[:, 1]
    own_seg = lax.dynamic_slice_in_dim(segment_numbers, start_row, tok_dev)
    own_pos = lax.dynamic_slice_in_dim(positions, start_row, tok_dev)
    cosine, sine_part = rope_tables(own_pos)
    inputs = tokens.astype(jnp.float32)
    normed = convert_half(rms_scale(inputs, gain_attn))
    in_pre = matrix_product(normed, in_weight)
    query_pre = in_pre[:, :query_width]
    keyval_pre = in_pre[:, query_width:]
    query_rows = convert_half(
        rotate(query_pre.reshape(tok_dev, NH, HD), cosine[:, None, :], sine_part[:, None, :])
        * scale
    ).reshape(row_total, HD)
    keyval_rows = lax.all_gather(
        jnp.concatenate(
            [
                convert_half(rotate(keyval_pre[:, :HD], cosine, sine_part)),
                convert_half(keyval_pre[:, HD:]),
            ],
            axis=1,
        ),
        "col",
        axis=0,
        tiled=True,
    )
    out_packed = jnp.concatenate(
        [
            convert_half(output_matrix),
            convert_half(output_adapter_first),
            convert_half(output_adapter_second).reshape(gain_len, -1),
            convert_half(down_adapter_second).reshape(gain_len, -1),
        ],
        axis=1,
    )
    keyval_rows, out_packed = tie(keyval_rows, out_packed)
    if by_pairs:
        (keyval_rows, out_packed, upper_y, lower_x, cot_two, cot_four, upper, lower, cot_mixed) = (
            tie(
                keyval_rows,
                out_packed,
                upper_y,
                lower_x,
                cot_two,
                cot_four,
                upper,
                lower,
                cot_mixed,
            )
        )
        upper_x = swap(upper, "row", 4, 1)
        lower_y = swap(lower, "row", 4, 2)
        cot_six = swap(cot_mixed, "col", 8, 6)
    out_gathered = lax.all_gather(out_packed, ("row", "col"), axis=0, tiled=True)
    key_rows = keyval_rows[:, :HD]
    value_rows = keyval_rows[:, HD:]
    row_index = start_row + jnp.arange(row_total, dtype=jnp.int32) // NH
    row_seg = jnp.repeat(own_seg, NH)
    key_index = jnp.arange(group_len, dtype=jnp.int32)
    allowed = (key_index[None, :] <= row_index[:, None]) & (
        (segment_numbers[None, :] == 0) | (segment_numbers[None, :] == row_seg[:, None])
    )
    scores = jnp.where(allowed, product(query_rows, key_rows, contract_last), masked_score)
    top_value = jnp.max(scores, axis=1)
    total_value = jnp.sum(jnp.exp(scores - top_value[:, None]), axis=1)
    log_norm = top_value + jnp.log(total_value)
    probs = convert_half(jnp.exp(scores - log_norm[:, None]))
    mixed_rows = matrix_product(probs, value_rows)
    head_context = convert_half(mixed_rows.reshape(tok_dev, NH * HD))
    if by_pairs:
        out_gathered, upper_x, lower_y, cot_six, head_context, upper_y, lower_x = tie(
            out_gathered, upper_x, lower_y, cot_six, head_context, upper_y, lower_x
        )
        far_upper = swap(upper_y, "row", 4, 1)
        far_lower = swap(lower_x, "row", 4, 2)
        cot_mine = jnp.concatenate([cot_mixed, cot_two, cot_four, cot_six], axis=0)
        cot_other = swap(cot_mine, "col", 8, 1)
        pieces = [[shard], [upper_x, lower_x], [upper_y, lower_y], [far_upper, far_lower]]
        places = [lax.axis_index("col") ^ (2 * step) for step in range(4)]
        cot_rows = place_blocks(
            [cot_mine[tok_dev * step : tok_dev * (step + 1)] for step in range(4)]
            + [cot_other[tok_dev * step : tok_dev * (step + 1)] for step in range(4)],
            places + [place ^ 1 for place in places],
            8,
        )
    else:
        pieces = [[shard]] + [
            [to_partner(shard, "row", step, row_size)] for step in range(1, row_size)
        ]
        cot_rows = lax.all_gather(cot_mixed, "col", axis=0, tiled=True)
    gate_weight = rows_of(pieces, 0, model_rows)
    up_weight = rows_of(pieces, model_rows, 2 * model_rows)
    down_weight = jnp.concatenate(
        [
            rows_of(pieces, 2 * model_rows, 3 * model_rows),
            rows_of(pieces, 3 * model_rows, 3 * model_rows + down_adapter_first.shape[0]),
        ],
        axis=0,
    )
    rank_width = output_adapter_first.shape[1]
    out_width = width + rank_width
    upper_width = adapter_rows * width // gain_len
    out_weight = out_gathered[:, :out_width]
    out_upper = out_gathered[:, out_width : out_width + upper_width].reshape(-1, width)
    down_upper = out_gathered[:, out_width + upper_width :].reshape(-1, width)
    out_pre = matrix_product(head_context, out_weight)
    output_rank_rows = convert_half(out_pre[:, width:])
    layer_state = inputs + out_pre[:, :width] + matrix_product(output_rank_rows, out_upper)
    normed_mlp = convert_half(rms_scale(layer_state, gain_mlp))
    normed_both = with_partner(normed, col_size)
    context_both = with_partner(head_context, col_size)
    rank_both = with_partner(output_rank_rows, col_size)
    cot_both = halves_with_partner(cotangent, col_size)

    ffn_in = lax.all_gather(reorder(normed_mlp, order), "col", axis=0, tiled=True)
    rank_part = rank_width // row_size
    upper_mixed = jnp.concatenate(
        [
            lax.dynamic_slice_in_dim(reorder(down_upper, order), place * rank_part, rank_part)
            for place in order
        ],
        axis=0,
    )
    rank_rows = convert_half(product(cot_rows, upper_mixed, contract_last))
    cot_rows = jnp.concatenate([cot_rows, rank_rows], axis=1)
    hidden_grad = matrix_product(cot_rows, down_weight)
    ffn_in, hidden_grad, gate_weight, up_weight = tie(
        ffn_in, hidden_grad, gate_weight, up_weight
    )
    gate_values = matrix_product(ffn_in, gate_weight)
    up_values = matrix_product(ffn_in, up_weight)
    hidden_activated = convert_half(jax.nn.gelu(gate_values, approximate=True) * up_values)
    gelu_out, gelu_pull = jax.vjp(partial(jax.nn.gelu, approximate=True), gate_values)
    gate_grad = convert_half(gelu_pull(hidden_grad * up_values)[0])
    up_grad = convert_half(hidden_grad * gelu_out)

    def blocks_of(values):
        size = values.shape[0] // row_size
        return [values[size * step : size * (step + 1)] for step in range(row_size)]

    grad_down = convert_half(product(cot_rows, hidden_activated, contract_first))
    grad_down, gate_grad, up_grad = tie(grad_down, gate_grad, up_grad)
    down_blocks = [
        jnp.concatenate([one, two], axis=0)
        for one, two in zip(blocks_of(grad_down[:width]), blocks_of(grad_down[width:]))
    ]
    if row_size == 4:
        own_down, far, free, last = split_blocks(down_blocks)
        far = send_pair(far)
        partial_sum = product(gate_grad, gate_weight, contract_last)
        *far, partial_sum, up_grad, free_x, free_y = tie(*far, partial_sum, up_grad, *free)
        last = add_pair(last, far)
        free = send_pair((free_x, free_y))
        normed_sum = convert_half(partial_sum + product(up_grad, up_weight, contract_last))
        *free, normed_sum, gate_grad, up_grad, last_x, last_y = tie(
            *free, normed_sum, gate_grad, up_grad, *last
        )
        normed_grad = lax.psum_scatter(normed_sum, "col", scatter_dimension=0, tiled=True)
        last = send_pair((last_x, last_y))
        grad_gate = convert_half(product(ffn_in, gate_grad, contract_first))
        *down_parts, grad_gate, up_grad = tie(own_down, *free, *last, grad_gate, up_grad)
        down_total = finish_sum(down_parts[0], down_parts[1:3], down_parts[3:])
        own_gate, far, free, last = split_blocks(blocks_of(grad_gate))
        far = send_pair(far)
        grad_up = convert_half(product(ffn_in, up_grad, contract_first))
        *far, grad_up, hidden_activated, free_x, free_y = tie(
            *far, grad_up, hidden_activated, *free
        )
        gate_last = add_pair(last, far)
        gate_free = send_pair((free_x, free_y))
        own_up, far, up_free, up_last = split_blocks(blocks_of(grad_up))
        far = send_pair(far)
        down_partial = convert_half(product(hidden_activated, down_weight, contract_last))
        *gate_free, far_x, far_y, normed_grad, down_partial = tie(
            *gate_free, *far, normed_grad, down_partial
        )
        up_last = add_pair(up_last, (far_x, far_y))
        gate_last = send_pair(gate_last)
        up_free = send_pair(up_free)
    else:
        normed_sum = convert_half(
            product(gate_grad, gate_weight, contract_last)
            + product(up_grad, up_weight, contract_last)
        )
        normed_grad = lax.psum_scatter(normed_sum, "col", scatter_dimension=0, tiled=True)
        grad_gate = convert_half(product(ffn_in, gate_grad, contract_first))
        grad_up = convert_half(product(ffn_in, up_grad, contract_first))
        down_partial = convert_half(product(hidden_activated, down_weight, contract_last))
        down_total = row_sum(down_blocks, row_size)
        gate_sum = row_sum(blocks_of(grad_gate), row_size)
        up_sum = row_sum(blocks_of(grad_up), row_size)
    down_sum, rank_sum = down_total[:model_rows], down_total[model_rows:]
    summed = lax.psum_scatter(down_partial, "col", scatter_dimension=0, tiled=True)

    normed_grad = reorder(normed_grad, order).astype(jnp.float32)
    state_out, norm_pull = jax.vjp(rms_scale, layer_state, gain_mlp)
    state_part, grad_gain_mlp = norm_pull(normed_grad)
    state_grad = cot_grad + state_part
    attn_grad = convert_half(state_grad)
    rank_out_grad = convert_half(product(attn_grad, out_upper, contract_last))
    out_grad = jnp.concatenate([attn_grad, rank_out_grad], axis=1)
    context_grad = product(out_grad, out_weight, contract_last)
    grad_rows = convert_half(context_grad).reshape(row_total, HD)
    delta = jnp.sum(grad_rows.astype(jnp.float32) * mixed_rows, axis=1)
    weight_grad = product(grad_rows, value_rows, contract_last)
    score_grad = convert_half(probs.astype(jnp.float32) * (weight_grad - delta[:, None]))
    if row_size == 4:
        *gate_last, up_free_x, up_free_y, score_grad, up_last_x, up_last_y = tie(
            *gate_last, *up_free, score_grad, *up_last
        )
        gate_sum = finish_sum(own_gate, gate_free, gate_last)
        up_last = send_pair((up_last_x, up_last_y))
    query_acc = matrix_product(score_grad, key_rows)
    if row_size == 4:
        *up_last, query_acc = tie(*up_last, query_acc)
        up_sum = finish_sum(own_up, (up_free_x, up_free_y), up_last)
    key_acc = product(score_grad, query_rows, contract_first)
    value_acc = product(probs, grad_rows, contract_first)
    keyval_part = jnp.concatenate([convert_half(key_acc), convert_half(value_acc)], axis=1)
    keyval_part, summed = tie(keyval_part, summed)
    keyval_sum = lax.psum_scatter(keyval_part, "col", scatter_dimension=0, tiled=True)
    query_grad = convert_half(
        unrotate(
            query_acc.reshape(tok_dev, NH, HD) * scale, cosine[:, None, :], sine_part[:, None, :]
        ).reshape(tok_dev, NH * HD)
    )
    core = lax.axis_index("col") % 2
    query_right = halves_with_partner(query_grad, col_size)
    grad_query = convert_half(product(normed_both, query_right, contract_first))
    keyval_sum, grad_query = tie(keyval_sum, grad_query)
    keyval_sum = keyval_sum.astype(jnp.float32)
    down_rank_rows = reorder(summed[:, width:], order)
    layer_out = convert_half(
        layer_state
        + reorder(summed[:, :width], order).astype(jnp.float32)
        + matrix_product(down_rank_rows, down_upper)
    )
    keyval_grad = jnp.concatenate(
        [convert_half(unrotate(keyval_sum[:, :HD], cosine, sine_part)), convert_half(keyval_sum[:, HD:])],
        axis=1,
    )
    in_grad = jnp.concatenate([query_grad, keyval_grad], axis=1)
    normed_back = product(in_grad, in_weight, contract_last)
    normed_out, first_pull = jax.vjp(rms_scale, inputs, gain_attn)
    input_part, grad_gain_attn = first_pull(normed_back)
    input_grad = convert_half(state_grad + input_part)

    chips = devices // 2

    def shared(values):
        return convert_half(values).reshape(chips, 2 * gain_len, -1)

    out_right = halves_with_partner(out_grad[:, :width], col_size)
    rank_right = halves_with_partner(out_grad[:, width:], col_size)
    grad_out = product(
        context_both, jnp.concatenate([out_right, rank_right], axis=1), contract_first
    )
    grad_out_upper = product(rank_both, out_right, contract_first)
    grad_keyval = product(
        normed_both, halves_with_partner(keyval_grad, col_size), contract_first
    )
    grad_down_upper = product(
        with_partner(down_rank_rows, col_size), cot_both, contract_first
    )
    gains = jnp.stack([grad_gain_attn, grad_gain_mlp])
    gain = lax.dynamic_index_in_dim(gains, core, 0, keepdims=False) + swap(
        lax.dynamic_index_in_dim(gains, 1 - core, 0, keepdims=False), "col", col_size, 1
    )
    out_first, out_second = share_cores(
        scatter_chips(
            jnp.concatenate([shared(grad_out), shared(grad_out_upper)], axis=2), row_size, col_size
        ),
        col_size,
    )
    query_first, query_second = share_cores(
        scatter_chips(shared(grad_query), row_size, col_size), col_size
    )
    keyval_first, keyval_second = share_cores(
        scatter_chips(
            jnp.concatenate(
                [
                    shared(grad_keyval),
                    shared(grad_down_upper),
                    jnp.pad(shared(gain), ((0, 0), (0, 0), (0, 127))),
                ],
                axis=2,
            ),
            row_size,
            col_size,
            parts=1,
        ),
        col_size,
    )

    def joined(first, second, start, size):
        return jnp.concatenate([first[:, start : start + size], second[:, start : start + size]], axis=1)

    def joined_rows(first, second, start, size):
        return jnp.concatenate(
            [
                half[:, start : start + size].reshape(adapter_rows, -1)
                for half in (first, second)
            ],
            axis=1,
        )

    half_width = width // 2
    half_rank = rank_width // 2
    half_keyval = key_value_matrix.shape[1] // 2
    half_upper = upper_width // 2
    return (
        layer_out,
        input_grad,
        keyval_first[:, half_keyval + half_upper],
        joined(query_first, query_second, 0, query_width // 2),
        joined(keyval_first, keyval_second, 0, half_keyval),
        joined(out_first, out_second, 0, half_width),
        joined(out_first, out_second, half_width, half_rank),
        joined_rows(out_first, out_second, half_width + half_rank, half_upper),
        keyval_second[:, half_keyval + half_upper],
        gate_sum,
        up_sum,
        down_sum,
        rank_sum,
        joined_rows(keyval_first, keyval_second, half_keyval, half_upper),
    )


def solution(mesh):
    return jax.shard_map(
        per_device,
        mesh=mesh,
        in_specs=(
            P(("row", "col"), None),
            P(("row", "col"), None),
            P("row"),
            P("row"),
            P(("row", "col")),
            P(("row", "col"), None),
            P(("row", "col"), None),
            P(("row", "col"), None),
            P(("row", "col"), None),
            P(("row", "col"), None),
            P(("row", "col")),
            P("row", "col"),
            P("row", "col"),
            P("row", "col"),
            P("row", "col"),
            P(("row", "col"), None),
        ),
        out_specs=(
            P(("row", "col"), None),
            P(("row", "col"), None),
            P(("row", "col")),
            P(("row", "col"), None),
            P(("row", "col"), None),
            P(("row", "col"), None),
            P(("row", "col"), None),
            P(("row", "col"), None),
            P(("row", "col")),
            P("row", "col"),
            P("row", "col"),
            P("row", "col"),
            P("row", "col"),
            P(("row", "col"), None),
        ),
        check_vma=False,
    )
```

```python
from functools import partial

import jax
import jax.numpy as jnp
from jax import lax
from jax.sharding import PartitionSpec as P

MODEL_WIDTH = 2048
NH = 8
HD = 256


masked_score = -1e30
epsilon = 1e-06
contract_last = (((1,), (1,)), ((), ()))
contract_first = (((0,), (0,)), ((), ()))


def convert_half(values):
    return values.astype(jnp.bfloat16)


def product(left_side, right_side, dims):
    return lax.dot_general(left_side, right_side, dims, preferred_element_type=jnp.float32)


def matrix_product(left_side, right_side):
    return jnp.dot(left_side, right_side, preferred_element_type=jnp.float32)


def rms_scale(values, gain):
    return values * lax.rsqrt(jnp.mean(values * values, axis=-1, keepdims=True) + epsilon) * gain


def rope_tables(positions):
    half_width = HD // 2
    inverse = 10000.0 ** (-jnp.arange(half_width, dtype=jnp.float32) * 2.0 / HD)
    angles = positions.astype(jnp.float32)[:, None] * inverse[None, :]
    return (jnp.cos(angles), jnp.sin(angles))


def rotate(tensor, cosine, sine_part):
    half_width = tensor.shape[-1] // 2
    leading = tensor[..., :half_width]
    trailing = tensor[..., half_width:]
    return jnp.concatenate(
        [leading * cosine - trailing * sine_part, trailing * cosine + leading * sine_part], axis=-1
    )


def unrotate(tensor, cosine, sine_part):
    half_width = tensor.shape[-1] // 2
    leading = tensor[..., :half_width]
    trailing = tensor[..., half_width:]
    return jnp.concatenate(
        [leading * cosine + trailing * sine_part, trailing * cosine - leading * sine_part], axis=-1
    )


def swap(values, axis, size, bit):
    return lax.ppermute(values, axis, [(i, i ^ bit) for i in range(size)])


def partner(own, step):
    return own ^ step


def to_partner(values, axis, step, size):
    return lax.ppermute(values, axis, [(i, partner(i, step)) for i in range(size)])


def reorder(values, order):
    width = values.shape[-1] // len(order)
    return jnp.concatenate(
        [lax.dynamic_slice_in_dim(values, place * width, width, axis=-1) for place in order], axis=-1
    )


def tie(*values):
    return lax.optimization_barrier(values)


def place_blocks(blocks, places, count):
    rows = blocks[0].shape[0]
    whole = jnp.zeros((rows * count, blocks[0].shape[1]), blocks[0].dtype)
    for block, place in zip(blocks, places):
        whole = lax.dynamic_update_slice_in_dim(whole, block, place * rows, axis=0)
    return whole


def rows_of(pieces, start, stop):
    found = []
    for parts in pieces:
        offset = 0
        for part in parts:
            first, last = max(start - offset, 0), min(stop - offset, part.shape[0])
            if first < last:
                found.append(part[first:last])
            offset += part.shape[0]
    return jnp.concatenate(found, axis=0)


def split_blocks(blocks):
    own, near_x, near_y, far = blocks
    half = own.shape[0] // 2
    return (
        own,
        (far[:half], far[half:]),
        (near_x[:half], near_y[half:]),
        (near_x[half:], near_y[:half]),
    )


def send_pair(pair):
    return swap(pair[0], "row", 4, 1), swap(pair[1], "row", 4, 2)


def add_pair(pair, got):
    return add_half(pair[0], got[1]), add_half(pair[1], got[0])


def finish_sum(own, free, last):
    half = own.shape[0] // 2
    upper = add_full(own[:half], free[0], last[1])
    lower = add_full(own[half:], last[0], free[1])
    return jnp.concatenate([upper, lower], axis=0)


def row_sum(blocks, size):
    total = blocks[0].astype(jnp.float32)
    for step in range(1, size):
        total = total + to_partner(blocks[step], "row", step, size).astype(jnp.float32)
    return total


def add_full(first, second, third):
    return first.astype(jnp.float32) + second.astype(jnp.float32) + third.astype(jnp.float32)


def add_half(first, second):
    return convert_half(first.astype(jnp.float32) + second.astype(jnp.float32))


def halve(values, dim, axis, size, bit):
    own = (lax.axis_index(axis) // bit) % 2
    kept = lax.dynamic_slice_in_dim(values, own, 1, axis=dim)
    sent = lax.dynamic_slice_in_dim(values, 1 - own, 1, axis=dim)
    return add_half(kept, swap(sent, axis, size, bit))


def scatter_chips(values, row_size, col_size, parts=2):
    chips, rows, width = values.shape
    line = col_size // 2
    bits = [1 << k for k in reversed(range(row_size.bit_length() - 1))]
    shaped = values.reshape((2,) * len(bits) + (line, rows, width))
    part = width // parts
    pieces = []
    for place in range(parts):
        piece = shaped[..., part * place : part * (place + 1)]
        for bit in bits if place % 2 == 0 else bits[::-1]:
            piece = halve(piece, bits.index(bit), "row", row_size, bit)
        pieces.append(piece.reshape(line, rows, part))
    whole = jnp.concatenate(pieces, axis=-1)
    at = lax.axis_index("col") // 2
    total = lax.dynamic_index_in_dim(whole, at, 0, keepdims=False).astype(jnp.float32)
    for step in range(1, line):
        block = lax.dynamic_index_in_dim(whole, at ^ step, 0, keepdims=False)
        total = total + swap(block, "col", col_size, 2 * step).astype(jnp.float32)
    return total


def share_cores(values, col_size):
    core = lax.axis_index("col") % 2
    rows = values.shape[0] // 2
    kept = lax.dynamic_slice_in_dim(values, core * rows, rows)
    got = swap(lax.dynamic_slice_in_dim(values, (1 - core) * rows, rows), "col", col_size, 1)
    first = core == 0
    return jnp.where(first, kept, got), jnp.where(first, got, kept)


def core_half(values, core):
    half = values.shape[-1] // 2
    return lax.dynamic_slice_in_dim(values, core * half, half, axis=-1)


def with_partner(values, col_size):
    got = swap(values, "col", col_size, 1)
    return jnp.concatenate([values, got], axis=0)


def halves_with_partner(values, col_size):
    core = lax.axis_index("col") % 2
    got = swap(core_half(values, 1 - core), "col", col_size, 1)
    return jnp.concatenate([core_half(values, core), got], axis=0)


def per_device(
    tokens,
    cotangent,
    segment_numbers,
    positions,
    attention_norm_gain,
    query_matrix,
    key_value_matrix,
    output_matrix,
    output_adapter_first,
    output_adapter_second,
    feedforward_norm_gain,
    gate_matrix,
    up_matrix,
    down_matrix,
    down_adapter_first,
    down_adapter_second,
):
    row_size = lax.axis_size("row")
    col_size = lax.axis_size("col")
    devices = row_size * col_size
    row_at = lax.axis_index("row")
    tok_dev, width = tokens.shape
    group_len = segment_numbers.shape[0]
    row_total = tok_dev * NH
    query_width = query_matrix.shape[1]
    adapter_rows = output_adapter_second.shape[0]
    gain_len = attention_norm_gain.shape[0]
    start_row = lax.axis_index("col") * tok_dev
    scale = HD ** (-0.5)
    order = [partner(row_at, step) for step in range(row_size)]

    in_gathered = lax.all_gather(
        jnp.concatenate(
            [
                convert_half(query_matrix),
                convert_half(key_value_matrix),
                convert_half(
                    jnp.pad(
                        jnp.stack([attention_norm_gain, feedforward_norm_gain], axis=1),
                        ((0, 0), (0, 126)),
                    )
                ),
            ],
            axis=1,
        ),
        ("row", "col"),
        axis=0,
        tiled=True,
    )
    shard = jnp.concatenate(
        [
            convert_half(gate_matrix),
            convert_half(up_matrix),
            convert_half(down_matrix),
            convert_half(down_adapter_first),
        ],
        axis=0,
    )
    own_seg = lax.dynamic_slice_in_dim(segment_numbers, start_row, tok_dev)
    own_pos = lax.dynamic_slice_in_dim(positions, start_row, tok_dev)
    cosine, sine_part = rope_tables(own_pos)
    in_gathered, cosine, sine_part = tie(in_gathered, cosine, sine_part)
    model_rows = gate_matrix.shape[0]
    by_pairs = row_size == 4 and col_size == 8
    cot_grad = cotangent.astype(jnp.float32)
    cot_mixed = reorder(cotangent, order)
    if by_pairs:
        half = shard.shape[0] // 2
        in_gathered, upper, lower, cot_mixed = tie(
            in_gathered, shard[:half], shard[half:], cot_mixed
        )
        upper_y = swap(upper, "row", 4, 2)
        lower_x = swap(lower, "row", 4, 1)
        cot_two = swap(cot_mixed, "col", 8, 2)
        cot_four = swap(cot_mixed, "col", 8, 4)
    in_width = in_gathered.shape[1] - 128
    in_weight = in_gathered[:, :in_width]
    gains = in_gathered[:, in_width:].astype(jnp.float32)
    gain_attn = gains[:, 0]
    gain_mlp = gains[:, 1]
    inputs = tokens.astype(jnp.float32)
    normed = convert_half(rms_scale(inputs, gain_attn))
    in_pre = matrix_product(normed, in_weight)
    query_pre = in_pre[:, :query_width]
    keyval_pre = in_pre[:, query_width:]
    query_rows = convert_half(
        rotate(query_pre.reshape(tok_dev, NH, HD), cosine[:, None, :], sine_part[:, None, :])
        * scale
    ).reshape(row_total, HD)
    keyval_rows = lax.all_gather(
        jnp.concatenate(
            [
                convert_half(rotate(keyval_pre[:, :HD], cosine, sine_part)),
                convert_half(keyval_pre[:, HD:]),
            ],
            axis=1,
        ),
        "col",
        axis=0,
        tiled=True,
    )
    out_packed = jnp.concatenate(
        [
            convert_half(output_matrix),
            convert_half(output_adapter_first),
            convert_half(output_adapter_second).reshape(gain_len, -1),
            convert_half(down_adapter_second).reshape(gain_len, -1),
        ],
        axis=1,
    )
    keyval_rows, out_packed = tie(keyval_rows, out_packed)
    if by_pairs:
        (keyval_rows, out_packed, upper_y, lower_x, cot_two, cot_four, upper, lower, cot_mixed) = (
            tie(
                keyval_rows,
                out_packed,
                upper_y,
                lower_x,
                cot_two,
                cot_four,
                upper,
                lower,
                cot_mixed,
            )
        )
        upper_x = swap(upper, "row", 4, 1)
        lower_y = swap(lower, "row", 4, 2)
        cot_six = swap(cot_mixed, "col", 8, 6)
    out_gathered = lax.all_gather(out_packed, ("row", "col"), axis=0, tiled=True)
    key_rows = keyval_rows[:, :HD]
    value_rows = keyval_rows[:, HD:]
    row_index = start_row + jnp.arange(row_total, dtype=jnp.int32) // NH
    row_seg = jnp.repeat(own_seg, NH)
    key_index = jnp.arange(group_len, dtype=jnp.int32)
    allowed = (key_index[None, :] <= row_index[:, None]) & (
        (segment_numbers[None, :] == 0) | (segment_numbers[None, :] == row_seg[:, None])
    )
    scores = jnp.where(allowed, product(query_rows, key_rows, contract_last), masked_score)
    top_value = jnp.max(scores, axis=1)
    total_value = jnp.sum(jnp.exp(scores - top_value[:, None]), axis=1)
    log_norm = top_value + jnp.log(total_value)
    probs = convert_half(jnp.exp(scores - log_norm[:, None]))
    mixed_rows = matrix_product(probs, value_rows)
    head_context = convert_half(mixed_rows.reshape(tok_dev, NH * HD))
    if by_pairs:
        head_context, upper_x, lower_y, cot_six, upper_y, lower_x = tie(
            head_context, upper_x, lower_y, cot_six, upper_y, lower_x
        )
        quarter = upper_y.shape[0] // 2
        cot_mine = jnp.concatenate([cot_mixed, cot_two, cot_four, cot_six], axis=0)
        cot_other = swap(cot_mine, "col", 8, 1)
        far_upper = [swap(upper_y[:quarter], "row", 4, 1)]
        far_lower = [swap(lower_x[:quarter], "row", 4, 2)]
    rank_width = output_adapter_first.shape[1]
    out_width = width + rank_width
    upper_width = adapter_rows * width // gain_len
    out_weight = out_gathered[:, :out_width]
    out_upper = out_gathered[:, out_width : out_width + upper_width].reshape(-1, width)
    down_upper = out_gathered[:, out_width + upper_width :].reshape(-1, width)
    out_pre = matrix_product(head_context, out_weight)
    output_rank_rows = convert_half(out_pre[:, width:])
    layer_state = inputs + out_pre[:, :width] + matrix_product(output_rank_rows, out_upper)
    normed_mlp = convert_half(rms_scale(layer_state, gain_mlp))
    normed_mlp = reorder(normed_mlp, order)
    if by_pairs:
        normed_mlp, far_upper[0], far_lower[0], cot_other, upper_y, lower_x = tie(
            normed_mlp, far_upper[0], far_lower[0], cot_other, upper_y, lower_x
        )
        far_upper.append(swap(upper_y[quarter:], "row", 4, 1))
        far_lower.append(swap(lower_x[quarter:], "row", 4, 2))
        pieces = [[shard], [upper_x, lower_x], [upper_y, lower_y], [*far_upper, *far_lower]]
        places = [lax.axis_index("col") ^ (2 * step) for step in range(4)]
        cot_rows = place_blocks(
            [cot_mine[tok_dev * step : tok_dev * (step + 1)] for step in range(4)]
            + [cot_other[tok_dev * step : tok_dev * (step + 1)] for step in range(4)],
            places + [place ^ 1 for place in places],
            8,
        )
    else:
        pieces = [[shard]] + [
            [to_partner(shard, "row", step, row_size)] for step in range(1, row_size)
        ]
        cot_rows = lax.all_gather(cot_mixed, "col", axis=0, tiled=True)
    gate_weight = rows_of(pieces, 0, model_rows)
    up_weight = rows_of(pieces, model_rows, 2 * model_rows)
    down_weight = jnp.concatenate(
        [
            rows_of(pieces, 2 * model_rows, 3 * model_rows),
            rows_of(pieces, 3 * model_rows, 3 * model_rows + down_adapter_first.shape[0]),
        ],
        axis=0,
    )
    ffn_in = lax.all_gather(normed_mlp, "col", axis=0, tiled=True)
    normed_both = with_partner(normed, col_size)
    context_both = with_partner(head_context, col_size)
    rank_both = with_partner(output_rank_rows, col_size)
    cot_both = halves_with_partner(cotangent, col_size)
    rank_part = rank_width // row_size
    upper_mixed = jnp.concatenate(
        [
            lax.dynamic_slice_in_dim(reorder(down_upper, order), place * rank_part, rank_part)
            for place in order
        ],
        axis=0,
    )
    rank_rows = convert_half(product(cot_rows, upper_mixed, contract_last))
    cot_rows = jnp.concatenate([cot_rows, rank_rows], axis=1)
    hidden_grad = matrix_product(cot_rows, down_weight)
    ffn_in, hidden_grad, gate_weight, up_weight, normed_both, context_both, rank_both, cot_both = (
        tie(
            ffn_in,
            hidden_grad,
            gate_weight,
            up_weight,
            normed_both,
            context_both,
            rank_both,
            cot_both,
        )
    )
    gate_values = matrix_product(ffn_in, gate_weight)
    up_values = matrix_product(ffn_in, up_weight)
    hidden_activated = convert_half(jax.nn.gelu(gate_values, approximate=True) * up_values)
    gelu_out, gelu_pull = jax.vjp(partial(jax.nn.gelu, approximate=True), gate_values)
    gate_grad = convert_half(gelu_pull(hidden_grad * up_values)[0])
    up_grad = convert_half(hidden_grad * gelu_out)

    def blocks_of(values):
        size = values.shape[0] // row_size
        return [values[size * step : size * (step + 1)] for step in range(row_size)]

    grad_down = convert_half(product(cot_rows, hidden_activated, contract_first))
    grad_down, gate_grad, up_grad = tie(grad_down, gate_grad, up_grad)
    down_blocks = [
        jnp.concatenate([one, two], axis=0)
        for one, two in zip(blocks_of(grad_down[:width]), blocks_of(grad_down[width:]))
    ]
    half_width = width // 2
    down_split = half_width + rank_width

    def normed_part(start, left_gate, left_up):
        stop = start + half_width
        return convert_half(
            product(left_gate, gate_weight[start:stop], contract_last)
            + product(left_up, up_weight[start:stop], contract_last)
        )

    def col_sum(values):
        return lax.psum_scatter(values, "col", scatter_dimension=0, tiled=True)

    def down_product():
        weight = jnp.concatenate([down_weight[half_width:], down_weight[:half_width]], axis=0)
        return convert_half(product(hidden_activated, weight, contract_last))

    if row_size == 4:
        own_down, far, free, last = split_blocks(down_blocks)
        far = send_pair(far)
        first_part = normed_part(0, gate_grad, up_grad)
        *far, first_part, gate_grad, up_grad, free_x, free_y = tie(
            *far, first_part, gate_grad, up_grad, *free
        )
        first_sum = col_sum(first_part)
        last = add_pair(last, far)
        free = send_pair((free_x, free_y))
        second_part = normed_part(half_width, gate_grad, up_grad)
        *free, second_part, gate_grad, up_grad, last_x, last_y = tie(
            *free, second_part, gate_grad, up_grad, *last
        )
        second_sum = col_sum(second_part)
        last = send_pair((last_x, last_y))
        grad_gate = convert_half(product(ffn_in, gate_grad, contract_first))
        *down_parts, grad_gate, up_grad = tie(own_down, *free, *last, grad_gate, up_grad)
        down_total = finish_sum(down_parts[0], down_parts[1:3], down_parts[3:])
        own_gate, far, free, last = split_blocks(blocks_of(grad_gate))
        far = send_pair(far)
        grad_up = convert_half(product(ffn_in, up_grad, contract_first))
        *far, grad_up, hidden_activated, free_x, free_y = tie(
            *far, grad_up, hidden_activated, *free
        )
        gate_last = add_pair(last, far)
        gate_free = send_pair((free_x, free_y))
        down_partial = down_product()
        *gate_free, last_x, last_y, down_partial, grad_up = tie(
            *gate_free, *gate_last, down_partial, grad_up
        )
        own_up, far, up_free, up_last = split_blocks(blocks_of(grad_up))
        gate_last = send_pair((last_x, last_y))
        up_far = send_pair(far)
    else:
        first_sum = col_sum(normed_part(0, gate_grad, up_grad))
        second_sum = col_sum(normed_part(half_width, gate_grad, up_grad))
        grad_gate = convert_half(product(ffn_in, gate_grad, contract_first))
        grad_up = convert_half(product(ffn_in, up_grad, contract_first))
        down_partial = down_product()
        down_total = row_sum(down_blocks, row_size)
        gate_sum = row_sum(blocks_of(grad_gate), row_size)
        up_sum = row_sum(blocks_of(grad_up), row_size)
    down_sum, rank_sum = down_total[:model_rows], down_total[model_rows:]
    summed = col_sum(down_partial[:, :down_split])
    down_rest = down_partial[:, down_split:]
    normed_grad = jnp.concatenate([first_sum, second_sum], axis=1)

    normed_grad = reorder(normed_grad, order).astype(jnp.float32)
    state_out, norm_pull = jax.vjp(rms_scale, layer_state, gain_mlp)
    state_part, grad_gain_mlp = norm_pull(normed_grad)
    state_grad = cot_grad + state_part
    attn_grad = convert_half(state_grad)
    rank_out_grad = convert_half(product(attn_grad, out_upper, contract_last))
    out_grad = jnp.concatenate([attn_grad, rank_out_grad], axis=1)
    context_grad = product(out_grad, out_weight, contract_last)
    grad_rows = convert_half(context_grad).reshape(row_total, HD)
    delta = jnp.sum(grad_rows.astype(jnp.float32) * mixed_rows, axis=1)
    weight_grad = product(grad_rows, value_rows, contract_last)
    score_grad = convert_half(probs.astype(jnp.float32) * (weight_grad - delta[:, None]))
    if row_size == 4:
        *gate_last, far_x, far_y, score_grad, free_x, free_y = tie(
            *gate_last, *up_far, score_grad, *up_free
        )
        gate_sum = finish_sum(own_gate, gate_free, gate_last)
        up_last = add_pair(up_last, (far_x, far_y))
        up_free = send_pair((free_x, free_y))
    query_acc = matrix_product(score_grad, key_rows)
    query_grad = convert_half(
        unrotate(
            query_acc.reshape(tok_dev, NH, HD) * scale, cosine[:, None, :], sine_part[:, None, :]
        ).reshape(tok_dev, NH * HD)
    )
    query_grad, score_grad = tie(query_grad, score_grad)
    key_acc = product(score_grad, query_rows, contract_first)
    value_acc = product(probs, grad_rows, contract_first)
    keyval_part = jnp.concatenate([convert_half(key_acc), convert_half(value_acc)], axis=1)
    if row_size == 4:
        *up_free, keyval_part, query_grad, last_x, last_y = tie(
            *up_free, keyval_part, query_grad, *up_last
        )
        up_last = send_pair((last_x, last_y))
    keyval_part, summed = tie(keyval_part, summed)
    keyval_sum = col_sum(keyval_part)
    core = lax.axis_index("col") % 2
    query_right = halves_with_partner(query_grad, col_size)
    grad_query = convert_half(product(normed_both, query_right, contract_first))
    chips = devices // 2

    def shared(values):
        return convert_half(values).reshape(chips, 2 * gain_len, -1)

    out_right = halves_with_partner(out_grad[:, :width], col_size)
    rank_right = halves_with_partner(out_grad[:, width:], col_size)
    grad_out = product(
        context_both, jnp.concatenate([out_right, rank_right], axis=1), contract_first
    )
    grad_out_upper = product(rank_both, out_right, contract_first)
    out_group = jnp.concatenate([shared(grad_out), shared(grad_out_upper)], axis=2)
    query_group = shared(grad_query)
    if row_size == 4:
        *up_last, out_group, query_group = tie(*up_last, out_group, query_group)
        up_sum = finish_sum(own_up, up_free, up_last)
    down_rank_rows = reorder(summed[:, half_width:], order)
    keyval_sum, down_rest = tie(keyval_sum, down_rest)
    down_rest = col_sum(down_rest)
    down_all = jnp.concatenate([down_rest, summed[:, :half_width]], axis=1)
    layer_out = convert_half(
        layer_state
        + reorder(down_all, order).astype(jnp.float32)
        + matrix_product(down_rank_rows, down_upper)
    )
    keyval_sum = keyval_sum.astype(jnp.float32)
    keyval_grad = jnp.concatenate(
        [convert_half(unrotate(keyval_sum[:, :HD], cosine, sine_part)), convert_half(keyval_sum[:, HD:])],
        axis=1,
    )
    in_grad = jnp.concatenate([query_grad, keyval_grad], axis=1)
    normed_back = product(in_grad, in_weight, contract_last)
    normed_out, first_pull = jax.vjp(rms_scale, inputs, gain_attn)
    input_part, grad_gain_attn = first_pull(normed_back)
    input_grad = convert_half(state_grad + input_part)

    grad_keyval = product(
        normed_both, halves_with_partner(keyval_grad, col_size), contract_first
    )
    grad_down_upper = product(
        with_partner(down_rank_rows, col_size), cot_both, contract_first
    )
    gains = jnp.stack([grad_gain_attn, grad_gain_mlp])
    gain = lax.dynamic_index_in_dim(gains, core, 0, keepdims=False) + swap(
        lax.dynamic_index_in_dim(gains, 1 - core, 0, keepdims=False), "col", col_size, 1
    )
    out_first, out_second = share_cores(
        scatter_chips(out_group, row_size, col_size), col_size
    )
    query_first, query_second = share_cores(
        scatter_chips(query_group, row_size, col_size), col_size
    )
    keyval_first, keyval_second = share_cores(
        scatter_chips(
            jnp.concatenate(
                [
                    shared(grad_keyval),
                    shared(grad_down_upper),
                    jnp.pad(shared(gain), ((0, 0), (0, 0), (0, 127))),
                ],
                axis=2,
            ),
            row_size,
            col_size,
            parts=1,
        ),
        col_size,
    )

    def joined(first, second, start, size):
        return jnp.concatenate([first[:, start : start + size], second[:, start : start + size]], axis=1)

    def joined_rows(first, second, start, size):
        return jnp.concatenate(
            [
                half[:, start : start + size].reshape(adapter_rows, -1)
                for half in (first, second)
            ],
            axis=1,
        )

    half_rank = rank_width // 2
    half_keyval = key_value_matrix.shape[1] // 2
    half_upper = upper_width // 2
    return (
        layer_out,
        input_grad,
        keyval_first[:, half_keyval + half_upper],
        joined(query_first, query_second, 0, query_width // 2),
        joined(keyval_first, keyval_second, 0, half_keyval),
        joined(out_first, out_second, 0, half_width),
        joined(out_first, out_second, half_width, half_rank),
        joined_rows(out_first, out_second, half_width + half_rank, half_upper),
        keyval_second[:, half_keyval + half_upper],
        gate_sum,
        up_sum,
        down_sum,
        rank_sum,
        joined_rows(keyval_first, keyval_second, half_keyval, half_upper),
    )


def solution(mesh):
    return jax.shard_map(
        per_device,
        mesh=mesh,
        in_specs=(
            P(("row", "col"), None),
            P(("row", "col"), None),
            P("row"),
            P("row"),
            P(("row", "col")),
            P(("row", "col"), None),
            P(("row", "col"), None),
            P(("row", "col"), None),
            P(("row", "col"), None),
            P(("row", "col"), None),
            P(("row", "col")),
            P("row", "col"),
            P("row", "col"),
            P("row", "col"),
            P("row", "col"),
            P(("row", "col"), None),
        ),
        out_specs=(
            P(("row", "col"), None),
            P(("row", "col"), None),
            P(("row", "col")),
            P(("row", "col"), None),
            P(("row", "col"), None),
            P(("row", "col"), None),
            P(("row", "col"), None),
            P(("row", "col"), None),
            P(("row", "col")),
            P("row", "col"),
            P("row", "col"),
            P("row", "col"),
            P("row", "col"),
            P(("row", "col"), None),
        ),
        check_vma=False,
    )
```

```python
from functools import partial

import jax
import jax.numpy as jnp
from jax import lax
from jax.sharding import PartitionSpec as P

MODEL_WIDTH = 2048
NH = 8
HD = 256


masked_score = -1e30
epsilon = 1e-06
contract_last = (((1,), (1,)), ((), ()))
contract_first = (((0,), (0,)), ((), ()))


def convert_half(values):
    return values.astype(jnp.bfloat16)


def product(left_side, right_side, dims):
    return lax.dot_general(left_side, right_side, dims, preferred_element_type=jnp.float32)


def matrix_product(left_side, right_side):
    return jnp.dot(left_side, right_side, preferred_element_type=jnp.float32)


def rms_scale(values, gain):
    return values * lax.rsqrt(jnp.mean(values * values, axis=-1, keepdims=True) + epsilon) * gain


def rope_tables(positions):
    half_width = HD // 2
    inverse = 10000.0 ** (-jnp.arange(half_width, dtype=jnp.float32) * 2.0 / HD)
    angles = positions.astype(jnp.float32)[:, None] * inverse[None, :]
    return (jnp.cos(angles), jnp.sin(angles))


def rotate(tensor, cosine, sine_part):
    half_width = tensor.shape[-1] // 2
    leading = tensor[..., :half_width]
    trailing = tensor[..., half_width:]
    return jnp.concatenate(
        [leading * cosine - trailing * sine_part, trailing * cosine + leading * sine_part], axis=-1
    )


def unrotate(tensor, cosine, sine_part):
    half_width = tensor.shape[-1] // 2
    leading = tensor[..., :half_width]
    trailing = tensor[..., half_width:]
    return jnp.concatenate(
        [leading * cosine + trailing * sine_part, trailing * cosine - leading * sine_part], axis=-1
    )


def swap(values, axis, size, bit):
    return lax.ppermute(values, axis, [(i, i ^ bit) for i in range(size)])


def partner(own, step):
    return own ^ step


def to_partner(values, axis, step, size):
    return lax.ppermute(values, axis, [(i, partner(i, step)) for i in range(size)])


def reorder(values, order):
    width = values.shape[-1] // len(order)
    return jnp.concatenate(
        [lax.dynamic_slice_in_dim(values, place * width, width, axis=-1) for place in order], axis=-1
    )


def tie(*values):
    return lax.optimization_barrier(values)


def place_blocks(blocks, places, count):
    rows = blocks[0].shape[0]
    whole = jnp.zeros((rows * count, blocks[0].shape[1]), blocks[0].dtype)
    for block, place in zip(blocks, places):
        whole = lax.dynamic_update_slice_in_dim(whole, block, place * rows, axis=0)
    return whole


def rows_of(pieces, start, stop):
    found = []
    for parts in pieces:
        offset = 0
        for part in parts:
            first, last = max(start - offset, 0), min(stop - offset, part.shape[0])
            if first < last:
                found.append(part[first:last])
            offset += part.shape[0]
    return jnp.concatenate(found, axis=0)


def split_blocks(blocks):
    own, near_x, near_y, far = blocks
    half = own.shape[0] // 2
    return (
        own,
        (far[:half], far[half:]),
        (near_x[:half], near_y[half:]),
        (near_x[half:], near_y[:half]),
    )


def send_pair(pair):
    return swap(pair[0], "row", 4, 1), swap(pair[1], "row", 4, 2)


def add_pair(pair, got):
    return add_half(pair[0], got[1]), add_half(pair[1], got[0])


def finish_sum(own, free, last):
    half = own.shape[0] // 2
    upper = add_full(own[:half], free[0], last[1])
    lower = add_full(own[half:], last[0], free[1])
    return jnp.concatenate([upper, lower], axis=0)


def row_sum(blocks, size):
    total = blocks[0].astype(jnp.float32)
    for step in range(1, size):
        total = total + to_partner(blocks[step], "row", step, size).astype(jnp.float32)
    return total


def add_full(first, second, third):
    return first.astype(jnp.float32) + second.astype(jnp.float32) + third.astype(jnp.float32)


def add_half(first, second):
    return convert_half(first.astype(jnp.float32) + second.astype(jnp.float32))


def halve(values, dim, axis, size, bit):
    own = (lax.axis_index(axis) // bit) % 2
    kept = lax.dynamic_slice_in_dim(values, own, 1, axis=dim)
    sent = lax.dynamic_slice_in_dim(values, 1 - own, 1, axis=dim)
    return add_half(kept, swap(sent, axis, size, bit))


def row_stages(values, row_size, col_size, parts=2):
    chips, rows, width = values.shape
    line = col_size // 2
    bits = [1 << k for k in reversed(range(row_size.bit_length() - 1))]
    shaped = values.reshape((2,) * len(bits) + (line, rows, width))
    part = width // parts
    pieces = []
    for place in range(parts):
        piece = shaped[..., part * place : part * (place + 1)]
        for bit in bits if place % 2 == 0 else bits[::-1]:
            piece = halve(piece, bits.index(bit), "row", row_size, bit)
        pieces.append(piece.reshape(line, rows, part))
    return jnp.concatenate(pieces, axis=-1)


def line_stage(whole, col_size):
    line = col_size // 2
    at = lax.axis_index("col") // 2
    total = lax.dynamic_index_in_dim(whole, at, 0, keepdims=False).astype(jnp.float32)
    for step in range(1, line):
        block = lax.dynamic_index_in_dim(whole, at ^ step, 0, keepdims=False)
        total = total + swap(block, "col", col_size, 2 * step).astype(jnp.float32)
    return total


def share_cores(values, col_size):
    core = lax.axis_index("col") % 2
    rows = values.shape[0] // 2
    kept = lax.dynamic_slice_in_dim(values, core * rows, rows)
    got = swap(lax.dynamic_slice_in_dim(values, (1 - core) * rows, rows), "col", col_size, 1)
    first = core == 0
    return jnp.where(first, kept, got), jnp.where(first, got, kept)


def core_half(values, core):
    half = values.shape[-1] // 2
    return lax.dynamic_slice_in_dim(values, core * half, half, axis=-1)


def with_partner(values, col_size):
    got = swap(values, "col", col_size, 1)
    return jnp.concatenate([values, got], axis=0)


def halves_with_partner(values, col_size):
    core = lax.axis_index("col") % 2
    got = swap(core_half(values, 1 - core), "col", col_size, 1)
    return jnp.concatenate([core_half(values, core), got], axis=0)


def per_device(
    tokens,
    cotangent,
    segment_numbers,
    positions,
    attention_norm_gain,
    query_matrix,
    key_value_matrix,
    output_matrix,
    output_adapter_first,
    output_adapter_second,
    feedforward_norm_gain,
    gate_matrix,
    up_matrix,
    down_matrix,
    down_adapter_first,
    down_adapter_second,
):
    row_size = lax.axis_size("row")
    col_size = lax.axis_size("col")
    devices = row_size * col_size
    row_at = lax.axis_index("row")
    tok_dev, width = tokens.shape
    group_len = segment_numbers.shape[0]
    row_total = tok_dev * NH
    query_width = query_matrix.shape[1]
    adapter_rows = output_adapter_second.shape[0]
    gain_len = attention_norm_gain.shape[0]
    start_row = lax.axis_index("col") * tok_dev
    scale = HD ** (-0.5)
    order = [partner(row_at, step) for step in range(row_size)]

    in_gathered = lax.all_gather(
        jnp.concatenate(
            [
                convert_half(query_matrix),
                convert_half(key_value_matrix),
                convert_half(
                    jnp.pad(
                        jnp.stack([attention_norm_gain, feedforward_norm_gain], axis=1),
                        ((0, 0), (0, 126)),
                    )
                ),
            ],
            axis=1,
        ),
        ("row", "col"),
        axis=0,
        tiled=True,
    )
    shard = jnp.concatenate(
        [
            convert_half(gate_matrix),
            convert_half(up_matrix),
            convert_half(down_matrix),
            convert_half(down_adapter_first),
        ],
        axis=0,
    )
    own_seg = lax.dynamic_slice_in_dim(segment_numbers, start_row, tok_dev)
    own_pos = lax.dynamic_slice_in_dim(positions, start_row, tok_dev)
    cosine, sine_part = rope_tables(own_pos)
    out_packed = jnp.concatenate(
        [
            convert_half(output_matrix),
            convert_half(output_adapter_first),
            convert_half(output_adapter_second).reshape(gain_len, -1),
            convert_half(down_adapter_second).reshape(gain_len, -1),
        ],
        axis=1,
    )
    in_gathered, cosine, sine_part, out_packed = tie(in_gathered, cosine, sine_part, out_packed)
    out_gathered = lax.all_gather(out_packed, ("row", "col"), axis=0, tiled=True)
    model_rows = gate_matrix.shape[0]
    by_pairs = row_size == 4 and col_size == 8
    cot_grad = cotangent.astype(jnp.float32)
    cot_mixed = reorder(cotangent, order)
    if by_pairs:
        half = shard.shape[0] // 2
        in_gathered, upper, lower, cot_mixed = tie(
            in_gathered, shard[:half], shard[half:], cot_mixed
        )
        upper_y = swap(upper, "row", 4, 2)
        lower_x = swap(lower, "row", 4, 1)
        cot_two = swap(cot_mixed, "col", 8, 2)
    in_width = in_gathered.shape[1] - 128
    in_weight = in_gathered[:, :in_width]
    gains = in_gathered[:, in_width:].astype(jnp.float32)
    gain_attn = gains[:, 0]
    gain_mlp = gains[:, 1]
    inputs = tokens.astype(jnp.float32)
    normed = convert_half(rms_scale(inputs, gain_attn))
    in_pre = matrix_product(normed, in_weight)
    query_pre = in_pre[:, :query_width]
    keyval_pre = in_pre[:, query_width:]
    query_rows = convert_half(
        rotate(query_pre.reshape(tok_dev, NH, HD), cosine[:, None, :], sine_part[:, None, :])
        * scale
    ).reshape(row_total, HD)
    keyval_own = jnp.concatenate(
        [
            convert_half(rotate(keyval_pre[:, :HD], cosine, sine_part)),
            convert_half(keyval_pre[:, HD:]),
        ],
        axis=1,
    )
    if by_pairs:
        places = [lax.axis_index("col") ^ (2 * step) for step in range(4)]
        places = places + [place ^ 1 for place in places]

        def gathered(mine, other):
            parts = [
                side[tok_dev * step : tok_dev * (step + 1)]
                for side in (mine, other)
                for step in range(4)
            ]
            return place_blocks(parts, places, 8)

        keyval_mine = jnp.concatenate(
            [keyval_own] + [swap(keyval_own, "col", 8, 2 * step) for step in range(1, 4)], axis=0
        )
        keyval_rows = gathered(keyval_mine, swap(keyval_mine, "col", 8, 1))
    else:
        keyval_rows = lax.all_gather(keyval_own, "col", axis=0, tiled=True)
    key_rows = keyval_rows[:, :HD]
    value_rows = keyval_rows[:, HD:]
    row_index = start_row + jnp.arange(row_total, dtype=jnp.int32) // NH
    row_seg = jnp.repeat(own_seg, NH)
    key_index = jnp.arange(group_len, dtype=jnp.int32)
    allowed = (key_index[None, :] <= row_index[:, None]) & (
        (segment_numbers[None, :] == 0) | (segment_numbers[None, :] == row_seg[:, None])
    )
    scores = jnp.where(allowed, product(query_rows, key_rows, contract_last), masked_score)
    top_value = jnp.max(scores, axis=1)
    total_value = jnp.sum(jnp.exp(scores - top_value[:, None]), axis=1)
    log_norm = top_value + jnp.log(total_value)
    if by_pairs:
        log_norm, upper_y, lower_x, cot_two, upper, lower, cot_mixed = tie(
            log_norm, upper_y, lower_x, cot_two, upper, lower, cot_mixed
        )
        upper_x = swap(upper, "row", 4, 1)
        lower_y = swap(lower, "row", 4, 2)
        cot_four = swap(cot_mixed, "col", 8, 4)
        cot_six = swap(cot_mixed, "col", 8, 6)
    probs = convert_half(jnp.exp(scores - log_norm[:, None]))
    mixed_rows = matrix_product(probs, value_rows)
    head_context = convert_half(mixed_rows.reshape(tok_dev, NH * HD))
    rank_width = output_adapter_first.shape[1]
    out_width = width + rank_width
    upper_width = adapter_rows * width // gain_len
    out_weight = out_gathered[:, :out_width]
    out_upper = out_gathered[:, out_width : out_width + upper_width].reshape(-1, width)
    down_upper = out_gathered[:, out_width + upper_width :].reshape(-1, width)
    out_pre = matrix_product(head_context, out_weight)
    output_rank_rows = convert_half(out_pre[:, width:])
    layer_state = inputs + out_pre[:, :width] + matrix_product(output_rank_rows, out_upper)
    normed_mlp = convert_half(rms_scale(layer_state, gain_mlp))
    normed_mlp = reorder(normed_mlp, order)
    if by_pairs:
        normed_mlp, upper_x, lower_y, cot_four, cot_six, upper_y, lower_x = tie(
            normed_mlp, upper_x, lower_y, cot_four, cot_six, upper_y, lower_x
        )
        far_upper = [swap(upper_y, "row", 4, 1)]
        far_lower = [swap(lower_x, "row", 4, 2)]
        cot_mine = jnp.concatenate([cot_mixed, cot_two, cot_four, cot_six], axis=0)
        cot_rows = gathered(cot_mine, swap(cot_mine, "col", 8, 1))
        pieces = [[shard], [upper_x, lower_x], [upper_y, lower_y], [*far_upper, *far_lower]]
    else:
        pieces = [[shard]] + [
            [to_partner(shard, "row", step, row_size)] for step in range(1, row_size)
        ]
        cot_rows = lax.all_gather(cot_mixed, "col", axis=0, tiled=True)
    gate_weight = rows_of(pieces, 0, model_rows)
    up_weight = rows_of(pieces, model_rows, 2 * model_rows)
    down_weight = jnp.concatenate(
        [
            rows_of(pieces, 2 * model_rows, 3 * model_rows),
            rows_of(pieces, 3 * model_rows, 3 * model_rows + down_adapter_first.shape[0]),
        ],
        axis=0,
    )
    ffn_in = lax.all_gather(normed_mlp, "col", axis=0, tiled=True)
    normed_both = with_partner(normed, col_size)
    context_both = with_partner(head_context, col_size)
    rank_both = with_partner(output_rank_rows, col_size)
    cot_both = halves_with_partner(cotangent, col_size)
    rank_part = rank_width // row_size
    upper_mixed = jnp.concatenate(
        [
            lax.dynamic_slice_in_dim(reorder(down_upper, order), place * rank_part, rank_part)
            for place in order
        ],
        axis=0,
    )
    rank_rows = convert_half(product(cot_rows, upper_mixed, contract_last))
    cot_rows = jnp.concatenate([cot_rows, rank_rows], axis=1)
    hidden_grad = matrix_product(cot_rows, down_weight)
    ffn_in, hidden_grad, gate_weight, up_weight, normed_both, context_both, rank_both, cot_both = (
        tie(
            ffn_in,
            hidden_grad,
            gate_weight,
            up_weight,
            normed_both,
            context_both,
            rank_both,
            cot_both,
        )
    )
    gate_values = matrix_product(ffn_in, gate_weight)
    up_values = matrix_product(ffn_in, up_weight)
    hidden_activated = convert_half(jax.nn.gelu(gate_values, approximate=True) * up_values)
    gelu_out, gelu_pull = jax.vjp(partial(jax.nn.gelu, approximate=True), gate_values)
    gate_grad = convert_half(gelu_pull(hidden_grad * up_values)[0])
    up_grad = convert_half(hidden_grad * gelu_out)

    def blocks_of(values):
        size = values.shape[0] // row_size
        return [values[size * step : size * (step + 1)] for step in range(row_size)]

    grad_down = convert_half(product(cot_rows, hidden_activated, contract_first))
    grad_down, gate_grad, up_grad = tie(grad_down, gate_grad, up_grad)
    down_blocks = [
        jnp.concatenate([one, two], axis=0)
        for one, two in zip(blocks_of(grad_down[:width]), blocks_of(grad_down[width:]))
    ]
    half_width = width // 2

    def normed_part(start, left_gate, left_up):
        stop = start + half_width
        return convert_half(
            product(left_gate, gate_weight[start:stop], contract_last)
            + product(left_up, up_weight[start:stop], contract_last)
        )

    def col_sum(values):
        return lax.psum_scatter(values, "col", scatter_dimension=0, tiled=True)

    def down_product(start, stop):
        return convert_half(product(hidden_activated, down_weight[start:stop], contract_last))

    if row_size == 4:
        own_down, far, free, last = split_blocks(down_blocks)
        far = send_pair(far)
        first_part = normed_part(0, gate_grad, up_grad)
        *far, first_part, gate_grad, up_grad, free_x, free_y = tie(
            *far, first_part, gate_grad, up_grad, *free
        )
        first_sum = col_sum(first_part)
        last = add_pair(last, far)
        free = send_pair((free_x, free_y))
        second_part = normed_part(half_width, gate_grad, up_grad)
        *free, second_part, gate_grad, up_grad, last_x, last_y = tie(
            *free, second_part, gate_grad, up_grad, *last
        )
        rank_partial = down_product(width, width + rank_width)
        second_part, rank_partial, hidden_activated = tie(
            second_part, rank_partial, hidden_activated
        )
        second_sum = col_sum(second_part)
        last = send_pair((last_x, last_y))
        grad_gate = convert_half(product(ffn_in, gate_grad, contract_first))
        *down_parts, grad_gate, up_grad = tie(own_down, *free, *last, grad_gate, up_grad)
        down_total = finish_sum(down_parts[0], down_parts[1:3], down_parts[3:])
        own_gate, far, free, last = split_blocks(blocks_of(grad_gate))
        far = send_pair(far)
        grad_up = convert_half(product(ffn_in, up_grad, contract_first))
        *far, grad_up, free_x, free_y = tie(*far, grad_up, *free)
        gate_last = add_pair(last, far)
        gate_free = send_pair((free_x, free_y))
        own_up, far, up_free, up_last = split_blocks(blocks_of(grad_up))
        up_far = send_pair(far)
    else:
        first_sum = col_sum(normed_part(0, gate_grad, up_grad))
        second_sum = col_sum(normed_part(half_width, gate_grad, up_grad))
        rank_partial = down_product(width, width + rank_width)
        grad_gate = convert_half(product(ffn_in, gate_grad, contract_first))
        grad_up = convert_half(product(ffn_in, up_grad, contract_first))
        down_total = row_sum(down_blocks, row_size)
        gate_sum = row_sum(blocks_of(grad_gate), row_size)
        up_sum = row_sum(blocks_of(grad_up), row_size)
    down_sum, rank_sum = down_total[:model_rows], down_total[model_rows:]
    rank_sums = col_sum(rank_partial)
    normed_grad = jnp.concatenate([first_sum, second_sum], axis=1)

    normed_grad = reorder(normed_grad, order).astype(jnp.float32)
    state_out, norm_pull = jax.vjp(rms_scale, layer_state, gain_mlp)
    state_part, grad_gain_mlp = norm_pull(normed_grad)
    state_grad = cot_grad + state_part
    attn_grad = convert_half(state_grad)
    rank_out_grad = convert_half(product(attn_grad, out_upper, contract_last))
    out_grad = jnp.concatenate([attn_grad, rank_out_grad], axis=1)
    context_grad = product(out_grad, out_weight, contract_last)
    grad_rows = convert_half(context_grad).reshape(row_total, HD)
    if row_size == 4:
        *gate_free, far_x, far_y, grad_rows, last_x, last_y, free_x, free_y = tie(
            *gate_free, *up_far, grad_rows, *gate_last, *up_free
        )
        up_last = add_pair(up_last, (far_x, far_y))
        gate_last = send_pair((last_x, last_y))
        up_free = (free_x, free_y)
    delta = jnp.sum(grad_rows.astype(jnp.float32) * mixed_rows, axis=1)
    weight_grad = product(grad_rows, value_rows, contract_last)
    score_grad = convert_half(probs.astype(jnp.float32) * (weight_grad - delta[:, None]))
    query_acc = matrix_product(score_grad, key_rows)
    query_grad = convert_half(
        unrotate(
            query_acc.reshape(tok_dev, NH, HD) * scale, cosine[:, None, :], sine_part[:, None, :]
        ).reshape(tok_dev, NH * HD)
    )
    query_grad, score_grad = tie(query_grad, score_grad)
    key_acc = product(score_grad, query_rows, contract_first)
    value_acc = product(probs, grad_rows, contract_first)
    keyval_part = jnp.concatenate([convert_half(key_acc), convert_half(value_acc)], axis=1)
    keyval_part, rank_sums = tie(keyval_part, rank_sums)
    if row_size == 4:
        *gate_last, keyval_part, free_x, free_y = tie(*gate_last, keyval_part, *up_free)
        gate_sum = finish_sum(own_gate, gate_free, gate_last)
        up_free = send_pair((free_x, free_y))
    keyval_sum = col_sum(keyval_part)
    core = lax.axis_index("col") % 2
    query_right = halves_with_partner(query_grad, col_size)
    grad_query = convert_half(product(normed_both, query_right, contract_first))
    chips = devices // 2

    def shared(values):
        return convert_half(values).reshape(chips, 2 * gain_len, -1)

    out_right = halves_with_partner(out_grad[:, :width], col_size)
    rank_right = halves_with_partner(out_grad[:, width:], col_size)
    grad_out = product(
        context_both, jnp.concatenate([out_right, rank_right], axis=1), contract_first
    )
    grad_out_upper = product(rank_both, out_right, contract_first)
    out_group = jnp.concatenate([shared(grad_out), shared(grad_out_upper)], axis=2)
    query_group = shared(grad_query)
    down_partial = down_product(0, width)
    if row_size == 4:
        *up_free, keyval_sum, down_partial, out_group, query_group, last_x, last_y = tie(
            *up_free, keyval_sum, down_partial, out_group, query_group, *up_last
        )
        up_sum = finish_sum(own_up, up_free, send_pair((last_x, last_y)))
    else:
        keyval_sum, down_partial = tie(keyval_sum, down_partial)
    query_lines = row_stages(query_group, row_size, col_size)
    out_lines = row_stages(out_group, row_size, col_size)
    down_rank_rows = reorder(rank_sums, order)
    summed = col_sum(down_partial)
    layer_out = convert_half(
        layer_state
        + reorder(summed, order).astype(jnp.float32)
        + matrix_product(down_rank_rows, down_upper)
    )
    keyval_sum = keyval_sum.astype(jnp.float32)
    keyval_grad = jnp.concatenate(
        [convert_half(unrotate(keyval_sum[:, :HD], cosine, sine_part)), convert_half(keyval_sum[:, HD:])],
        axis=1,
    )
    in_grad = jnp.concatenate([query_grad, keyval_grad], axis=1)
    normed_back = product(in_grad, in_weight, contract_last)
    normed_out, first_pull = jax.vjp(rms_scale, inputs, gain_attn)
    input_part, grad_gain_attn = first_pull(normed_back)
    input_grad = convert_half(state_grad + input_part)

    grad_keyval = product(
        normed_both, halves_with_partner(keyval_grad, col_size), contract_first
    )
    grad_down_upper = product(
        with_partner(down_rank_rows, col_size), cot_both, contract_first
    )
    gains = jnp.stack([grad_gain_attn, grad_gain_mlp])
    gain = lax.dynamic_index_in_dim(gains, core, 0, keepdims=False) + swap(
        lax.dynamic_index_in_dim(gains, 1 - core, 0, keepdims=False), "col", col_size, 1
    )
    keyval_group = jnp.concatenate(
        [
            shared(grad_keyval),
            shared(grad_down_upper),
            jnp.pad(shared(gain), ((0, 0), (0, 0), (0, 127))),
        ],
        axis=2,
    )
    lines = jnp.concatenate([query_lines, out_lines], axis=2)
    lines, keyval_group = tie(lines, keyval_group)
    first, second = share_cores(line_stage(lines, col_size), col_size)
    keyval_first, keyval_second = share_cores(
        line_stage(row_stages(keyval_group, row_size, col_size, parts=1), col_size), col_size
    )
    half_query = query_width // 2
    query_first, query_second = first[:, :half_query], second[:, :half_query]
    out_first, out_second = first[:, half_query:], second[:, half_query:]

    def joined(first, second, start, size):
        return jnp.concatenate([first[:, start : start + size], second[:, start : start + size]], axis=1)

    def joined_rows(first, second, start, size):
        return jnp.concatenate(
            [
                half[:, start : start + size].reshape(adapter_rows, -1)
                for half in (first, second)
            ],
            axis=1,
        )

    half_rank = rank_width // 2
    half_keyval = key_value_matrix.shape[1] // 2
    half_upper = upper_width // 2
    return (
        layer_out,
        input_grad,
        keyval_first[:, half_keyval + half_upper],
        joined(query_first, query_second, 0, query_width // 2),
        joined(keyval_first, keyval_second, 0, half_keyval),
        joined(out_first, out_second, 0, half_width),
        joined(out_first, out_second, half_width, half_rank),
        joined_rows(out_first, out_second, half_width + half_rank, half_upper),
        keyval_second[:, half_keyval + half_upper],
        gate_sum,
        up_sum,
        down_sum,
        rank_sum,
        joined_rows(keyval_first, keyval_second, half_keyval, half_upper),
    )


def solution(mesh):
    return jax.shard_map(
        per_device,
        mesh=mesh,
        in_specs=(
            P(("row", "col"), None),
            P(("row", "col"), None),
            P("row"),
            P("row"),
            P(("row", "col")),
            P(("row", "col"), None),
            P(("row", "col"), None),
            P(("row", "col"), None),
            P(("row", "col"), None),
            P(("row", "col"), None),
            P(("row", "col")),
            P("row", "col"),
            P("row", "col"),
            P("row", "col"),
            P("row", "col"),
            P(("row", "col"), None),
        ),
        out_specs=(
            P(("row", "col"), None),
            P(("row", "col"), None),
            P(("row", "col")),
            P(("row", "col"), None),
            P(("row", "col"), None),
            P(("row", "col"), None),
            P(("row", "col"), None),
            P(("row", "col"), None),
            P(("row", "col")),
            P("row", "col"),
            P("row", "col"),
            P("row", "col"),
            P("row", "col"),
            P(("row", "col"), None),
        ),
        check_vma=False,
    )
```

```python
from functools import partial

import jax
import jax.numpy as jnp
from jax import lax
from jax.sharding import PartitionSpec as P

MODEL_WIDTH = 2048
NH = 8
HD = 256


masked_score = -1e30
epsilon = 1e-06
contract_last = (((1,), (1,)), ((), ()))
contract_first = (((0,), (0,)), ((), ()))


def convert_half(values):
    return values.astype(jnp.bfloat16)


def product(left_side, right_side, dims):
    return lax.dot_general(left_side, right_side, dims, preferred_element_type=jnp.float32)


def matrix_product(left_side, right_side):
    return jnp.dot(left_side, right_side, preferred_element_type=jnp.float32)


def rms_scale(values, gain):
    return values * lax.rsqrt(jnp.mean(values * values, axis=-1, keepdims=True) + epsilon) * gain


def rope_tables(positions):
    half_width = HD // 2
    inverse = 10000.0 ** (-jnp.arange(half_width, dtype=jnp.float32) * 2.0 / HD)
    angles = positions.astype(jnp.float32)[:, None] * inverse[None, :]
    return (jnp.cos(angles), jnp.sin(angles))


def rotate(tensor, cosine, sine_part):
    half_width = tensor.shape[-1] // 2
    leading = tensor[..., :half_width]
    trailing = tensor[..., half_width:]
    return jnp.concatenate(
        [leading * cosine - trailing * sine_part, trailing * cosine + leading * sine_part], axis=-1
    )


def unrotate(tensor, cosine, sine_part):
    half_width = tensor.shape[-1] // 2
    leading = tensor[..., :half_width]
    trailing = tensor[..., half_width:]
    return jnp.concatenate(
        [leading * cosine + trailing * sine_part, trailing * cosine - leading * sine_part], axis=-1
    )


def swap(values, axis, size, bit):
    return lax.ppermute(values, axis, [(i, i ^ bit) for i in range(size)])


def partner(own, step):
    return own ^ step


def to_partner(values, axis, step, size):
    return lax.ppermute(values, axis, [(i, partner(i, step)) for i in range(size)])


def reorder(values, order):
    width = values.shape[-1] // len(order)
    return jnp.concatenate(
        [lax.dynamic_slice_in_dim(values, place * width, width, axis=-1) for place in order], axis=-1
    )


def tie(*values):
    return lax.optimization_barrier(values)


def place_blocks(blocks, places, count):
    rows = blocks[0].shape[0]
    whole = jnp.zeros((rows * count, blocks[0].shape[1]), blocks[0].dtype)
    for block, place in zip(blocks, places):
        whole = lax.dynamic_update_slice_in_dim(whole, block, place * rows, axis=0)
    return whole


def rows_of(pieces, start, stop):
    found = []
    for parts in pieces:
        offset = 0
        for part in parts:
            first, last = max(start - offset, 0), min(stop - offset, part.shape[0])
            if first < last:
                found.append(part[first:last])
            offset += part.shape[0]
    return jnp.concatenate(found, axis=0)


def split_blocks(blocks):
    own, near_x, near_y, far = blocks
    half = own.shape[0] // 2
    return (
        own,
        (far[:half], far[half:]),
        (near_x[:half], near_y[half:]),
        (near_x[half:], near_y[:half]),
    )


def send_pair(pair):
    return swap(pair[0], "row", 4, 1), swap(pair[1], "row", 4, 2)


def add_pair(pair, got):
    return add_half(pair[0], got[1]), add_half(pair[1], got[0])


def finish_sum(own, free, last):
    half = own.shape[0] // 2
    upper = add_full(own[:half], free[0], last[1])
    lower = add_full(own[half:], last[0], free[1])
    return jnp.concatenate([upper, lower], axis=0)


def row_sum(blocks, size):
    total = blocks[0].astype(jnp.float32)
    for step in range(1, size):
        total = total + to_partner(blocks[step], "row", step, size).astype(jnp.float32)
    return total


def add_full(first, second, third):
    return first.astype(jnp.float32) + second.astype(jnp.float32) + third.astype(jnp.float32)


def add_half(first, second):
    return convert_half(first.astype(jnp.float32) + second.astype(jnp.float32))


def halve(values, dim, axis, size, bit):
    own = (lax.axis_index(axis) // bit) % 2
    kept = lax.dynamic_slice_in_dim(values, own, 1, axis=dim)
    sent = lax.dynamic_slice_in_dim(values, 1 - own, 1, axis=dim)
    return add_half(kept, swap(sent, axis, size, bit))


def row_bits(row_size, place):
    bits = [1 << k for k in reversed(range(row_size.bit_length() - 1))]
    return bits, bits if place % 2 == 0 else bits[::-1]


def row_first(values, row_size, col_size, parts=2):
    chips, rows, width = values.shape
    bits, order = row_bits(row_size, 0)
    shaped = values.reshape((2,) * len(bits) + (col_size // 2, rows, width))
    part = width // parts
    pieces = []
    for place in range(parts):
        bits, order = row_bits(row_size, place)
        piece = shaped[..., part * place : part * (place + 1)]
        pieces.append(halve(piece, bits.index(order[0]), "row", row_size, order[0]))
    return pieces


def row_rest(pieces, row_size):
    done = []
    for place, piece in enumerate(pieces):
        bits, order = row_bits(row_size, place)
        for bit in order[1:]:
            piece = halve(piece, bits.index(bit), "row", row_size, bit)
        done.append(piece.reshape(piece.shape[-3:]))
    return jnp.concatenate(done, axis=-1)


def line_stage(whole, col_size):
    line = col_size // 2
    at = lax.axis_index("col") // 2
    total = lax.dynamic_index_in_dim(whole, at, 0, keepdims=False).astype(jnp.float32)
    for step in range(1, line):
        block = lax.dynamic_index_in_dim(whole, at ^ step, 0, keepdims=False)
        total = total + swap(block, "col", col_size, 2 * step).astype(jnp.float32)
    return total


def share_cores(values, col_size):
    core = lax.axis_index("col") % 2
    rows = values.shape[0] // 2
    kept = lax.dynamic_slice_in_dim(values, core * rows, rows)
    got = swap(lax.dynamic_slice_in_dim(values, (1 - core) * rows, rows), "col", col_size, 1)
    first = core == 0
    return jnp.where(first, kept, got), jnp.where(first, got, kept)


def core_half(values, core):
    half = values.shape[-1] // 2
    return lax.dynamic_slice_in_dim(values, core * half, half, axis=-1)


def with_partner(values, col_size):
    got = swap(values, "col", col_size, 1)
    return jnp.concatenate([values, got], axis=0)


def halves_with_partner(values, col_size):
    core = lax.axis_index("col") % 2
    got = swap(core_half(values, 1 - core), "col", col_size, 1)
    return jnp.concatenate([core_half(values, core), got], axis=0)


def per_device(
    tokens,
    cotangent,
    segment_numbers,
    positions,
    attention_norm_gain,
    query_matrix,
    key_value_matrix,
    output_matrix,
    output_adapter_first,
    output_adapter_second,
    feedforward_norm_gain,
    gate_matrix,
    up_matrix,
    down_matrix,
    down_adapter_first,
    down_adapter_second,
):
    row_size = lax.axis_size("row")
    col_size = lax.axis_size("col")
    devices = row_size * col_size
    row_at = lax.axis_index("row")
    tok_dev, width = tokens.shape
    group_len = segment_numbers.shape[0]
    row_total = tok_dev * NH
    query_width = query_matrix.shape[1]
    adapter_rows = output_adapter_second.shape[0]
    gain_len = attention_norm_gain.shape[0]
    start_row = lax.axis_index("col") * tok_dev
    scale = HD ** (-0.5)
    order = [partner(row_at, step) for step in range(row_size)]

    in_gathered = lax.all_gather(
        jnp.concatenate(
            [
                convert_half(query_matrix),
                convert_half(key_value_matrix),
                convert_half(
                    jnp.pad(
                        jnp.stack([attention_norm_gain, feedforward_norm_gain], axis=1),
                        ((0, 0), (0, 126)),
                    )
                ),
            ],
            axis=1,
        ),
        ("row", "col"),
        axis=0,
        tiled=True,
    )
    shard = jnp.concatenate(
        [
            convert_half(gate_matrix),
            convert_half(up_matrix),
            convert_half(down_matrix),
            convert_half(down_adapter_first),
        ],
        axis=0,
    )
    own_seg = lax.dynamic_slice_in_dim(segment_numbers, start_row, tok_dev)
    own_pos = lax.dynamic_slice_in_dim(positions, start_row, tok_dev)
    cosine, sine_part = rope_tables(own_pos)
    out_packed = jnp.concatenate(
        [
            convert_half(output_matrix),
            convert_half(output_adapter_first),
            convert_half(output_adapter_second).reshape(gain_len, -1),
            convert_half(down_adapter_second).reshape(gain_len, -1),
        ],
        axis=1,
    )
    in_gathered, cosine, sine_part = tie(in_gathered, cosine, sine_part)
    model_rows = gate_matrix.shape[0]
    by_pairs = row_size == 4 and col_size == 8
    cot_grad = cotangent.astype(jnp.float32)
    cot_mixed = reorder(cotangent, order)
    if by_pairs:
        half = shard.shape[0] // 2
        upper, lower = shard[:half], shard[half:]
        upper_y = swap(upper, "row", 4, 2)
        lower_x = swap(lower, "row", 4, 1)
        cot_two = swap(cot_mixed, "col", 8, 2)
        cot_four = swap(cot_mixed, "col", 8, 4)
        in_gathered, upper_y, lower_x, cot_two, cot_four, upper, lower, cot_mixed = tie(
            in_gathered, upper_y, lower_x, cot_two, cot_four, upper, lower, cot_mixed
        )
        upper_x = swap(upper, "row", 4, 1)
        lower_y = swap(lower, "row", 4, 2)
    in_width = in_gathered.shape[1] - 128
    in_weight = in_gathered[:, :in_width]
    gains = in_gathered[:, in_width:].astype(jnp.float32)
    gain_attn = gains[:, 0]
    gain_mlp = gains[:, 1]
    inputs = tokens.astype(jnp.float32)
    normed = convert_half(rms_scale(inputs, gain_attn))
    in_pre = matrix_product(normed, in_weight)
    query_pre = in_pre[:, :query_width]
    keyval_pre = in_pre[:, query_width:]
    query_rows = convert_half(
        rotate(query_pre.reshape(tok_dev, NH, HD), cosine[:, None, :], sine_part[:, None, :])
        * scale
    ).reshape(row_total, HD)
    keyval_own = jnp.concatenate(
        [
            convert_half(rotate(keyval_pre[:, :HD], cosine, sine_part)),
            convert_half(keyval_pre[:, HD:]),
        ],
        axis=1,
    )
    if by_pairs:
        places = [lax.axis_index("col") ^ (2 * step) for step in range(4)]
        places = places + [place ^ 1 for place in places]

        def gathered(mine, other):
            parts = [
                side[tok_dev * step : tok_dev * (step + 1)]
                for side in (mine, other)
                for step in range(4)
            ]
            return place_blocks(parts, places, 8)

    keyval_rows = lax.all_gather(keyval_own, "col", axis=0, tiled=True)
    keyval_rows, out_packed = tie(keyval_rows, out_packed)
    out_gathered = lax.all_gather(out_packed, ("row", "col"), axis=0, tiled=True)
    key_rows = keyval_rows[:, :HD]
    value_rows = keyval_rows[:, HD:]
    row_index = start_row + jnp.arange(row_total, dtype=jnp.int32) // NH
    row_seg = jnp.repeat(own_seg, NH)
    key_index = jnp.arange(group_len, dtype=jnp.int32)
    allowed = (key_index[None, :] <= row_index[:, None]) & (
        (segment_numbers[None, :] == 0) | (segment_numbers[None, :] == row_seg[:, None])
    )
    scores = jnp.where(allowed, product(query_rows, key_rows, contract_last), masked_score)
    top_value = jnp.max(scores, axis=1)
    total_value = jnp.sum(jnp.exp(scores - top_value[:, None]), axis=1)
    log_norm = top_value + jnp.log(total_value)
    if by_pairs:
        log_norm, upper_y, lower_x, upper_x, lower_y, cot_mixed = tie(
            log_norm, upper_y, lower_x, upper_x, lower_y, cot_mixed
        )
        far_upper = swap(upper_y, "row", 4, 1)
        far_lower = swap(lower_x, "row", 4, 2)
        cot_six = swap(cot_mixed, "col", 8, 6)
    probs = convert_half(jnp.exp(scores - log_norm[:, None]))
    mixed_rows = matrix_product(probs, value_rows)
    head_context = convert_half(mixed_rows.reshape(tok_dev, NH * HD))
    rank_width = output_adapter_first.shape[1]
    out_width = width + rank_width
    upper_width = adapter_rows * width // gain_len
    out_weight = out_gathered[:, :out_width]
    out_upper = out_gathered[:, out_width : out_width + upper_width].reshape(-1, width)
    down_upper = out_gathered[:, out_width + upper_width :].reshape(-1, width)
    out_pre = matrix_product(head_context, out_weight)
    output_rank_rows = convert_half(out_pre[:, width:])
    layer_state = inputs + out_pre[:, :width] + matrix_product(output_rank_rows, out_upper)
    normed_mlp = convert_half(rms_scale(layer_state, gain_mlp))
    normed_mlp = reorder(normed_mlp, order)
    if by_pairs:
        normed_mlp, far_upper, far_lower, cot_six = tie(normed_mlp, far_upper, far_lower, cot_six)
        cot_mine = jnp.concatenate([cot_mixed, cot_two, cot_four, cot_six], axis=0)
        cot_rows = gathered(cot_mine, swap(cot_mine, "col", 8, 1))
        pieces = [[shard], [upper_x, lower_x], [upper_y, lower_y], [far_upper, far_lower]]
    else:
        pieces = [[shard]] + [
            [to_partner(shard, "row", step, row_size)] for step in range(1, row_size)
        ]
        cot_rows = lax.all_gather(cot_mixed, "col", axis=0, tiled=True)
    gate_weight = rows_of(pieces, 0, model_rows)
    up_weight = rows_of(pieces, model_rows, 2 * model_rows)
    down_weight = jnp.concatenate(
        [
            rows_of(pieces, 2 * model_rows, 3 * model_rows),
            rows_of(pieces, 3 * model_rows, 3 * model_rows + down_adapter_first.shape[0]),
        ],
        axis=0,
    )
    ffn_in = lax.all_gather(normed_mlp, "col", axis=0, tiled=True)
    normed_both = with_partner(normed, col_size)
    context_both = with_partner(head_context, col_size)
    rank_both = with_partner(output_rank_rows, col_size)
    cot_both = halves_with_partner(cotangent, col_size)
    rank_part = rank_width // row_size
    upper_mixed = jnp.concatenate(
        [
            lax.dynamic_slice_in_dim(reorder(down_upper, order), place * rank_part, rank_part)
            for place in order
        ],
        axis=0,
    )
    rank_rows = convert_half(product(cot_rows, upper_mixed, contract_last))
    cot_rows = jnp.concatenate([cot_rows, rank_rows], axis=1)
    hidden_grad = matrix_product(cot_rows, down_weight)
    ffn_in, hidden_grad, gate_weight, up_weight, normed_both, context_both, rank_both, cot_both = (
        tie(
            ffn_in,
            hidden_grad,
            gate_weight,
            up_weight,
            normed_both,
            context_both,
            rank_both,
            cot_both,
        )
    )
    gate_values = matrix_product(ffn_in, gate_weight)
    up_values = matrix_product(ffn_in, up_weight)
    hidden_activated = convert_half(jax.nn.gelu(gate_values, approximate=True) * up_values)
    gelu_out, gelu_pull = jax.vjp(partial(jax.nn.gelu, approximate=True), gate_values)
    gate_grad = convert_half(gelu_pull(hidden_grad * up_values)[0])
    up_grad = convert_half(hidden_grad * gelu_out)

    def blocks_of(values):
        size = values.shape[0] // row_size
        return [values[size * step : size * (step + 1)] for step in range(row_size)]

    grad_down = convert_half(product(cot_rows, hidden_activated, contract_first))
    grad_down, gate_grad, up_grad = tie(grad_down, gate_grad, up_grad)
    down_blocks = [
        jnp.concatenate([one, two], axis=0)
        for one, two in zip(blocks_of(grad_down[:width]), blocks_of(grad_down[width:]))
    ]
    half_width = width // 2

    def normed_part(start, left_gate, left_up):
        stop = start + half_width
        return convert_half(
            product(left_gate, gate_weight[start:stop], contract_last)
            + product(left_up, up_weight[start:stop], contract_last)
        )

    def col_sum(values):
        return lax.psum_scatter(values, "col", scatter_dimension=0, tiled=True)

    def down_product(start, stop):
        return convert_half(product(hidden_activated, down_weight[start:stop], contract_last))

    if row_size == 4:
        own_down, far, free, last = split_blocks(down_blocks)
        far = send_pair(far)
        grad_gate = convert_half(product(ffn_in, gate_grad, contract_first))
        *far, grad_gate, up_grad, free_x, free_y = tie(*far, grad_gate, up_grad, *free)
        last = add_pair(last, far)
        down_free = send_pair((free_x, free_y))
        own_gate, gate_far, gate_free, gate_last = split_blocks(blocks_of(grad_gate))
        grad_up = convert_half(product(ffn_in, up_grad, contract_first))
        *down_free, grad_up, gate_grad, last_x, last_y, far_x, far_y = tie(
            *down_free, grad_up, gate_grad, *last, *gate_far
        )
        down_last = send_pair((last_x, last_y))
        far = send_pair((far_x, far_y))
        own_up, up_far, up_free, up_last = split_blocks(blocks_of(grad_up))
        first_part = normed_part(0, gate_grad, up_grad)
        *down_last, far_x, far_y, first_part, gate_grad, free_x, free_y, next_x, next_y = tie(
            *down_last, *far, first_part, gate_grad, *gate_free, *up_far
        )
        first_sum = col_sum(first_part)
        gate_last = add_pair(gate_last, (far_x, far_y))
        gate_free = send_pair((free_x, free_y))
        up_far = send_pair((next_x, next_y))
        second_part = normed_part(half_width, gate_grad, up_grad)
        *gate_free, far_x, far_y, second_part, last_x, last_y, free_x, free_y, hidden_activated = tie(
            *gate_free, *up_far, second_part, *gate_last, *up_free, hidden_activated
        )
        second_sum = col_sum(second_part)
        up_last = add_pair(up_last, (far_x, far_y))
        gate_last = send_pair((last_x, last_y))
        up_free = send_pair((free_x, free_y))
        rank_partial = down_product(width, width + rank_width)
        down_partial = down_product(0, width)
        *gate_last, free_x, free_y, second_sum, down_partial, last_x, last_y = tie(
            *gate_last, *up_free, second_sum, down_partial, *up_last
        )
        up_free = (free_x, free_y)
        up_last = send_pair((last_x, last_y))
    else:
        down_partial = down_product(0, width)
        first_sum = col_sum(normed_part(0, gate_grad, up_grad))
        second_sum = col_sum(normed_part(half_width, gate_grad, up_grad))
        rank_partial = down_product(width, width + rank_width)
        grad_gate = convert_half(product(ffn_in, gate_grad, contract_first))
        grad_up = convert_half(product(ffn_in, up_grad, contract_first))
        down_total = row_sum(down_blocks, row_size)
        gate_sum = row_sum(blocks_of(grad_gate), row_size)
        up_sum = row_sum(blocks_of(grad_up), row_size)
    rank_sums = col_sum(rank_partial)
    normed_grad = jnp.concatenate([first_sum, second_sum], axis=1)

    normed_grad = reorder(normed_grad, order).astype(jnp.float32)
    state_out, norm_pull = jax.vjp(rms_scale, layer_state, gain_mlp)
    state_part, grad_gain_mlp = norm_pull(normed_grad)
    state_grad = cot_grad + state_part
    attn_grad = convert_half(state_grad)
    rank_out_grad = convert_half(product(attn_grad, out_upper, contract_last))
    out_grad = jnp.concatenate([attn_grad, rank_out_grad], axis=1)
    context_grad = product(out_grad, out_weight, contract_last)
    grad_rows = convert_half(context_grad).reshape(row_total, HD)
    if row_size == 4:
        *up_last, grad_rows = tie(*up_last, grad_rows)
    delta = jnp.sum(grad_rows.astype(jnp.float32) * mixed_rows, axis=1)
    weight_grad = product(grad_rows, value_rows, contract_last)
    score_grad = convert_half(probs.astype(jnp.float32) * (weight_grad - delta[:, None]))
    query_acc = matrix_product(score_grad, key_rows)
    query_grad = convert_half(
        unrotate(
            query_acc.reshape(tok_dev, NH, HD) * scale, cosine[:, None, :], sine_part[:, None, :]
        ).reshape(tok_dev, NH * HD)
    )
    query_grad, score_grad = tie(query_grad, score_grad)
    key_acc = product(score_grad, query_rows, contract_first)
    value_acc = product(probs, grad_rows, contract_first)
    keyval_part = jnp.concatenate([convert_half(key_acc), convert_half(value_acc)], axis=1)
    keyval_part, rank_sums = tie(keyval_part, rank_sums)
    keyval_sum = col_sum(keyval_part)
    core = lax.axis_index("col") % 2
    query_right = halves_with_partner(query_grad, col_size)
    grad_query = convert_half(product(normed_both, query_right, contract_first))
    chips = devices // 2

    def shared(values):
        return convert_half(values).reshape(chips, 2 * gain_len, -1)

    out_right = halves_with_partner(out_grad[:, :width], col_size)
    rank_right = halves_with_partner(out_grad[:, width:], col_size)
    grad_out = product(
        context_both, jnp.concatenate([out_right, rank_right], axis=1), contract_first
    )
    grad_out_upper = product(rank_both, out_right, contract_first)
    out_group = jnp.concatenate([shared(grad_out), shared(grad_out_upper)], axis=2)
    query_group = shared(grad_query)
    query_parts = row_first(query_group, row_size, col_size)
    out_parts = row_first(out_group, row_size, col_size)
    keyval_sum, down_partial, *parts = tie(keyval_sum, down_partial, *query_parts, *out_parts)
    query_parts, out_parts = parts[:2], parts[2:]
    if row_size == 4:
        down_total = finish_sum(own_down, down_free, down_last)
        gate_sum = finish_sum(own_gate, gate_free, gate_last)
        up_sum = finish_sum(own_up, up_free, up_last)
    down_sum, rank_sum = down_total[:model_rows], down_total[model_rows:]
    query_lines = row_rest(query_parts, row_size)
    out_lines = row_rest(out_parts, row_size)
    down_rank_rows = reorder(rank_sums, order)
    summed = col_sum(down_partial)
    layer_out = convert_half(
        layer_state
        + reorder(summed, order).astype(jnp.float32)
        + matrix_product(down_rank_rows, down_upper)
    )
    keyval_sum = keyval_sum.astype(jnp.float32)
    keyval_grad = jnp.concatenate(
        [convert_half(unrotate(keyval_sum[:, :HD], cosine, sine_part)), convert_half(keyval_sum[:, HD:])],
        axis=1,
    )
    in_grad = jnp.concatenate([query_grad, keyval_grad], axis=1)
    normed_back = product(in_grad, in_weight, contract_last)
    normed_out, first_pull = jax.vjp(rms_scale, inputs, gain_attn)
    input_part, grad_gain_attn = first_pull(normed_back)
    input_grad = convert_half(state_grad + input_part)

    grad_keyval = product(
        normed_both, halves_with_partner(keyval_grad, col_size), contract_first
    )
    grad_down_upper = product(
        with_partner(down_rank_rows, col_size), cot_both, contract_first
    )
    gains = jnp.stack([grad_gain_attn, grad_gain_mlp])
    gain = lax.dynamic_index_in_dim(gains, core, 0, keepdims=False) + swap(
        lax.dynamic_index_in_dim(gains, 1 - core, 0, keepdims=False), "col", col_size, 1
    )
    keyval_group = jnp.concatenate(
        [
            shared(grad_keyval),
            shared(grad_down_upper),
            jnp.pad(shared(gain), ((0, 0), (0, 0), (0, 127))),
        ],
        axis=2,
    )
    lines = jnp.concatenate([query_lines, out_lines], axis=2)
    lines, keyval_group = tie(lines, keyval_group)
    first, second = share_cores(line_stage(lines, col_size), col_size)
    keyval_first, keyval_second = share_cores(
        line_stage(row_rest(row_first(keyval_group, row_size, col_size, parts=1), row_size), col_size), col_size
    )
    half_query = query_width // 2
    query_first, query_second = first[:, :half_query], second[:, :half_query]
    out_first, out_second = first[:, half_query:], second[:, half_query:]

    def joined(first, second, start, size):
        return jnp.concatenate([first[:, start : start + size], second[:, start : start + size]], axis=1)

    def joined_rows(first, second, start, size):
        return jnp.concatenate(
            [
                half[:, start : start + size].reshape(adapter_rows, -1)
                for half in (first, second)
            ],
            axis=1,
        )

    half_rank = rank_width // 2
    half_keyval = key_value_matrix.shape[1] // 2
    half_upper = upper_width // 2
    return (
        layer_out,
        input_grad,
        keyval_first[:, half_keyval + half_upper],
        joined(query_first, query_second, 0, query_width // 2),
        joined(keyval_first, keyval_second, 0, half_keyval),
        joined(out_first, out_second, 0, half_width),
        joined(out_first, out_second, half_width, half_rank),
        joined_rows(out_first, out_second, half_width + half_rank, half_upper),
        keyval_second[:, half_keyval + half_upper],
        gate_sum,
        up_sum,
        down_sum,
        rank_sum,
        joined_rows(keyval_first, keyval_second, half_keyval, half_upper),
    )


def solution(mesh):
    return jax.shard_map(
        per_device,
        mesh=mesh,
        in_specs=(
            P(("row", "col"), None),
            P(("row", "col"), None),
            P("row"),
            P("row"),
            P(("row", "col")),
            P(("row", "col"), None),
            P(("row", "col"), None),
            P(("row", "col"), None),
            P(("row", "col"), None),
            P(("row", "col"), None),
            P(("row", "col")),
            P("row", "col"),
            P("row", "col"),
            P("row", "col"),
            P("row", "col"),
            P(("row", "col"), None),
        ),
        out_specs=(
            P(("row", "col"), None),
            P(("row", "col"), None),
            P(("row", "col")),
            P(("row", "col"), None),
            P(("row", "col"), None),
            P(("row", "col"), None),
            P(("row", "col"), None),
            P(("row", "col"), None),
            P(("row", "col")),
            P("row", "col"),
            P("row", "col"),
            P("row", "col"),
            P("row", "col"),
            P(("row", "col"), None),
        ),
        check_vma=False,
    )
```

```python
from functools import partial

import jax
import jax.numpy as jnp
from jax import lax
from jax.sharding import PartitionSpec as P

MODEL_WIDTH = 2048
NH = 8
HD = 256


masked_score = -1e30
epsilon = 1e-06
contract_last = (((1,), (1,)), ((), ()))
contract_first = (((0,), (0,)), ((), ()))


def convert_half(values):
    return values.astype(jnp.bfloat16)


def product(left_side, right_side, dims):
    return lax.dot_general(left_side, right_side, dims, preferred_element_type=jnp.float32)


def matrix_product(left_side, right_side):
    return jnp.dot(left_side, right_side, preferred_element_type=jnp.float32)


def rms_scale(values, gain):
    return values * lax.rsqrt(jnp.mean(values * values, axis=-1, keepdims=True) + epsilon) * gain


def rope_tables(positions):
    half_width = HD // 2
    inverse = 10000.0 ** (-jnp.arange(half_width, dtype=jnp.float32) * 2.0 / HD)
    angles = positions.astype(jnp.float32)[:, None] * inverse[None, :]
    return (jnp.cos(angles), jnp.sin(angles))


def rotate(tensor, cosine, sine_part):
    half_width = tensor.shape[-1] // 2
    leading = tensor[..., :half_width]
    trailing = tensor[..., half_width:]
    return jnp.concatenate(
        [leading * cosine - trailing * sine_part, trailing * cosine + leading * sine_part], axis=-1
    )


def unrotate(tensor, cosine, sine_part):
    half_width = tensor.shape[-1] // 2
    leading = tensor[..., :half_width]
    trailing = tensor[..., half_width:]
    return jnp.concatenate(
        [leading * cosine + trailing * sine_part, trailing * cosine - leading * sine_part], axis=-1
    )


def swap(values, axis, size, bit):
    return lax.ppermute(values, axis, [(i, i ^ bit) for i in range(size)])


def partner(own, step):
    return own ^ step


def to_partner(values, axis, step, size):
    return lax.ppermute(values, axis, [(i, partner(i, step)) for i in range(size)])


def reorder(values, order):
    width = values.shape[-1] // len(order)
    return jnp.concatenate(
        [lax.dynamic_slice_in_dim(values, place * width, width, axis=-1) for place in order], axis=-1
    )


def tie(*values):
    return lax.optimization_barrier(values)


def place_blocks(blocks, places, count):
    rows = blocks[0].shape[0]
    whole = jnp.zeros((rows * count, blocks[0].shape[1]), blocks[0].dtype)
    for block, place in zip(blocks, places):
        whole = lax.dynamic_update_slice_in_dim(whole, block, place * rows, axis=0)
    return whole


def rows_of(pieces, start, stop):
    found = []
    for parts in pieces:
        offset = 0
        for part in parts:
            first, last = max(start - offset, 0), min(stop - offset, part.shape[0])
            if first < last:
                found.append(part[first:last])
            offset += part.shape[0]
    return jnp.concatenate(found, axis=0)


def split_blocks(blocks):
    own, near_x, near_y, far = blocks
    half = own.shape[0] // 2
    return (
        own,
        (far[:half], far[half:]),
        (near_x[:half], near_y[half:]),
        (near_x[half:], near_y[:half]),
    )


def send_pair(pair):
    return swap(pair[0], "row", 4, 1), swap(pair[1], "row", 4, 2)


def add_pair(pair, got):
    return add_half(pair[0], got[1]), add_half(pair[1], got[0])


def finish_sum(own, free, last):
    half = own.shape[0] // 2
    upper = add_full(own[:half], free[0], last[1])
    lower = add_full(own[half:], last[0], free[1])
    return jnp.concatenate([upper, lower], axis=0)


def row_scatter(values, order):
    size = values.shape[0] // len(order)
    natural = jnp.concatenate(
        [lax.dynamic_slice_in_dim(values, place * size, size) for place in order], axis=0
    )
    return lax.psum_scatter(natural, "row", scatter_dimension=0, tiled=True)


def row_sum(blocks, size):
    total = blocks[0].astype(jnp.float32)
    for step in range(1, size):
        total = total + to_partner(blocks[step], "row", step, size).astype(jnp.float32)
    return total


def add_full(first, second, third):
    return first.astype(jnp.float32) + second.astype(jnp.float32) + third.astype(jnp.float32)


def add_half(first, second):
    return convert_half(first.astype(jnp.float32) + second.astype(jnp.float32))


def halve(values, dim, axis, size, bit):
    own = (lax.axis_index(axis) // bit) % 2
    kept = lax.dynamic_slice_in_dim(values, own, 1, axis=dim)
    sent = lax.dynamic_slice_in_dim(values, 1 - own, 1, axis=dim)
    return add_half(kept, swap(sent, axis, size, bit))


def row_bits(row_size, place):
    bits = [1 << k for k in reversed(range(row_size.bit_length() - 1))]
    return bits, bits if place % 2 == 0 else bits[::-1]


def row_first(values, row_size, col_size, parts=2):
    chips, rows, width = values.shape
    bits, order = row_bits(row_size, 0)
    shaped = values.reshape((2,) * len(bits) + (col_size // 2, rows, width))
    part = width // parts
    pieces = []
    for place in range(parts):
        bits, order = row_bits(row_size, place)
        piece = shaped[..., part * place : part * (place + 1)]
        pieces.append(halve(piece, bits.index(order[0]), "row", row_size, order[0]))
    return pieces


def row_rest(pieces, row_size):
    done = []
    for place, piece in enumerate(pieces):
        bits, order = row_bits(row_size, place)
        for bit in order[1:]:
            piece = halve(piece, bits.index(bit), "row", row_size, bit)
        done.append(piece.reshape(piece.shape[-3:]))
    return jnp.concatenate(done, axis=-1)


def line_stage(whole, col_size):
    line = col_size // 2
    at = lax.axis_index("col") // 2
    total = lax.dynamic_index_in_dim(whole, at, 0, keepdims=False).astype(jnp.float32)
    for step in range(1, line):
        block = lax.dynamic_index_in_dim(whole, at ^ step, 0, keepdims=False)
        total = total + swap(block, "col", col_size, 2 * step).astype(jnp.float32)
    return total


def share_cores(values, col_size):
    core = lax.axis_index("col") % 2
    rows = values.shape[0] // 2
    kept = lax.dynamic_slice_in_dim(values, core * rows, rows)
    got = swap(lax.dynamic_slice_in_dim(values, (1 - core) * rows, rows), "col", col_size, 1)
    first = core == 0
    return jnp.where(first, kept, got), jnp.where(first, got, kept)


def core_half(values, core):
    half = values.shape[-1] // 2
    return lax.dynamic_slice_in_dim(values, core * half, half, axis=-1)


def with_partner(values, col_size):
    got = swap(values, "col", col_size, 1)
    return jnp.concatenate([values, got], axis=0)


def halves_with_partner(values, col_size):
    core = lax.axis_index("col") % 2
    got = swap(core_half(values, 1 - core), "col", col_size, 1)
    return jnp.concatenate([core_half(values, core), got], axis=0)


def per_device(
    tokens,
    cotangent,
    segment_numbers,
    positions,
    attention_norm_gain,
    query_matrix,
    key_value_matrix,
    output_matrix,
    output_adapter_first,
    output_adapter_second,
    feedforward_norm_gain,
    gate_matrix,
    up_matrix,
    down_matrix,
    down_adapter_first,
    down_adapter_second,
):
    row_size = lax.axis_size("row")
    col_size = lax.axis_size("col")
    devices = row_size * col_size
    row_at = lax.axis_index("row")
    tok_dev, width = tokens.shape
    group_len = segment_numbers.shape[0]
    row_total = tok_dev * NH
    query_width = query_matrix.shape[1]
    adapter_rows = output_adapter_second.shape[0]
    gain_len = attention_norm_gain.shape[0]
    start_row = lax.axis_index("col") * tok_dev
    scale = HD ** (-0.5)
    order = [partner(row_at, step) for step in range(row_size)]

    in_gathered = lax.all_gather(
        jnp.concatenate(
            [
                convert_half(query_matrix),
                convert_half(key_value_matrix),
                convert_half(
                    jnp.pad(
                        jnp.stack([attention_norm_gain, feedforward_norm_gain], axis=1),
                        ((0, 0), (0, 126)),
                    )
                ),
            ],
            axis=1,
        ),
        ("row", "col"),
        axis=0,
        tiled=True,
    )
    shard = jnp.concatenate(
        [
            convert_half(gate_matrix),
            convert_half(up_matrix),
            convert_half(down_matrix),
            convert_half(down_adapter_first),
        ],
        axis=0,
    )
    own_seg = lax.dynamic_slice_in_dim(segment_numbers, start_row, tok_dev)
    own_pos = lax.dynamic_slice_in_dim(positions, start_row, tok_dev)
    cosine, sine_part = rope_tables(own_pos)
    out_packed = jnp.concatenate(
        [
            convert_half(output_matrix),
            convert_half(output_adapter_first),
            convert_half(output_adapter_second).reshape(gain_len, -1),
            convert_half(down_adapter_second).reshape(gain_len, -1),
        ],
        axis=1,
    )
    in_gathered, cosine, sine_part = tie(in_gathered, cosine, sine_part)
    model_rows = gate_matrix.shape[0]
    by_pairs = row_size == 4 and col_size == 8
    cot_grad = cotangent.astype(jnp.float32)
    cot_mixed = reorder(cotangent, order)
    if by_pairs:
        half = shard.shape[0] // 2
        upper, lower = shard[:half], shard[half:]
        upper_y = swap(upper, "row", 4, 2)
        lower_x = swap(lower, "row", 4, 1)
        cot_two = swap(cot_mixed, "col", 8, 2)
        cot_four = swap(cot_mixed, "col", 8, 4)
        in_gathered, upper_y, lower_x, cot_two, cot_four, upper, lower, cot_mixed = tie(
            in_gathered, upper_y, lower_x, cot_two, cot_four, upper, lower, cot_mixed
        )
        upper_x = swap(upper, "row", 4, 1)
        lower_y = swap(lower, "row", 4, 2)
    in_width = in_gathered.shape[1] - 128
    in_weight = in_gathered[:, :in_width]
    gains = in_gathered[:, in_width:].astype(jnp.float32)
    gain_attn = gains[:, 0]
    gain_mlp = gains[:, 1]
    inputs = tokens.astype(jnp.float32)
    normed = convert_half(rms_scale(inputs, gain_attn))
    in_pre = matrix_product(normed, in_weight)
    query_pre = in_pre[:, :query_width]
    keyval_pre = in_pre[:, query_width:]
    query_rows = convert_half(
        rotate(query_pre.reshape(tok_dev, NH, HD), cosine[:, None, :], sine_part[:, None, :])
        * scale
    ).reshape(row_total, HD)
    keyval_own = jnp.concatenate(
        [
            convert_half(rotate(keyval_pre[:, :HD], cosine, sine_part)),
            convert_half(keyval_pre[:, HD:]),
        ],
        axis=1,
    )
    if by_pairs:
        places = [lax.axis_index("col") ^ (2 * step) for step in range(4)]
        places = places + [place ^ 1 for place in places]

        def gathered(mine, other):
            parts = [
                side[tok_dev * step : tok_dev * (step + 1)]
                for side in (mine, other)
                for step in range(4)
            ]
            return place_blocks(parts, places, 8)

    keyval_rows = lax.all_gather(keyval_own, "col", axis=0, tiled=True)
    keyval_rows, out_packed = tie(keyval_rows, out_packed)
    out_gathered = lax.all_gather(out_packed, ("row", "col"), axis=0, tiled=True)
    if by_pairs:
        keyval_rows, upper_y, lower_x, upper_x, lower_y, cot_mixed = tie(
            keyval_rows, upper_y, lower_x, upper_x, lower_y, cot_mixed
        )
        far_upper = swap(upper_y, "row", 4, 1)
        far_lower = swap(lower_x, "row", 4, 2)
        cot_six = swap(cot_mixed, "col", 8, 6)
    key_rows = keyval_rows[:, :HD]
    value_rows = keyval_rows[:, HD:]
    row_index = start_row + jnp.arange(row_total, dtype=jnp.int32) // NH
    row_seg = jnp.repeat(own_seg, NH)
    key_index = jnp.arange(group_len, dtype=jnp.int32)
    allowed = (key_index[None, :] <= row_index[:, None]) & (
        (segment_numbers[None, :] == 0) | (segment_numbers[None, :] == row_seg[:, None])
    )
    scores = jnp.where(allowed, product(query_rows, key_rows, contract_last), masked_score)
    top_value = jnp.max(scores, axis=1)
    total_value = jnp.sum(jnp.exp(scores - top_value[:, None]), axis=1)
    log_norm = top_value + jnp.log(total_value)
    probs = convert_half(jnp.exp(scores - log_norm[:, None]))
    mixed_rows = matrix_product(probs, value_rows)
    head_context = convert_half(mixed_rows.reshape(tok_dev, NH * HD))
    rank_width = output_adapter_first.shape[1]
    out_width = width + rank_width
    upper_width = adapter_rows * width // gain_len
    out_weight = out_gathered[:, :out_width]
    out_upper = out_gathered[:, out_width : out_width + upper_width].reshape(-1, width)
    down_upper = out_gathered[:, out_width + upper_width :].reshape(-1, width)
    out_pre = matrix_product(head_context, out_weight)
    output_rank_rows = convert_half(out_pre[:, width:])
    layer_state = inputs + out_pre[:, :width] + matrix_product(output_rank_rows, out_upper)
    normed_mlp = convert_half(rms_scale(layer_state, gain_mlp))
    normed_mlp = reorder(normed_mlp, order)
    if by_pairs:
        normed_mlp, far_upper, far_lower, cot_six = tie(normed_mlp, far_upper, far_lower, cot_six)
        cot_mine = jnp.concatenate([cot_mixed, cot_two, cot_four, cot_six], axis=0)
        cot_rows = gathered(cot_mine, swap(cot_mine, "col", 8, 1))
        pieces = [[shard], [upper_x, lower_x], [upper_y, lower_y], [far_upper, far_lower]]
    else:
        pieces = [[shard]] + [
            [to_partner(shard, "row", step, row_size)] for step in range(1, row_size)
        ]
        cot_rows = lax.all_gather(cot_mixed, "col", axis=0, tiled=True)
    gate_weight = rows_of(pieces, 0, model_rows)
    up_weight = rows_of(pieces, model_rows, 2 * model_rows)
    down_weight = jnp.concatenate(
        [
            rows_of(pieces, 2 * model_rows, 3 * model_rows),
            rows_of(pieces, 3 * model_rows, 3 * model_rows + down_adapter_first.shape[0]),
        ],
        axis=0,
    )
    ffn_in = lax.all_gather(normed_mlp, "col", axis=0, tiled=True)
    normed_both = with_partner(normed, col_size)
    context_both = with_partner(head_context, col_size)
    rank_both = with_partner(output_rank_rows, col_size)
    cot_both = halves_with_partner(cotangent, col_size)
    rank_part = rank_width // row_size
    upper_mixed = jnp.concatenate(
        [
            lax.dynamic_slice_in_dim(reorder(down_upper, order), place * rank_part, rank_part)
            for place in order
        ],
        axis=0,
    )
    rank_rows = convert_half(product(cot_rows, upper_mixed, contract_last))
    cot_rows = jnp.concatenate([cot_rows, rank_rows], axis=1)
    hidden_grad = matrix_product(cot_rows, down_weight)
    ffn_in, hidden_grad, gate_weight, up_weight, normed_both, context_both, rank_both, cot_both = (
        tie(
            ffn_in,
            hidden_grad,
            gate_weight,
            up_weight,
            normed_both,
            context_both,
            rank_both,
            cot_both,
        )
    )
    gate_values = matrix_product(ffn_in, gate_weight)
    up_values = matrix_product(ffn_in, up_weight)
    hidden_activated = convert_half(jax.nn.gelu(gate_values, approximate=True) * up_values)
    gelu_out, gelu_pull = jax.vjp(partial(jax.nn.gelu, approximate=True), gate_values)
    gate_grad = convert_half(gelu_pull(hidden_grad * up_values)[0])
    up_grad = convert_half(hidden_grad * gelu_out)

    def blocks_of(values):
        size = values.shape[0] // row_size
        return [values[size * step : size * (step + 1)] for step in range(row_size)]

    grad_down = convert_half(product(cot_rows, hidden_activated, contract_first))
    grad_down, gate_grad, up_grad = tie(grad_down, gate_grad, up_grad)
    half_width = width // 2

    def normed_part(start, left_gate, left_up):
        stop = start + half_width
        return convert_half(
            product(left_gate, gate_weight[start:stop], contract_last)
            + product(left_up, up_weight[start:stop], contract_last)
        )

    def col_sum(values):
        return lax.psum_scatter(values, "col", scatter_dimension=0, tiled=True)

    def down_product(start, stop):
        return convert_half(product(hidden_activated, down_weight[start:stop], contract_last))

    if row_size == 4:
        down_total = row_scatter(
            jnp.concatenate(
                [
                    jnp.concatenate([one, two], axis=0)
                    for one, two in zip(blocks_of(grad_down[:width]), blocks_of(grad_down[width:]))
                ],
                axis=0,
            ),
            order,
        )
        rank_partial = down_product(width, width + rank_width)
        first_part = jnp.concatenate([normed_part(0, gate_grad, up_grad), rank_partial], axis=1)
        second_part = normed_part(half_width, gate_grad, up_grad)
        down_total, first_part, second_part, gate_grad, up_grad, hidden_activated = tie(
            down_total, first_part, second_part, gate_grad, up_grad, hidden_activated
        )
        first_sum = col_sum(first_part)
        second_sum = col_sum(second_part)
        first_sum, rank_sums = first_sum[:, :half_width], first_sum[:, half_width:]
        grad_gate = convert_half(product(ffn_in, gate_grad, contract_first))
        grad_gate, up_grad = tie(grad_gate, up_grad)
        own_gate, gate_far, gate_free, gate_last = split_blocks(blocks_of(grad_gate))
        far = send_pair(gate_far)
        grad_up = convert_half(product(ffn_in, up_grad, contract_first))
        *far, grad_up, hidden_activated, free_x, free_y = tie(
            *far, grad_up, hidden_activated, *gate_free
        )
        up_total = row_scatter(grad_up, order)
        gate_last = add_pair(gate_last, far)
        gate_free = send_pair((free_x, free_y))
        down_partial = down_product(0, width)
        *gate_free, second_sum, down_partial, last_x, last_y = tie(
            *gate_free, second_sum, down_partial, *gate_last
        )
        gate_last = send_pair((last_x, last_y))
    else:
        down_partial = down_product(0, width)
        first_sum = col_sum(normed_part(0, gate_grad, up_grad))
        second_sum = col_sum(normed_part(half_width, gate_grad, up_grad))
        rank_sums = col_sum(down_product(width, width + rank_width))
        grad_gate = convert_half(product(ffn_in, gate_grad, contract_first))
        grad_up = convert_half(product(ffn_in, up_grad, contract_first))
        down_total = row_scatter(
            jnp.concatenate(
                [
                    jnp.concatenate([one, two], axis=0)
                    for one, two in zip(blocks_of(grad_down[:width]), blocks_of(grad_down[width:]))
                ],
                axis=0,
            ),
            order,
        )
        gate_sum = row_sum(blocks_of(grad_gate), row_size)
        up_total = row_scatter(grad_up, order)
    normed_grad = jnp.concatenate([first_sum, second_sum], axis=1)

    normed_grad = reorder(normed_grad, order).astype(jnp.float32)
    state_out, norm_pull = jax.vjp(rms_scale, layer_state, gain_mlp)
    state_part, grad_gain_mlp = norm_pull(normed_grad)
    state_grad = cot_grad + state_part
    attn_grad = convert_half(state_grad)
    rank_out_grad = convert_half(product(attn_grad, out_upper, contract_last))
    out_grad = jnp.concatenate([attn_grad, rank_out_grad], axis=1)
    context_grad = product(out_grad, out_weight, contract_last)
    grad_rows = convert_half(context_grad).reshape(row_total, HD)
    if row_size == 4:
        *gate_last, grad_rows = tie(*gate_last, grad_rows)
    delta = jnp.sum(grad_rows.astype(jnp.float32) * mixed_rows, axis=1)
    weight_grad = product(grad_rows, value_rows, contract_last)
    score_grad = convert_half(probs.astype(jnp.float32) * (weight_grad - delta[:, None]))
    query_acc = matrix_product(score_grad, key_rows)
    query_grad = convert_half(
        unrotate(
            query_acc.reshape(tok_dev, NH, HD) * scale, cosine[:, None, :], sine_part[:, None, :]
        ).reshape(tok_dev, NH * HD)
    )
    query_grad, score_grad = tie(query_grad, score_grad)
    key_acc = product(score_grad, query_rows, contract_first)
    value_acc = product(probs, grad_rows, contract_first)
    keyval_part = jnp.concatenate([convert_half(key_acc), convert_half(value_acc)], axis=1)
    keyval_part, up_total = tie(keyval_part, up_total)
    keyval_sum = col_sum(keyval_part)
    core = lax.axis_index("col") % 2
    query_right = halves_with_partner(query_grad, col_size)
    grad_query = convert_half(product(normed_both, query_right, contract_first))
    chips = devices // 2

    def shared(values):
        return convert_half(values).reshape(chips, 2 * gain_len, -1)

    out_right = halves_with_partner(out_grad[:, :width], col_size)
    rank_right = halves_with_partner(out_grad[:, width:], col_size)
    grad_out = product(
        context_both, jnp.concatenate([out_right, rank_right], axis=1), contract_first
    )
    grad_out_upper = product(rank_both, out_right, contract_first)
    out_group = jnp.concatenate([shared(grad_out), shared(grad_out_upper)], axis=2)
    query_group = shared(grad_query)
    query_parts = row_first(query_group, row_size, col_size)
    out_parts = row_first(out_group, row_size, col_size)
    keyval_sum, down_partial, *parts = tie(keyval_sum, down_partial, *query_parts, *out_parts)
    query_parts, out_parts = parts[:2], parts[2:]
    query_lines = row_rest(query_parts, row_size)
    out_lines = row_rest(out_parts, row_size)
    lines = jnp.concatenate([query_lines, out_lines], axis=2)
    lines, keyval_sum = tie(lines, keyval_sum)
    down_rank_rows = reorder(rank_sums, order)
    summed = col_sum(down_partial)
    layer_out = convert_half(
        layer_state
        + reorder(summed, order).astype(jnp.float32)
        + matrix_product(down_rank_rows, down_upper)
    )
    keyval_sum = keyval_sum.astype(jnp.float32)
    keyval_grad = jnp.concatenate(
        [convert_half(unrotate(keyval_sum[:, :HD], cosine, sine_part)), convert_half(keyval_sum[:, HD:])],
        axis=1,
    )
    in_grad = jnp.concatenate([query_grad, keyval_grad], axis=1)
    normed_back = product(in_grad, in_weight, contract_last)
    normed_out, first_pull = jax.vjp(rms_scale, inputs, gain_attn)
    input_part, grad_gain_attn = first_pull(normed_back)
    input_grad = convert_half(state_grad + input_part)

    grad_keyval = product(
        normed_both, halves_with_partner(keyval_grad, col_size), contract_first
    )
    grad_down_upper = product(
        with_partner(down_rank_rows, col_size), cot_both, contract_first
    )
    gains = jnp.stack([grad_gain_attn, grad_gain_mlp])
    gain = lax.dynamic_index_in_dim(gains, core, 0, keepdims=False) + swap(
        lax.dynamic_index_in_dim(gains, 1 - core, 0, keepdims=False), "col", col_size, 1
    )
    keyval_group = jnp.concatenate(
        [
            shared(grad_keyval),
            shared(grad_down_upper),
            jnp.pad(shared(gain), ((0, 0), (0, 0), (0, 127))),
        ],
        axis=2,
    )
    if row_size == 4:
        lines, *sums = tie(lines, own_gate, *gate_free, *gate_last)
        gate_sum = finish_sum(sums[0], sums[1:3], sums[3:])
    down_total = down_total.astype(jnp.float32)
    down_sum, rank_sum = down_total[:model_rows], down_total[model_rows:]
    up_sum = up_total.astype(jnp.float32)
    first, second = share_cores(line_stage(lines, col_size), col_size)
    keyval_first, keyval_second = share_cores(
        line_stage(row_rest(row_first(keyval_group, row_size, col_size, parts=1), row_size), col_size), col_size
    )
    half_query = query_width // 2
    query_first, query_second = first[:, :half_query], second[:, :half_query]
    out_first, out_second = first[:, half_query:], second[:, half_query:]

    def joined(first, second, start, size):
        return jnp.concatenate([first[:, start : start + size], second[:, start : start + size]], axis=1)

    def joined_rows(first, second, start, size):
        return jnp.concatenate(
            [
                half[:, start : start + size].reshape(adapter_rows, -1)
                for half in (first, second)
            ],
            axis=1,
        )

    half_rank = rank_width // 2
    half_keyval = key_value_matrix.shape[1] // 2
    half_upper = upper_width // 2
    return (
        layer_out,
        input_grad,
        keyval_first[:, half_keyval + half_upper],
        joined(query_first, query_second, 0, query_width // 2),
        joined(keyval_first, keyval_second, 0, half_keyval),
        joined(out_first, out_second, 0, half_width),
        joined(out_first, out_second, half_width, half_rank),
        joined_rows(out_first, out_second, half_width + half_rank, half_upper),
        keyval_second[:, half_keyval + half_upper],
        gate_sum,
        up_sum,
        down_sum,
        rank_sum,
        joined_rows(keyval_first, keyval_second, half_keyval, half_upper),
    )


def solution(mesh):
    return jax.shard_map(
        per_device,
        mesh=mesh,
        in_specs=(
            P(("row", "col"), None),
            P(("row", "col"), None),
            P("row"),
            P("row"),
            P(("row", "col")),
            P(("row", "col"), None),
            P(("row", "col"), None),
            P(("row", "col"), None),
            P(("row", "col"), None),
            P(("row", "col"), None),
            P(("row", "col")),
            P("row", "col"),
            P("row", "col"),
            P("row", "col"),
            P("row", "col"),
            P(("row", "col"), None),
        ),
        out_specs=(
            P(("row", "col"), None),
            P(("row", "col"), None),
            P(("row", "col")),
            P(("row", "col"), None),
            P(("row", "col"), None),
            P(("row", "col"), None),
            P(("row", "col"), None),
            P(("row", "col"), None),
            P(("row", "col")),
            P("row", "col"),
            P("row", "col"),
            P("row", "col"),
            P("row", "col"),
            P(("row", "col"), None),
        ),
        check_vma=False,
    )
```

```python
from functools import partial

import jax
import jax.numpy as jnp
from jax import lax
from jax.sharding import PartitionSpec as P

MODEL_WIDTH = 2048
NH = 8
HD = 256


masked_score = -1e30
epsilon = 1e-06
contract_last = (((1,), (1,)), ((), ()))
contract_first = (((0,), (0,)), ((), ()))


def convert_half(values):
    return values.astype(jnp.bfloat16)


def product(left_side, right_side, dims):
    return lax.dot_general(left_side, right_side, dims, preferred_element_type=jnp.float32)


def matrix_product(left_side, right_side):
    return jnp.dot(left_side, right_side, preferred_element_type=jnp.float32)


def rms_scale(values, gain):
    return values * lax.rsqrt(jnp.mean(values * values, axis=-1, keepdims=True) + epsilon) * gain


def rope_tables(positions):
    half_width = HD // 2
    inverse = 10000.0 ** (-jnp.arange(half_width, dtype=jnp.float32) * 2.0 / HD)
    angles = positions.astype(jnp.float32)[:, None] * inverse[None, :]
    return (jnp.cos(angles), jnp.sin(angles))


def rotate(tensor, cosine, sine_part):
    half_width = tensor.shape[-1] // 2
    leading = tensor[..., :half_width]
    trailing = tensor[..., half_width:]
    return jnp.concatenate(
        [leading * cosine - trailing * sine_part, trailing * cosine + leading * sine_part], axis=-1
    )


def unrotate(tensor, cosine, sine_part):
    half_width = tensor.shape[-1] // 2
    leading = tensor[..., :half_width]
    trailing = tensor[..., half_width:]
    return jnp.concatenate(
        [leading * cosine + trailing * sine_part, trailing * cosine - leading * sine_part], axis=-1
    )


def swap(values, axis, size, bit):
    return lax.ppermute(values, axis, [(i, i ^ bit) for i in range(size)])


def partner(own, step):
    return own ^ step


def to_partner(values, axis, step, size):
    return lax.ppermute(values, axis, [(i, partner(i, step)) for i in range(size)])


def reorder(values, order):
    width = values.shape[-1] // len(order)
    return jnp.concatenate(
        [lax.dynamic_slice_in_dim(values, place * width, width, axis=-1) for place in order], axis=-1
    )


def tie(*values):
    return lax.optimization_barrier(values)


def place_blocks(blocks, places, count):
    rows = blocks[0].shape[0]
    whole = jnp.zeros((rows * count, blocks[0].shape[1]), blocks[0].dtype)
    for block, place in zip(blocks, places):
        whole = lax.dynamic_update_slice_in_dim(whole, block, place * rows, axis=0)
    return whole


def rows_of(pieces, start, stop):
    found = []
    for parts in pieces:
        offset = 0
        for part in parts:
            first, last = max(start - offset, 0), min(stop - offset, part.shape[0])
            if first < last:
                found.append(part[first:last])
            offset += part.shape[0]
    return jnp.concatenate(found, axis=0)


def split_blocks(blocks):
    own, near_x, near_y, far = blocks
    half = own.shape[0] // 2
    return (
        own,
        (far[:half], far[half:]),
        (near_x[:half], near_y[half:]),
        (near_x[half:], near_y[:half]),
    )


def send_pair(pair):
    return swap(pair[0], "row", 4, 1), swap(pair[1], "row", 4, 2)


def add_pair(pair, got):
    return add_half(pair[0], got[1]), add_half(pair[1], got[0])


def finish_sum(own, free, last):
    half = own.shape[0] // 2
    upper = add_full(own[:half], free[0], last[1])
    lower = add_full(own[half:], last[0], free[1])
    return jnp.concatenate([upper, lower], axis=0)


def row_sum(blocks, size):
    total = blocks[0].astype(jnp.float32)
    for step in range(1, size):
        total = total + to_partner(blocks[step], "row", step, size).astype(jnp.float32)
    return total


def add_full(first, second, third):
    return first.astype(jnp.float32) + second.astype(jnp.float32) + third.astype(jnp.float32)


def add_half(first, second):
    return convert_half(first.astype(jnp.float32) + second.astype(jnp.float32))


def halve(values, dim, axis, size, bit):
    own = (lax.axis_index(axis) // bit) % 2
    kept = lax.dynamic_slice_in_dim(values, own, 1, axis=dim)
    sent = lax.dynamic_slice_in_dim(values, 1 - own, 1, axis=dim)
    return add_half(kept, swap(sent, axis, size, bit))


def row_stages(values, row_size, col_size, parts=2):
    chips, rows, width = values.shape
    line = col_size // 2
    bits = [1 << k for k in reversed(range(row_size.bit_length() - 1))]
    shaped = values.reshape((2,) * len(bits) + (line, rows, width))
    part = width // parts
    pieces = []
    for place in range(parts):
        piece = shaped[..., part * place : part * (place + 1)]
        for bit in bits if place % 2 == 0 else bits[::-1]:
            piece = halve(piece, bits.index(bit), "row", row_size, bit)
        pieces.append(piece.reshape(line, rows, part))
    return jnp.concatenate(pieces, axis=-1)


def line_stage(whole, col_size):
    line = col_size // 2
    at = lax.axis_index("col") // 2
    total = lax.dynamic_index_in_dim(whole, at, 0, keepdims=False).astype(jnp.float32)
    for step in range(1, line):
        block = lax.dynamic_index_in_dim(whole, at ^ step, 0, keepdims=False)
        total = total + swap(block, "col", col_size, 2 * step).astype(jnp.float32)
    return total


def share_cores(values, col_size):
    core = lax.axis_index("col") % 2
    rows = values.shape[0] // 2
    kept = lax.dynamic_slice_in_dim(values, core * rows, rows)
    got = swap(lax.dynamic_slice_in_dim(values, (1 - core) * rows, rows), "col", col_size, 1)
    first = core == 0
    return jnp.where(first, kept, got), jnp.where(first, got, kept)


def core_half(values, core):
    half = values.shape[-1] // 2
    return lax.dynamic_slice_in_dim(values, core * half, half, axis=-1)


def with_partner(values, col_size):
    got = swap(values, "col", col_size, 1)
    return jnp.concatenate([values, got], axis=0)


def halves_with_partner(values, col_size):
    core = lax.axis_index("col") % 2
    got = swap(core_half(values, 1 - core), "col", col_size, 1)
    return jnp.concatenate([core_half(values, core), got], axis=0)


def per_device(
    tokens,
    cotangent,
    segment_numbers,
    positions,
    attention_norm_gain,
    query_matrix,
    key_value_matrix,
    output_matrix,
    output_adapter_first,
    output_adapter_second,
    feedforward_norm_gain,
    gate_matrix,
    up_matrix,
    down_matrix,
    down_adapter_first,
    down_adapter_second,
):
    row_size = lax.axis_size("row")
    col_size = lax.axis_size("col")
    devices = row_size * col_size
    row_at = lax.axis_index("row")
    tok_dev, width = tokens.shape
    group_len = segment_numbers.shape[0]
    row_total = tok_dev * NH
    query_width = query_matrix.shape[1]
    adapter_rows = output_adapter_second.shape[0]
    gain_len = attention_norm_gain.shape[0]
    start_row = lax.axis_index("col") * tok_dev
    scale = HD ** (-0.5)
    order = [partner(row_at, step) for step in range(row_size)]

    in_gathered = lax.all_gather(
        jnp.concatenate(
            [
                convert_half(query_matrix),
                convert_half(key_value_matrix),
                convert_half(
                    jnp.pad(
                        jnp.stack([attention_norm_gain, feedforward_norm_gain], axis=1),
                        ((0, 0), (0, 126)),
                    )
                ),
            ],
            axis=1,
        ),
        ("row", "col"),
        axis=0,
        tiled=True,
    )
    shard = jnp.concatenate(
        [
            convert_half(gate_matrix),
            convert_half(up_matrix),
            convert_half(down_matrix),
            convert_half(down_adapter_first),
        ],
        axis=0,
    )
    own_seg = lax.dynamic_slice_in_dim(segment_numbers, start_row, tok_dev)
    own_pos = lax.dynamic_slice_in_dim(positions, start_row, tok_dev)
    cosine, sine_part = rope_tables(own_pos)
    in_gathered, cosine, sine_part = tie(in_gathered, cosine, sine_part)
    model_rows = gate_matrix.shape[0]
    by_pairs = row_size == 4 and col_size == 8
    cot_grad = cotangent.astype(jnp.float32)
    cot_mixed = reorder(cotangent, order)
    if by_pairs:
        half = shard.shape[0] // 2
        in_gathered, upper, lower, cot_mixed = tie(
            in_gathered, shard[:half], shard[half:], cot_mixed
        )
        upper_y = swap(upper, "row", 4, 2)
        lower_x = swap(lower, "row", 4, 1)
        cot_two = swap(cot_mixed, "col", 8, 2)
        cot_four = swap(cot_mixed, "col", 8, 4)
    in_width = in_gathered.shape[1] - 128
    in_weight = in_gathered[:, :in_width]
    gains = in_gathered[:, in_width:].astype(jnp.float32)
    gain_attn = gains[:, 0]
    gain_mlp = gains[:, 1]
    inputs = tokens.astype(jnp.float32)
    normed = convert_half(rms_scale(inputs, gain_attn))
    in_pre = matrix_product(normed, in_weight)
    query_pre = in_pre[:, :query_width]
    keyval_pre = in_pre[:, query_width:]
    query_rows = convert_half(
        rotate(query_pre.reshape(tok_dev, NH, HD), cosine[:, None, :], sine_part[:, None, :])
        * scale
    ).reshape(row_total, HD)
    keyval_rows = lax.all_gather(
        jnp.concatenate(
            [
                convert_half(rotate(keyval_pre[:, :HD], cosine, sine_part)),
                convert_half(keyval_pre[:, HD:]),
            ],
            axis=1,
        ),
        "col",
        axis=0,
        tiled=True,
    )
    out_packed = jnp.concatenate(
        [
            convert_half(output_matrix),
            convert_half(output_adapter_first),
            convert_half(output_adapter_second).reshape(gain_len, -1),
            convert_half(down_adapter_second).reshape(gain_len, -1),
        ],
        axis=1,
    )
    keyval_rows, out_packed = tie(keyval_rows, out_packed)
    if by_pairs:
        (keyval_rows, out_packed, upper_y, lower_x, cot_two, cot_four, upper, lower, cot_mixed) = (
            tie(
                keyval_rows,
                out_packed,
                upper_y,
                lower_x,
                cot_two,
                cot_four,
                upper,
                lower,
                cot_mixed,
            )
        )
        upper_x = swap(upper, "row", 4, 1)
        lower_y = swap(lower, "row", 4, 2)
        cot_six = swap(cot_mixed, "col", 8, 6)
    out_gathered = lax.all_gather(out_packed, ("row", "col"), axis=0, tiled=True)
    key_rows = keyval_rows[:, :HD]
    value_rows = keyval_rows[:, HD:]
    row_index = start_row + jnp.arange(row_total, dtype=jnp.int32) // NH
    row_seg = jnp.repeat(own_seg, NH)
    key_index = jnp.arange(group_len, dtype=jnp.int32)
    allowed = (key_index[None, :] <= row_index[:, None]) & (
        (segment_numbers[None, :] == 0) | (segment_numbers[None, :] == row_seg[:, None])
    )
    scores = jnp.where(allowed, product(query_rows, key_rows, contract_last), masked_score)
    top_value = jnp.max(scores, axis=1)
    total_value = jnp.sum(jnp.exp(scores - top_value[:, None]), axis=1)
    log_norm = top_value + jnp.log(total_value)
    probs = convert_half(jnp.exp(scores - log_norm[:, None]))
    mixed_rows = matrix_product(probs, value_rows)
    head_context = convert_half(mixed_rows.reshape(tok_dev, NH * HD))
    if by_pairs:
        head_context, upper_x, lower_y, cot_six, upper_y, lower_x = tie(
            head_context, upper_x, lower_y, cot_six, upper_y, lower_x
        )
        quarter = upper_y.shape[0] // 2
        cot_mine = jnp.concatenate([cot_mixed, cot_two, cot_four, cot_six], axis=0)
        cot_other = swap(cot_mine, "col", 8, 1)
        far_upper = [swap(upper_y[:quarter], "row", 4, 1)]
        far_lower = [swap(lower_x[:quarter], "row", 4, 2)]
    rank_width = output_adapter_first.shape[1]
    out_width = width + rank_width
    upper_width = adapter_rows * width // gain_len
    out_weight = out_gathered[:, :out_width]
    out_upper = out_gathered[:, out_width : out_width + upper_width].reshape(-1, width)
    down_upper = out_gathered[:, out_width + upper_width :].reshape(-1, width)
    out_pre = matrix_product(head_context, out_weight)
    output_rank_rows = convert_half(out_pre[:, width:])
    layer_state = inputs + out_pre[:, :width] + matrix_product(output_rank_rows, out_upper)
    normed_mlp = convert_half(rms_scale(layer_state, gain_mlp))
    normed_mlp = reorder(normed_mlp, order)
    if by_pairs:
        normed_mlp, far_upper[0], far_lower[0], cot_other, upper_y, lower_x = tie(
            normed_mlp, far_upper[0], far_lower[0], cot_other, upper_y, lower_x
        )
        far_upper.append(swap(upper_y[quarter:], "row", 4, 1))
        far_lower.append(swap(lower_x[quarter:], "row", 4, 2))
        pieces = [[shard], [upper_x, lower_x], [upper_y, lower_y], [*far_upper, *far_lower]]
        places = [lax.axis_index("col") ^ (2 * step) for step in range(4)]
        cot_rows = place_blocks(
            [cot_mine[tok_dev * step : tok_dev * (step + 1)] for step in range(4)]
            + [cot_other[tok_dev * step : tok_dev * (step + 1)] for step in range(4)],
            places + [place ^ 1 for place in places],
            8,
        )
    else:
        pieces = [[shard]] + [
            [to_partner(shard, "row", step, row_size)] for step in range(1, row_size)
        ]
        cot_rows = lax.all_gather(cot_mixed, "col", axis=0, tiled=True)
    gate_weight = rows_of(pieces, 0, model_rows)
    up_weight = rows_of(pieces, model_rows, 2 * model_rows)
    down_weight = jnp.concatenate(
        [
            rows_of(pieces, 2 * model_rows, 3 * model_rows),
            rows_of(pieces, 3 * model_rows, 3 * model_rows + down_adapter_first.shape[0]),
        ],
        axis=0,
    )
    ffn_in = lax.all_gather(normed_mlp, "col", axis=0, tiled=True)
    normed_both = with_partner(normed, col_size)
    context_both = with_partner(head_context, col_size)
    rank_both = with_partner(output_rank_rows, col_size)
    cot_both = halves_with_partner(cotangent, col_size)
    rank_part = rank_width // row_size
    upper_mixed = jnp.concatenate(
        [
            lax.dynamic_slice_in_dim(reorder(down_upper, order), place * rank_part, rank_part)
            for place in order
        ],
        axis=0,
    )
    rank_rows = convert_half(product(cot_rows, upper_mixed, contract_last))
    cot_rows = jnp.concatenate([cot_rows, rank_rows], axis=1)
    hidden_grad = matrix_product(cot_rows, down_weight)
    ffn_in, hidden_grad, gate_weight, up_weight, normed_both, context_both, rank_both, cot_both = (
        tie(
            ffn_in,
            hidden_grad,
            gate_weight,
            up_weight,
            normed_both,
            context_both,
            rank_both,
            cot_both,
        )
    )
    gate_values = matrix_product(ffn_in, gate_weight)
    up_values = matrix_product(ffn_in, up_weight)
    hidden_activated = convert_half(jax.nn.gelu(gate_values, approximate=True) * up_values)
    gelu_out, gelu_pull = jax.vjp(partial(jax.nn.gelu, approximate=True), gate_values)
    gate_grad = convert_half(gelu_pull(hidden_grad * up_values)[0])
    up_grad = convert_half(hidden_grad * gelu_out)

    def blocks_of(values):
        size = values.shape[0] // row_size
        return [values[size * step : size * (step + 1)] for step in range(row_size)]

    grad_down = convert_half(product(cot_rows, hidden_activated, contract_first))
    grad_down, gate_grad, up_grad = tie(grad_down, gate_grad, up_grad)
    down_blocks = [
        jnp.concatenate([one, two], axis=0)
        for one, two in zip(blocks_of(grad_down[:width]), blocks_of(grad_down[width:]))
    ]
    half_width = width // 2

    def normed_part(start, left_gate, left_up):
        stop = start + half_width
        return convert_half(
            product(left_gate, gate_weight[start:stop], contract_last)
            + product(left_up, up_weight[start:stop], contract_last)
        )

    def col_sum(values):
        return lax.psum_scatter(values, "col", scatter_dimension=0, tiled=True)

    def down_product(start, stop):
        return convert_half(product(hidden_activated, down_weight[start:stop], contract_last))

    if row_size == 4:
        own_down, far, free, last = split_blocks(down_blocks)
        far = send_pair(far)
        first_part = normed_part(0, gate_grad, up_grad)
        *far, first_part, gate_grad, up_grad, free_x, free_y = tie(
            *far, first_part, gate_grad, up_grad, *free
        )
        first_sum = col_sum(first_part)
        last = add_pair(last, far)
        down_free = send_pair((free_x, free_y))
        down_last = send_pair(last)
        second_part = normed_part(half_width, gate_grad, up_grad)
        rank_partial = down_product(width, width + rank_width)
        *down_free, second_part, gate_grad, up_grad, rank_partial, hidden_activated = tie(
            *down_free, second_part, gate_grad, up_grad, rank_partial, hidden_activated
        )
        second_sum = col_sum(second_part)
        grad_gate = convert_half(product(ffn_in, gate_grad, contract_first))
        *down_last, grad_gate, up_grad = tie(*down_last, grad_gate, up_grad)
        own_gate, far, free, gate_last = split_blocks(blocks_of(grad_gate))
        far = send_pair(far)
        gate_free = send_pair(free)
        grad_up = convert_half(product(ffn_in, up_grad, contract_first))
        *far, grad_up = tie(*far, grad_up)
        gate_last = add_pair(gate_last, far)
        own_up, up_far, up_free, up_last = split_blocks(blocks_of(grad_up))
        gate_last = send_pair(gate_last)
        up_far = send_pair(up_far)
    else:
        first_sum = col_sum(normed_part(0, gate_grad, up_grad))
        second_sum = col_sum(normed_part(half_width, gate_grad, up_grad))
        rank_partial = down_product(width, width + rank_width)
        grad_gate = convert_half(product(ffn_in, gate_grad, contract_first))
        grad_up = convert_half(product(ffn_in, up_grad, contract_first))
        down_total = row_sum(down_blocks, row_size)
        gate_sum = row_sum(blocks_of(grad_gate), row_size)
        up_sum = row_sum(blocks_of(grad_up), row_size)
    rank_sums = col_sum(rank_partial)
    normed_grad = jnp.concatenate([first_sum, second_sum], axis=1)

    normed_grad = reorder(normed_grad, order).astype(jnp.float32)
    state_out, norm_pull = jax.vjp(rms_scale, layer_state, gain_mlp)
    state_part, grad_gain_mlp = norm_pull(normed_grad)
    state_grad = cot_grad + state_part
    attn_grad = convert_half(state_grad)
    rank_out_grad = convert_half(product(attn_grad, out_upper, contract_last))
    out_grad = jnp.concatenate([attn_grad, rank_out_grad], axis=1)
    context_grad = product(out_grad, out_weight, contract_last)
    grad_rows = convert_half(context_grad).reshape(row_total, HD)
    if row_size == 4:
        *sums, far_x, far_y, grad_rows, free_x, free_y = tie(
            *gate_free, *gate_last, *up_far, grad_rows, *up_free
        )
        gate_free, gate_last = sums[:2], sums[2:]
        up_last = send_pair(add_pair(up_last, (far_x, far_y)))
        up_free = send_pair((free_x, free_y))
    delta = jnp.sum(grad_rows.astype(jnp.float32) * mixed_rows, axis=1)
    weight_grad = product(grad_rows, value_rows, contract_last)
    score_grad = convert_half(probs.astype(jnp.float32) * (weight_grad - delta[:, None]))
    query_acc = matrix_product(score_grad, key_rows)
    query_grad = convert_half(
        unrotate(
            query_acc.reshape(tok_dev, NH, HD) * scale, cosine[:, None, :], sine_part[:, None, :]
        ).reshape(tok_dev, NH * HD)
    )
    query_grad, score_grad = tie(query_grad, score_grad)
    key_acc = product(score_grad, query_rows, contract_first)
    value_acc = product(probs, grad_rows, contract_first)
    keyval_part = jnp.concatenate([convert_half(key_acc), convert_half(value_acc)], axis=1)
    keyval_part, rank_sums = tie(keyval_part, rank_sums)
    keyval_sum = col_sum(keyval_part)
    core = lax.axis_index("col") % 2
    query_right = halves_with_partner(query_grad, col_size)
    grad_query = convert_half(product(normed_both, query_right, contract_first))
    chips = devices // 2

    def shared(values):
        return convert_half(values).reshape(chips, 2 * gain_len, -1)

    out_right = halves_with_partner(out_grad[:, :width], col_size)
    rank_right = halves_with_partner(out_grad[:, width:], col_size)
    grad_out = product(
        context_both, jnp.concatenate([out_right, rank_right], axis=1), contract_first
    )
    grad_out_upper = product(rank_both, out_right, contract_first)
    out_group = jnp.concatenate([shared(grad_out), shared(grad_out_upper)], axis=2)
    query_group = shared(grad_query)
    down_partial = down_product(0, width)
    if row_size == 4:
        *sums, keyval_sum, down_partial, out_group, query_group = tie(
            *up_free, *up_last, keyval_sum, down_partial, out_group, query_group
        )
        up_free, up_last = sums[:2], sums[2:]
    else:
        keyval_sum, down_partial = tie(keyval_sum, down_partial)
    query_lines = row_stages(query_group, row_size, col_size)
    out_lines = row_stages(out_group, row_size, col_size)
    down_rank_rows = reorder(rank_sums, order)
    summed = col_sum(down_partial)
    layer_out = convert_half(
        layer_state
        + reorder(summed, order).astype(jnp.float32)
        + matrix_product(down_rank_rows, down_upper)
    )
    keyval_sum = keyval_sum.astype(jnp.float32)
    keyval_grad = jnp.concatenate(
        [convert_half(unrotate(keyval_sum[:, :HD], cosine, sine_part)), convert_half(keyval_sum[:, HD:])],
        axis=1,
    )
    in_grad = jnp.concatenate([query_grad, keyval_grad], axis=1)
    normed_back = product(in_grad, in_weight, contract_last)
    normed_out, first_pull = jax.vjp(rms_scale, inputs, gain_attn)
    input_part, grad_gain_attn = first_pull(normed_back)
    input_grad = convert_half(state_grad + input_part)

    grad_keyval = product(
        normed_both, halves_with_partner(keyval_grad, col_size), contract_first
    )
    grad_down_upper = product(
        with_partner(down_rank_rows, col_size), cot_both, contract_first
    )
    gains = jnp.stack([grad_gain_attn, grad_gain_mlp])
    gain = lax.dynamic_index_in_dim(gains, core, 0, keepdims=False) + swap(
        lax.dynamic_index_in_dim(gains, 1 - core, 0, keepdims=False), "col", col_size, 1
    )
    keyval_group = jnp.concatenate(
        [
            shared(grad_keyval),
            shared(grad_down_upper),
            jnp.pad(shared(gain), ((0, 0), (0, 0), (0, 127))),
        ],
        axis=2,
    )
    lines = jnp.concatenate([query_lines, out_lines], axis=2)
    lines, keyval_group = tie(lines, keyval_group)
    if row_size == 4:
        lines, own_down, own_gate, own_up = tie(lines, own_down, own_gate, own_up)
        down_total = finish_sum(own_down, down_free, down_last)
        gate_sum = finish_sum(own_gate, gate_free, gate_last)
        up_sum = finish_sum(own_up, up_free, up_last)
    down_sum, rank_sum = down_total[:model_rows], down_total[model_rows:]
    first, second = share_cores(line_stage(lines, col_size), col_size)
    keyval_first, keyval_second = share_cores(
        line_stage(row_stages(keyval_group, row_size, col_size, parts=1), col_size), col_size
    )
    half_query = query_width // 2
    query_first, query_second = first[:, :half_query], second[:, :half_query]
    out_first, out_second = first[:, half_query:], second[:, half_query:]

    def joined(first, second, start, size):
        return jnp.concatenate([first[:, start : start + size], second[:, start : start + size]], axis=1)

    def joined_rows(first, second, start, size):
        return jnp.concatenate(
            [
                half[:, start : start + size].reshape(adapter_rows, -1)
                for half in (first, second)
            ],
            axis=1,
        )

    half_rank = rank_width // 2
    half_keyval = key_value_matrix.shape[1] // 2
    half_upper = upper_width // 2
    return (
        layer_out,
        input_grad,
        keyval_first[:, half_keyval + half_upper],
        joined(query_first, query_second, 0, query_width // 2),
        joined(keyval_first, keyval_second, 0, half_keyval),
        joined(out_first, out_second, 0, half_width),
        joined(out_first, out_second, half_width, half_rank),
        joined_rows(out_first, out_second, half_width + half_rank, half_upper),
        keyval_second[:, half_keyval + half_upper],
        gate_sum,
        up_sum,
        down_sum,
        rank_sum,
        joined_rows(keyval_first, keyval_second, half_keyval, half_upper),
    )


def solution(mesh):
    return jax.shard_map(
        per_device,
        mesh=mesh,
        in_specs=(
            P(("row", "col"), None),
            P(("row", "col"), None),
            P("row"),
            P("row"),
            P(("row", "col")),
            P(("row", "col"), None),
            P(("row", "col"), None),
            P(("row", "col"), None),
            P(("row", "col"), None),
            P(("row", "col"), None),
            P(("row", "col")),
            P("row", "col"),
            P("row", "col"),
            P("row", "col"),
            P("row", "col"),
            P(("row", "col"), None),
        ),
        out_specs=(
            P(("row", "col"), None),
            P(("row", "col"), None),
            P(("row", "col")),
            P(("row", "col"), None),
            P(("row", "col"), None),
            P(("row", "col"), None),
            P(("row", "col"), None),
            P(("row", "col"), None),
            P(("row", "col")),
            P("row", "col"),
            P("row", "col"),
            P("row", "col"),
            P("row", "col"),
            P(("row", "col"), None),
        ),
        check_vma=False,
    )
```

```python
from functools import partial

import jax
import jax.numpy as jnp
from jax import lax
from jax.sharding import PartitionSpec as P

MODEL_WIDTH = 2048
NH = 8
HD = 256


masked_score = -1e30
epsilon = 1e-06
contract_last = (((1,), (1,)), ((), ()))
contract_first = (((0,), (0,)), ((), ()))


def convert_half(values):
    return values.astype(jnp.bfloat16)


def product(left_side, right_side, dims):
    return lax.dot_general(left_side, right_side, dims, preferred_element_type=jnp.float32)


def matrix_product(left_side, right_side):
    return jnp.dot(left_side, right_side, preferred_element_type=jnp.float32)


def rms_scale(values, gain):
    return values * lax.rsqrt(jnp.mean(values * values, axis=-1, keepdims=True) + epsilon) * gain


def rope_tables(positions):
    half_width = HD // 2
    inverse = 10000.0 ** (-jnp.arange(half_width, dtype=jnp.float32) * 2.0 / HD)
    angles = positions.astype(jnp.float32)[:, None] * inverse[None, :]
    return (jnp.cos(angles), jnp.sin(angles))


def rotate(tensor, cosine, sine_part):
    half_width = tensor.shape[-1] // 2
    leading = tensor[..., :half_width]
    trailing = tensor[..., half_width:]
    return jnp.concatenate(
        [leading * cosine - trailing * sine_part, trailing * cosine + leading * sine_part], axis=-1
    )


def unrotate(tensor, cosine, sine_part):
    half_width = tensor.shape[-1] // 2
    leading = tensor[..., :half_width]
    trailing = tensor[..., half_width:]
    return jnp.concatenate(
        [leading * cosine + trailing * sine_part, trailing * cosine - leading * sine_part], axis=-1
    )


def swap(values, axis, size, bit):
    return lax.ppermute(values, axis, [(i, i ^ bit) for i in range(size)])


def partner(own, step):
    return own ^ step


def to_partner(values, axis, step, size):
    return lax.ppermute(values, axis, [(i, partner(i, step)) for i in range(size)])


def reorder(values, order):
    width = values.shape[-1] // len(order)
    return jnp.concatenate(
        [lax.dynamic_slice_in_dim(values, place * width, width, axis=-1) for place in order], axis=-1
    )


def tie(*values):
    return lax.optimization_barrier(values)


def place_blocks(blocks, places, count):
    rows = blocks[0].shape[0]
    whole = jnp.zeros((rows * count, blocks[0].shape[1]), blocks[0].dtype)
    for block, place in zip(blocks, places):
        whole = lax.dynamic_update_slice_in_dim(whole, block, place * rows, axis=0)
    return whole


def rows_of(pieces, start, stop):
    found = []
    for parts in pieces:
        offset = 0
        for part in parts:
            first, last = max(start - offset, 0), min(stop - offset, part.shape[0])
            if first < last:
                found.append(part[first:last])
            offset += part.shape[0]
    return jnp.concatenate(found, axis=0)


def split_blocks(blocks):
    own, near_x, near_y, far = blocks
    half = own.shape[0] // 2
    return (
        own,
        (far[:half], far[half:]),
        (near_x[:half], near_y[half:]),
        (near_x[half:], near_y[:half]),
    )


def send_pair(pair):
    return swap(pair[0], "row", 4, 1), swap(pair[1], "row", 4, 2)


def add_pair(pair, got):
    return add_half(pair[0], got[1]), add_half(pair[1], got[0])


def finish_sum(own, free, last):
    half = own.shape[0] // 2
    upper = add_full(own[:half], free[0], last[1])
    lower = add_full(own[half:], last[0], free[1])
    return jnp.concatenate([upper, lower], axis=0)


def row_sum(blocks, size):
    total = blocks[0].astype(jnp.float32)
    for step in range(1, size):
        total = total + to_partner(blocks[step], "row", step, size).astype(jnp.float32)
    return total


def add_full(first, second, third):
    return first.astype(jnp.float32) + second.astype(jnp.float32) + third.astype(jnp.float32)


def add_half(first, second):
    return convert_half(first.astype(jnp.float32) + second.astype(jnp.float32))


def halve(values, dim, axis, size, bit):
    own = (lax.axis_index(axis) // bit) % 2
    kept = lax.dynamic_slice_in_dim(values, own, 1, axis=dim)
    sent = lax.dynamic_slice_in_dim(values, 1 - own, 1, axis=dim)
    return add_half(kept, swap(sent, axis, size, bit))


def row_bits(row_size, place):
    bits = [1 << k for k in reversed(range(row_size.bit_length() - 1))]
    return bits, bits if place % 2 == 0 else bits[::-1]


def row_first(values, row_size, col_size, parts=2):
    chips, rows, width = values.shape
    bits, order = row_bits(row_size, 0)
    shaped = values.reshape((2,) * len(bits) + (col_size // 2, rows, width))
    part = width // parts
    pieces = []
    for place in range(parts):
        bits, order = row_bits(row_size, place)
        piece = shaped[..., part * place : part * (place + 1)]
        pieces.append(halve(piece, bits.index(order[0]), "row", row_size, order[0]))
    return pieces


def row_rest(pieces, row_size):
    done = []
    for place, piece in enumerate(pieces):
        bits, order = row_bits(row_size, place)
        for bit in order[1:]:
            piece = halve(piece, bits.index(bit), "row", row_size, bit)
        done.append(piece.reshape(piece.shape[-3:]))
    return jnp.concatenate(done, axis=-1)


def line_stage(whole, col_size):
    line = col_size // 2
    at = lax.axis_index("col") // 2
    total = lax.dynamic_index_in_dim(whole, at, 0, keepdims=False).astype(jnp.float32)
    for step in range(1, line):
        block = lax.dynamic_index_in_dim(whole, at ^ step, 0, keepdims=False)
        total = total + swap(block, "col", col_size, 2 * step).astype(jnp.float32)
    return total


def share_cores(values, col_size):
    core = lax.axis_index("col") % 2
    rows = values.shape[0] // 2
    kept = lax.dynamic_slice_in_dim(values, core * rows, rows)
    got = swap(lax.dynamic_slice_in_dim(values, (1 - core) * rows, rows), "col", col_size, 1)
    first = core == 0
    return jnp.where(first, kept, got), jnp.where(first, got, kept)


def core_half(values, core):
    half = values.shape[-1] // 2
    return lax.dynamic_slice_in_dim(values, core * half, half, axis=-1)


def with_partner(values, col_size):
    got = swap(values, "col", col_size, 1)
    return jnp.concatenate([values, got], axis=0)


def halves_with_partner(values, col_size):
    core = lax.axis_index("col") % 2
    got = swap(core_half(values, 1 - core), "col", col_size, 1)
    return jnp.concatenate([core_half(values, core), got], axis=0)


def per_device(
    tokens,
    cotangent,
    segment_numbers,
    positions,
    attention_norm_gain,
    query_matrix,
    key_value_matrix,
    output_matrix,
    output_adapter_first,
    output_adapter_second,
    feedforward_norm_gain,
    gate_matrix,
    up_matrix,
    down_matrix,
    down_adapter_first,
    down_adapter_second,
):
    row_size = lax.axis_size("row")
    col_size = lax.axis_size("col")
    devices = row_size * col_size
    row_at = lax.axis_index("row")
    tok_dev, width = tokens.shape
    group_len = segment_numbers.shape[0]
    row_total = tok_dev * NH
    query_width = query_matrix.shape[1]
    adapter_rows = output_adapter_second.shape[0]
    gain_len = attention_norm_gain.shape[0]
    start_row = lax.axis_index("col") * tok_dev
    scale = HD ** (-0.5)
    order = [partner(row_at, step) for step in range(row_size)]

    in_gathered = lax.all_gather(
        jnp.concatenate(
            [
                convert_half(query_matrix),
                convert_half(key_value_matrix),
                convert_half(
                    jnp.pad(
                        jnp.stack([attention_norm_gain, feedforward_norm_gain], axis=1),
                        ((0, 0), (0, 126)),
                    )
                ),
            ],
            axis=1,
        ),
        ("row", "col"),
        axis=0,
        tiled=True,
    )
    shard = jnp.concatenate(
        [
            convert_half(gate_matrix),
            convert_half(up_matrix),
            convert_half(down_matrix),
            convert_half(down_adapter_first),
        ],
        axis=0,
    )
    own_seg = lax.dynamic_slice_in_dim(segment_numbers, start_row, tok_dev)
    own_pos = lax.dynamic_slice_in_dim(positions, start_row, tok_dev)
    cosine, sine_part = rope_tables(own_pos)
    in_gathered, cosine, sine_part = tie(in_gathered, cosine, sine_part)
    model_rows = gate_matrix.shape[0]
    by_pairs = row_size == 4 and col_size == 8
    cot_grad = cotangent.astype(jnp.float32)
    cot_mixed = reorder(cotangent, order)
    if by_pairs:
        half = shard.shape[0] // 2
        in_gathered, upper, lower, cot_mixed = tie(
            in_gathered, shard[:half], shard[half:], cot_mixed
        )
        upper_y = swap(upper, "row", 4, 2)
        lower_x = swap(lower, "row", 4, 1)
        cot_two = swap(cot_mixed, "col", 8, 2)
        cot_four = swap(cot_mixed, "col", 8, 4)
    in_width = in_gathered.shape[1] - 128
    in_weight = in_gathered[:, :in_width]
    gains = in_gathered[:, in_width:].astype(jnp.float32)
    gain_attn = gains[:, 0]
    gain_mlp = gains[:, 1]
    inputs = tokens.astype(jnp.float32)
    normed = convert_half(rms_scale(inputs, gain_attn))
    in_pre = matrix_product(normed, in_weight)
    query_pre = in_pre[:, :query_width]
    keyval_pre = in_pre[:, query_width:]
    query_rows = convert_half(
        rotate(query_pre.reshape(tok_dev, NH, HD), cosine[:, None, :], sine_part[:, None, :])
        * scale
    ).reshape(row_total, HD)
    keyval_rows = lax.all_gather(
        jnp.concatenate(
            [
                convert_half(rotate(keyval_pre[:, :HD], cosine, sine_part)),
                convert_half(keyval_pre[:, HD:]),
            ],
            axis=1,
        ),
        "col",
        axis=0,
        tiled=True,
    )
    out_packed = jnp.concatenate(
        [
            convert_half(output_matrix),
            convert_half(output_adapter_first),
            convert_half(output_adapter_second).reshape(gain_len, -1),
            convert_half(down_adapter_second).reshape(gain_len, -1),
        ],
        axis=1,
    )
    keyval_rows, out_packed = tie(keyval_rows, out_packed)
    if by_pairs:
        (keyval_rows, out_packed, upper_y, lower_x, cot_two, cot_four, upper, lower, cot_mixed) = (
            tie(
                keyval_rows,
                out_packed,
                upper_y,
                lower_x,
                cot_two,
                cot_four,
                upper,
                lower,
                cot_mixed,
            )
        )
        upper_x = swap(upper, "row", 4, 1)
        lower_y = swap(lower, "row", 4, 2)
        cot_six = swap(cot_mixed, "col", 8, 6)
    out_gathered = lax.all_gather(out_packed, ("row", "col"), axis=0, tiled=True)
    key_rows = keyval_rows[:, :HD]
    value_rows = keyval_rows[:, HD:]
    row_index = start_row + jnp.arange(row_total, dtype=jnp.int32) // NH
    row_seg = jnp.repeat(own_seg, NH)
    key_index = jnp.arange(group_len, dtype=jnp.int32)
    allowed = (key_index[None, :] <= row_index[:, None]) & (
        (segment_numbers[None, :] == 0) | (segment_numbers[None, :] == row_seg[:, None])
    )
    scores = jnp.where(allowed, product(query_rows, key_rows, contract_last), masked_score)
    top_value = jnp.max(scores, axis=1)
    total_value = jnp.sum(jnp.exp(scores - top_value[:, None]), axis=1)
    log_norm = top_value + jnp.log(total_value)
    probs = convert_half(jnp.exp(scores - log_norm[:, None]))
    mixed_rows = matrix_product(probs, value_rows)
    head_context = convert_half(mixed_rows.reshape(tok_dev, NH * HD))
    if by_pairs:
        head_context, upper_x, lower_y, cot_six, upper_y, lower_x = tie(
            head_context, upper_x, lower_y, cot_six, upper_y, lower_x
        )
        quarter = upper_y.shape[0] // 2
        cot_mine = jnp.concatenate([cot_mixed, cot_two, cot_four, cot_six], axis=0)
        cot_other = swap(cot_mine, "col", 8, 1)
        far_upper = [swap(upper_y[:quarter], "row", 4, 1)]
        far_lower = [swap(lower_x[:quarter], "row", 4, 2)]
    rank_width = output_adapter_first.shape[1]
    out_width = width + rank_width
    upper_width = adapter_rows * width // gain_len
    out_weight = out_gathered[:, :out_width]
    out_upper = out_gathered[:, out_width : out_width + upper_width].reshape(-1, width)
    down_upper = out_gathered[:, out_width + upper_width :].reshape(-1, width)
    out_pre = matrix_product(head_context, out_weight)
    output_rank_rows = convert_half(out_pre[:, width:])
    layer_state = inputs + out_pre[:, :width] + matrix_product(output_rank_rows, out_upper)
    normed_mlp = convert_half(rms_scale(layer_state, gain_mlp))
    normed_mlp = reorder(normed_mlp, order)
    if by_pairs:
        normed_mlp, far_upper[0], far_lower[0], cot_other, upper_y, lower_x = tie(
            normed_mlp, far_upper[0], far_lower[0], cot_other, upper_y, lower_x
        )
        far_upper.append(swap(upper_y[quarter:], "row", 4, 1))
        far_lower.append(swap(lower_x[quarter:], "row", 4, 2))
        pieces = [[shard], [upper_x, lower_x], [upper_y, lower_y], [*far_upper, *far_lower]]
        places = [lax.axis_index("col") ^ (2 * step) for step in range(4)]
        cot_rows = place_blocks(
            [cot_mine[tok_dev * step : tok_dev * (step + 1)] for step in range(4)]
            + [cot_other[tok_dev * step : tok_dev * (step + 1)] for step in range(4)],
            places + [place ^ 1 for place in places],
            8,
        )
    else:
        pieces = [[shard]] + [
            [to_partner(shard, "row", step, row_size)] for step in range(1, row_size)
        ]
        cot_rows = lax.all_gather(cot_mixed, "col", axis=0, tiled=True)
    gate_weight = rows_of(pieces, 0, model_rows)
    up_weight = rows_of(pieces, model_rows, 2 * model_rows)
    down_weight = jnp.concatenate(
        [
            rows_of(pieces, 2 * model_rows, 3 * model_rows),
            rows_of(pieces, 3 * model_rows, 3 * model_rows + down_adapter_first.shape[0]),
        ],
        axis=0,
    )
    ffn_in = lax.all_gather(normed_mlp, "col", axis=0, tiled=True)
    normed_both = with_partner(normed, col_size)
    context_both = with_partner(head_context, col_size)
    rank_both = with_partner(output_rank_rows, col_size)
    cot_both = halves_with_partner(cotangent, col_size)
    rank_part = rank_width // row_size
    upper_mixed = jnp.concatenate(
        [
            lax.dynamic_slice_in_dim(reorder(down_upper, order), place * rank_part, rank_part)
            for place in order
        ],
        axis=0,
    )
    rank_rows = convert_half(product(cot_rows, upper_mixed, contract_last))
    cot_rows = jnp.concatenate([cot_rows, rank_rows], axis=1)
    hidden_grad = matrix_product(cot_rows, down_weight)
    ffn_in, hidden_grad, gate_weight, up_weight, normed_both, context_both, rank_both, cot_both = (
        tie(
            ffn_in,
            hidden_grad,
            gate_weight,
            up_weight,
            normed_both,
            context_both,
            rank_both,
            cot_both,
        )
    )
    gate_values = matrix_product(ffn_in, gate_weight)
    up_values = matrix_product(ffn_in, up_weight)
    hidden_activated = convert_half(jax.nn.gelu(gate_values, approximate=True) * up_values)
    gelu_out, gelu_pull = jax.vjp(partial(jax.nn.gelu, approximate=True), gate_values)
    gate_grad = convert_half(gelu_pull(hidden_grad * up_values)[0])
    up_grad = convert_half(hidden_grad * gelu_out)

    def blocks_of(values):
        size = values.shape[0] // row_size
        return [values[size * step : size * (step + 1)] for step in range(row_size)]

    grad_down = convert_half(product(cot_rows, hidden_activated, contract_first))
    grad_down, gate_grad, up_grad = tie(grad_down, gate_grad, up_grad)
    down_blocks = [
        jnp.concatenate([one, two], axis=0)
        for one, two in zip(blocks_of(grad_down[:width]), blocks_of(grad_down[width:]))
    ]
    half_width = width // 2

    def normed_part(start, left_gate, left_up):
        stop = start + half_width
        return convert_half(
            product(left_gate, gate_weight[start:stop], contract_last)
            + product(left_up, up_weight[start:stop], contract_last)
        )

    def col_sum(values):
        return lax.psum_scatter(values, "col", scatter_dimension=0, tiled=True)

    def down_product(start, stop):
        return convert_half(product(hidden_activated, down_weight[start:stop], contract_last))

    if row_size == 4:
        own_down, far, free, last = split_blocks(down_blocks)
        far = send_pair(far)
        first_part = normed_part(0, gate_grad, up_grad)
        *far, first_part, gate_grad, up_grad, free_x, free_y = tie(
            *far, first_part, gate_grad, up_grad, *free
        )
        first_sum = col_sum(first_part)
        last = add_pair(last, far)
        down_free = send_pair((free_x, free_y))
        down_last = send_pair(last)
        second_part = normed_part(half_width, gate_grad, up_grad)
        rank_partial = down_product(width, width + rank_width)
        *down_free, second_part, gate_grad, up_grad, rank_partial, hidden_activated = tie(
            *down_free, second_part, gate_grad, up_grad, rank_partial, hidden_activated
        )
        second_sum = col_sum(second_part)
        grad_gate = convert_half(product(ffn_in, gate_grad, contract_first))
        *down_last, grad_gate, up_grad = tie(*down_last, grad_gate, up_grad)
        own_gate, far, free, gate_last = split_blocks(blocks_of(grad_gate))
        far = send_pair(far)
        gate_free = send_pair(free)
        grad_up = convert_half(product(ffn_in, up_grad, contract_first))
        *far, grad_up = tie(*far, grad_up)
        gate_last = add_pair(gate_last, far)
        own_up, up_far, up_free, up_last = split_blocks(blocks_of(grad_up))
        gate_last = send_pair(gate_last)
        up_far = send_pair(up_far)
    else:
        first_sum = col_sum(normed_part(0, gate_grad, up_grad))
        second_sum = col_sum(normed_part(half_width, gate_grad, up_grad))
        rank_partial = down_product(width, width + rank_width)
        grad_gate = convert_half(product(ffn_in, gate_grad, contract_first))
        grad_up = convert_half(product(ffn_in, up_grad, contract_first))
        down_total = row_sum(down_blocks, row_size)
        gate_sum = row_sum(blocks_of(grad_gate), row_size)
        up_sum = row_sum(blocks_of(grad_up), row_size)
    rank_sums = col_sum(rank_partial)
    normed_grad = jnp.concatenate([first_sum, second_sum], axis=1)

    normed_grad = reorder(normed_grad, order).astype(jnp.float32)
    state_out, norm_pull = jax.vjp(rms_scale, layer_state, gain_mlp)
    state_part, grad_gain_mlp = norm_pull(normed_grad)
    state_grad = cot_grad + state_part
    attn_grad = convert_half(state_grad)
    rank_out_grad = convert_half(product(attn_grad, out_upper, contract_last))
    out_grad = jnp.concatenate([attn_grad, rank_out_grad], axis=1)
    context_grad = product(out_grad, out_weight, contract_last)
    grad_rows = convert_half(context_grad).reshape(row_total, HD)
    if row_size == 4:
        *sums, far_x, far_y, grad_rows, free_x, free_y = tie(
            *gate_free, *gate_last, *up_far, grad_rows, *up_free
        )
        gate_free, gate_last = sums[:2], sums[2:]
        up_last = add_pair(up_last, (far_x, far_y))
        up_free = send_pair((free_x, free_y))
    delta = jnp.sum(grad_rows.astype(jnp.float32) * mixed_rows, axis=1)
    weight_grad = product(grad_rows, value_rows, contract_last)
    score_grad = convert_half(probs.astype(jnp.float32) * (weight_grad - delta[:, None]))
    query_acc = matrix_product(score_grad, key_rows)
    query_grad = convert_half(
        unrotate(
            query_acc.reshape(tok_dev, NH, HD) * scale, cosine[:, None, :], sine_part[:, None, :]
        ).reshape(tok_dev, NH * HD)
    )
    query_grad, score_grad = tie(query_grad, score_grad)
    key_acc = product(score_grad, query_rows, contract_first)
    value_acc = product(probs, grad_rows, contract_first)
    keyval_part = jnp.concatenate([convert_half(key_acc), convert_half(value_acc)], axis=1)
    keyval_part, rank_sums = tie(keyval_part, rank_sums)
    keyval_sum = col_sum(keyval_part)
    down_partial = down_product(0, width)
    if row_size == 4:
        *up_free, down_partial, normed_both, context_both, last_x, last_y = tie(
            *up_free, down_partial, normed_both, context_both, *up_last
        )
        up_last = send_pair((last_x, last_y))
    core = lax.axis_index("col") % 2
    query_right = halves_with_partner(query_grad, col_size)
    grad_query = convert_half(product(normed_both, query_right, contract_first))
    chips = devices // 2

    def shared(values):
        return convert_half(values).reshape(chips, 2 * gain_len, -1)

    out_right = halves_with_partner(out_grad[:, :width], col_size)
    rank_right = halves_with_partner(out_grad[:, width:], col_size)
    grad_out = product(
        context_both, jnp.concatenate([out_right, rank_right], axis=1), contract_first
    )
    grad_out_upper = product(rank_both, out_right, contract_first)
    out_group = jnp.concatenate([shared(grad_out), shared(grad_out_upper)], axis=2)
    query_group = shared(grad_query)
    *up_last, keyval_sum, down_partial, out_group, query_group = tie(
        *(up_last if row_size == 4 else ()), keyval_sum, down_partial, out_group, query_group
    )
    query_parts = row_first(query_group, row_size, col_size)
    out_parts = row_first(out_group, row_size, col_size)
    down_rank_rows = reorder(rank_sums, order)
    summed = col_sum(down_partial)
    layer_out = convert_half(
        layer_state
        + reorder(summed, order).astype(jnp.float32)
        + matrix_product(down_rank_rows, down_upper)
    )
    keyval_sum = keyval_sum.astype(jnp.float32)
    keyval_grad = jnp.concatenate(
        [convert_half(unrotate(keyval_sum[:, :HD], cosine, sine_part)), convert_half(keyval_sum[:, HD:])],
        axis=1,
    )
    in_grad = jnp.concatenate([query_grad, keyval_grad], axis=1)
    grad_keyval = product(
        normed_both, halves_with_partner(keyval_grad, col_size), contract_first
    )
    in_grad, grad_keyval, *parts = tie(in_grad, grad_keyval, *query_parts, *out_parts)
    lines = jnp.concatenate([row_rest(parts[:2], row_size), row_rest(parts[2:], row_size)], axis=2)
    normed_back = product(in_grad, in_weight, contract_last)
    normed_out, first_pull = jax.vjp(rms_scale, inputs, gain_attn)
    input_part, grad_gain_attn = first_pull(normed_back)
    input_grad = convert_half(state_grad + input_part)

    grad_down_upper = product(
        with_partner(down_rank_rows, col_size), cot_both, contract_first
    )
    gains = jnp.stack([grad_gain_attn, grad_gain_mlp])
    gain = lax.dynamic_index_in_dim(gains, core, 0, keepdims=False) + swap(
        lax.dynamic_index_in_dim(gains, 1 - core, 0, keepdims=False), "col", col_size, 1
    )
    keyval_group = jnp.concatenate(
        [
            shared(grad_keyval),
            shared(grad_down_upper),
            jnp.pad(shared(gain), ((0, 0), (0, 0), (0, 127))),
        ],
        axis=2,
    )
    lines, keyval_group = tie(lines, keyval_group)
    if row_size == 4:
        lines, own_down, own_gate, own_up = tie(lines, own_down, own_gate, own_up)
        down_total = finish_sum(own_down, down_free, down_last)
        gate_sum = finish_sum(own_gate, gate_free, gate_last)
        up_sum = finish_sum(own_up, up_free, up_last)
    down_sum, rank_sum = down_total[:model_rows], down_total[model_rows:]
    first, second = share_cores(line_stage(lines, col_size), col_size)
    keyval_first, keyval_second = share_cores(
        line_stage(row_rest(row_first(keyval_group, row_size, col_size, parts=1), row_size), col_size), col_size
    )
    half_query = query_width // 2
    query_first, query_second = first[:, :half_query], second[:, :half_query]
    out_first, out_second = first[:, half_query:], second[:, half_query:]

    def joined(first, second, start, size):
        return jnp.concatenate([first[:, start : start + size], second[:, start : start + size]], axis=1)

    def joined_rows(first, second, start, size):
        return jnp.concatenate(
            [
                half[:, start : start + size].reshape(adapter_rows, -1)
                for half in (first, second)
            ],
            axis=1,
        )

    half_rank = rank_width // 2
    half_keyval = key_value_matrix.shape[1] // 2
    half_upper = upper_width // 2
    return (
        layer_out,
        input_grad,
        keyval_first[:, half_keyval + half_upper],
        joined(query_first, query_second, 0, query_width // 2),
        joined(keyval_first, keyval_second, 0, half_keyval),
        joined(out_first, out_second, 0, half_width),
        joined(out_first, out_second, half_width, half_rank),
        joined_rows(out_first, out_second, half_width + half_rank, half_upper),
        keyval_second[:, half_keyval + half_upper],
        gate_sum,
        up_sum,
        down_sum,
        rank_sum,
        joined_rows(keyval_first, keyval_second, half_keyval, half_upper),
    )


def solution(mesh):
    return jax.shard_map(
        per_device,
        mesh=mesh,
        in_specs=(
            P(("row", "col"), None),
            P(("row", "col"), None),
            P("row"),
            P("row"),
            P(("row", "col")),
            P(("row", "col"), None),
            P(("row", "col"), None),
            P(("row", "col"), None),
            P(("row", "col"), None),
            P(("row", "col"), None),
            P(("row", "col")),
            P("row", "col"),
            P("row", "col"),
            P("row", "col"),
            P("row", "col"),
            P(("row", "col"), None),
        ),
        out_specs=(
            P(("row", "col"), None),
            P(("row", "col"), None),
            P(("row", "col")),
            P(("row", "col"), None),
            P(("row", "col"), None),
            P(("row", "col"), None),
            P(("row", "col"), None),
            P(("row", "col"), None),
            P(("row", "col")),
            P("row", "col"),
            P("row", "col"),
            P("row", "col"),
            P("row", "col"),
            P(("row", "col"), None),
        ),
        check_vma=False,
    )
```

```python
from functools import partial

import jax
import jax.numpy as jnp
from jax import lax
from jax.sharding import PartitionSpec as P

MODEL_WIDTH = 2048
NH = 8
HD = 256


masked_score = -1e30
epsilon = 1e-06
contract_last = (((1,), (1,)), ((), ()))
contract_first = (((0,), (0,)), ((), ()))


def convert_half(values):
    return values.astype(jnp.bfloat16)


def product(left_side, right_side, dims):
    return lax.dot_general(left_side, right_side, dims, preferred_element_type=jnp.float32)


def matrix_product(left_side, right_side):
    return jnp.dot(left_side, right_side, preferred_element_type=jnp.float32)


def rms_scale(values, gain):
    return values * lax.rsqrt(jnp.mean(values * values, axis=-1, keepdims=True) + epsilon) * gain


def rope_tables(positions):
    half_width = HD // 2
    inverse = 10000.0 ** (-jnp.arange(half_width, dtype=jnp.float32) * 2.0 / HD)
    angles = positions.astype(jnp.float32)[:, None] * inverse[None, :]
    return (jnp.cos(angles), jnp.sin(angles))


def rotate(tensor, cosine, sine_part):
    half_width = tensor.shape[-1] // 2
    leading = tensor[..., :half_width]
    trailing = tensor[..., half_width:]
    return jnp.concatenate(
        [leading * cosine - trailing * sine_part, trailing * cosine + leading * sine_part], axis=-1
    )


def unrotate(tensor, cosine, sine_part):
    half_width = tensor.shape[-1] // 2
    leading = tensor[..., :half_width]
    trailing = tensor[..., half_width:]
    return jnp.concatenate(
        [leading * cosine + trailing * sine_part, trailing * cosine - leading * sine_part], axis=-1
    )


def swap(values, axis, size, bit):
    return lax.ppermute(values, axis, [(i, i ^ bit) for i in range(size)])


def partner(own, step):
    return own ^ step


def to_partner(values, axis, step, size):
    return lax.ppermute(values, axis, [(i, partner(i, step)) for i in range(size)])


def reorder(values, order):
    width = values.shape[-1] // len(order)
    return jnp.concatenate(
        [lax.dynamic_slice_in_dim(values, place * width, width, axis=-1) for place in order], axis=-1
    )


def tie(*values):
    return lax.optimization_barrier(values)


def place_blocks(blocks, places, count):
    rows = blocks[0].shape[0]
    whole = jnp.zeros((rows * count, blocks[0].shape[1]), blocks[0].dtype)
    for block, place in zip(blocks, places):
        whole = lax.dynamic_update_slice_in_dim(whole, block, place * rows, axis=0)
    return whole


def rows_of(pieces, start, stop):
    found = []
    for parts in pieces:
        offset = 0
        for part in parts:
            first, last = max(start - offset, 0), min(stop - offset, part.shape[0])
            if first < last:
                found.append(part[first:last])
            offset += part.shape[0]
    return jnp.concatenate(found, axis=0)


def split_blocks(blocks):
    own, near_x, near_y, far = blocks
    half = own.shape[0] // 2
    return (
        own,
        (far[:half], far[half:]),
        (near_x[:half], near_y[half:]),
        (near_x[half:], near_y[:half]),
    )


def send_pair(pair):
    return swap(pair[0], "row", 4, 1), swap(pair[1], "row", 4, 2)


def add_pair(pair, got):
    return add_half(pair[0], got[1]), add_half(pair[1], got[0])


def finish_sum(own, free, last):
    half = own.shape[0] // 2
    upper = add_full(own[:half], free[0], last[1])
    lower = add_full(own[half:], last[0], free[1])
    return jnp.concatenate([upper, lower], axis=0)


def row_sum(blocks, size):
    total = blocks[0].astype(jnp.float32)
    for step in range(1, size):
        total = total + to_partner(blocks[step], "row", step, size).astype(jnp.float32)
    return total


def add_full(first, second, third):
    return first.astype(jnp.float32) + second.astype(jnp.float32) + third.astype(jnp.float32)


def add_half(first, second):
    return convert_half(first.astype(jnp.float32) + second.astype(jnp.float32))


def halve(values, dim, axis, size, bit):
    own = (lax.axis_index(axis) // bit) % 2
    kept = lax.dynamic_slice_in_dim(values, own, 1, axis=dim)
    sent = lax.dynamic_slice_in_dim(values, 1 - own, 1, axis=dim)
    return add_half(kept, swap(sent, axis, size, bit))


def row_bits(row_size, place):
    bits = [1 << k for k in reversed(range(row_size.bit_length() - 1))]
    return bits, bits if place % 2 == 0 else bits[::-1]


def row_first(values, row_size, col_size, parts=2):
    chips, rows, width = values.shape
    bits, order = row_bits(row_size, 0)
    shaped = values.reshape((2,) * len(bits) + (col_size // 2, rows, width))
    part = width // parts
    pieces = []
    for place in range(parts):
        bits, order = row_bits(row_size, place)
        piece = shaped[..., part * place : part * (place + 1)]
        pieces.append(halve(piece, bits.index(order[0]), "row", row_size, order[0]))
    return pieces


def row_rest(pieces, row_size):
    done = []
    for place, piece in enumerate(pieces):
        bits, order = row_bits(row_size, place)
        for bit in order[1:]:
            piece = halve(piece, bits.index(bit), "row", row_size, bit)
        done.append(piece.reshape(piece.shape[-3:]))
    return jnp.concatenate(done, axis=-1)


def line_stage(whole, col_size):
    line = col_size // 2
    at = lax.axis_index("col") // 2
    total = lax.dynamic_index_in_dim(whole, at, 0, keepdims=False).astype(jnp.float32)
    for step in range(1, line):
        block = lax.dynamic_index_in_dim(whole, at ^ step, 0, keepdims=False)
        total = total + swap(block, "col", col_size, 2 * step).astype(jnp.float32)
    return total


def share_cores(values, col_size):
    core = lax.axis_index("col") % 2
    rows = values.shape[0] // 2
    kept = lax.dynamic_slice_in_dim(values, core * rows, rows)
    got = swap(lax.dynamic_slice_in_dim(values, (1 - core) * rows, rows), "col", col_size, 1)
    first = core == 0
    return jnp.where(first, kept, got), jnp.where(first, got, kept)


def core_half(values, core):
    half = values.shape[-1] // 2
    return lax.dynamic_slice_in_dim(values, core * half, half, axis=-1)


def with_partner(values, col_size):
    got = swap(values, "col", col_size, 1)
    return jnp.concatenate([values, got], axis=0)


def halves_with_partner(values, col_size):
    core = lax.axis_index("col") % 2
    got = swap(core_half(values, 1 - core), "col", col_size, 1)
    return jnp.concatenate([core_half(values, core), got], axis=0)


def per_device(
    tokens,
    cotangent,
    segment_numbers,
    positions,
    attention_norm_gain,
    query_matrix,
    key_value_matrix,
    output_matrix,
    output_adapter_first,
    output_adapter_second,
    feedforward_norm_gain,
    gate_matrix,
    up_matrix,
    down_matrix,
    down_adapter_first,
    down_adapter_second,
):
    row_size = lax.axis_size("row")
    col_size = lax.axis_size("col")
    devices = row_size * col_size
    row_at = lax.axis_index("row")
    tok_dev, width = tokens.shape
    group_len = segment_numbers.shape[0]
    row_total = tok_dev * NH
    query_width = query_matrix.shape[1]
    adapter_rows = output_adapter_second.shape[0]
    gain_len = attention_norm_gain.shape[0]
    start_row = lax.axis_index("col") * tok_dev
    scale = HD ** (-0.5)
    order = [partner(row_at, step) for step in range(row_size)]

    in_gathered = lax.all_gather(
        jnp.concatenate(
            [
                convert_half(query_matrix),
                convert_half(key_value_matrix),
                convert_half(
                    jnp.pad(
                        jnp.stack([attention_norm_gain, feedforward_norm_gain], axis=1),
                        ((0, 0), (0, 126)),
                    )
                ),
            ],
            axis=1,
        ),
        ("row", "col"),
        axis=0,
        tiled=True,
    )
    shard = jnp.concatenate(
        [
            convert_half(gate_matrix),
            convert_half(up_matrix),
            convert_half(down_matrix),
            convert_half(down_adapter_first),
        ],
        axis=0,
    )
    own_seg = lax.dynamic_slice_in_dim(segment_numbers, start_row, tok_dev)
    own_pos = lax.dynamic_slice_in_dim(positions, start_row, tok_dev)
    cosine, sine_part = rope_tables(own_pos)
    in_gathered, cosine, sine_part = tie(in_gathered, cosine, sine_part)
    model_rows = gate_matrix.shape[0]
    by_pairs = row_size == 4 and col_size == 8
    cot_grad = cotangent.astype(jnp.float32)
    cot_mixed = reorder(cotangent, order)
    if by_pairs:
        half = shard.shape[0] // 2
        in_gathered, upper, lower, cot_mixed = tie(
            in_gathered, shard[:half], shard[half:], cot_mixed
        )
        upper_y = swap(upper, "row", 4, 2)
        lower_x = swap(lower, "row", 4, 1)
        cot_two = swap(cot_mixed, "col", 8, 2)
        cot_four = swap(cot_mixed, "col", 8, 4)
    in_width = in_gathered.shape[1] - 128
    in_weight = in_gathered[:, :in_width]
    gains = in_gathered[:, in_width:].astype(jnp.float32)
    gain_attn = gains[:, 0]
    gain_mlp = gains[:, 1]
    inputs = tokens.astype(jnp.float32)
    normed = convert_half(rms_scale(inputs, gain_attn))
    in_pre = matrix_product(normed, in_weight)
    query_pre = in_pre[:, :query_width]
    keyval_pre = in_pre[:, query_width:]
    query_rows = convert_half(
        rotate(query_pre.reshape(tok_dev, NH, HD), cosine[:, None, :], sine_part[:, None, :])
        * scale
    ).reshape(row_total, HD)
    keyval_rows = lax.all_gather(
        jnp.concatenate(
            [
                convert_half(rotate(keyval_pre[:, :HD], cosine, sine_part)),
                convert_half(keyval_pre[:, HD:]),
            ],
            axis=1,
        ),
        "col",
        axis=0,
        tiled=True,
    )
    out_packed = jnp.concatenate(
        [
            convert_half(output_matrix),
            convert_half(output_adapter_first),
            convert_half(output_adapter_second).reshape(gain_len, -1),
            convert_half(down_adapter_second).reshape(gain_len, -1),
        ],
        axis=1,
    )
    keyval_rows, out_packed = tie(keyval_rows, out_packed)
    if by_pairs:
        (keyval_rows, out_packed, upper_y, lower_x, cot_two, cot_four, upper, lower, cot_mixed) = (
            tie(
                keyval_rows,
                out_packed,
                upper_y,
                lower_x,
                cot_two,
                cot_four,
                upper,
                lower,
                cot_mixed,
            )
        )
        upper_x = swap(upper, "row", 4, 1)
        lower_y = swap(lower, "row", 4, 2)
        cot_six = swap(cot_mixed, "col", 8, 6)
    out_gathered = lax.all_gather(out_packed, ("row", "col"), axis=0, tiled=True)
    key_rows = keyval_rows[:, :HD]
    value_rows = keyval_rows[:, HD:]
    row_index = start_row + jnp.arange(row_total, dtype=jnp.int32) // NH
    row_seg = jnp.repeat(own_seg, NH)
    key_index = jnp.arange(group_len, dtype=jnp.int32)
    allowed = (key_index[None, :] <= row_index[:, None]) & (
        (segment_numbers[None, :] == 0) | (segment_numbers[None, :] == row_seg[:, None])
    )
    scores = jnp.where(allowed, product(query_rows, key_rows, contract_last), masked_score)
    top_value = jnp.max(scores, axis=1)
    total_value = jnp.sum(jnp.exp(scores - top_value[:, None]), axis=1)
    log_norm = top_value + jnp.log(total_value)
    probs = convert_half(jnp.exp(scores - log_norm[:, None]))
    mixed_rows = matrix_product(probs, value_rows)
    head_context = convert_half(mixed_rows.reshape(tok_dev, NH * HD))
    if by_pairs:
        head_context, upper_x, lower_y, cot_six, upper_y, lower_x = tie(
            head_context, upper_x, lower_y, cot_six, upper_y, lower_x
        )
        quarter = upper_y.shape[0] // 2
        cot_mine = jnp.concatenate([cot_mixed, cot_two, cot_four, cot_six], axis=0)
        cot_other = swap(cot_mine, "col", 8, 1)
        far_upper = [swap(upper_y[:quarter], "row", 4, 1)]
        far_lower = [swap(lower_x[:quarter], "row", 4, 2)]
    rank_width = output_adapter_first.shape[1]
    out_width = width + rank_width
    upper_width = adapter_rows * width // gain_len
    out_weight = out_gathered[:, :out_width]
    out_upper = out_gathered[:, out_width : out_width + upper_width].reshape(-1, width)
    down_upper = out_gathered[:, out_width + upper_width :].reshape(-1, width)
    out_pre = matrix_product(head_context, out_weight)
    output_rank_rows = convert_half(out_pre[:, width:])
    layer_state = inputs + out_pre[:, :width] + matrix_product(output_rank_rows, out_upper)
    normed_mlp = convert_half(rms_scale(layer_state, gain_mlp))
    normed_mlp = reorder(normed_mlp, order)
    if by_pairs:
        normed_mlp, far_upper[0], far_lower[0], cot_other, upper_y, lower_x = tie(
            normed_mlp, far_upper[0], far_lower[0], cot_other, upper_y, lower_x
        )
        far_upper.append(swap(upper_y[quarter:], "row", 4, 1))
        far_lower.append(swap(lower_x[quarter:], "row", 4, 2))
        pieces = [[shard], [upper_x, lower_x], [upper_y, lower_y], [*far_upper, *far_lower]]
        places = [lax.axis_index("col") ^ (2 * step) for step in range(4)]
        cot_rows = place_blocks(
            [cot_mine[tok_dev * step : tok_dev * (step + 1)] for step in range(4)]
            + [cot_other[tok_dev * step : tok_dev * (step + 1)] for step in range(4)],
            places + [place ^ 1 for place in places],
            8,
        )
    else:
        pieces = [[shard]] + [
            [to_partner(shard, "row", step, row_size)] for step in range(1, row_size)
        ]
        cot_rows = lax.all_gather(cot_mixed, "col", axis=0, tiled=True)
    gate_weight = rows_of(pieces, 0, model_rows)
    up_weight = rows_of(pieces, model_rows, 2 * model_rows)
    down_weight = jnp.concatenate(
        [
            rows_of(pieces, 2 * model_rows, 3 * model_rows),
            rows_of(pieces, 3 * model_rows, 3 * model_rows + down_adapter_first.shape[0]),
        ],
        axis=0,
    )
    ffn_in = lax.all_gather(normed_mlp, "col", axis=0, tiled=True)
    normed_both = with_partner(normed, col_size)
    context_both = with_partner(head_context, col_size)
    rank_both = with_partner(output_rank_rows, col_size)
    cot_both = halves_with_partner(cotangent, col_size)
    rank_part = rank_width // row_size
    upper_mixed = jnp.concatenate(
        [
            lax.dynamic_slice_in_dim(reorder(down_upper, order), place * rank_part, rank_part)
            for place in order
        ],
        axis=0,
    )
    rank_rows = convert_half(product(cot_rows, upper_mixed, contract_last))
    cot_rows = jnp.concatenate([cot_rows, rank_rows], axis=1)
    hidden_grad = matrix_product(cot_rows, down_weight)
    ffn_in, hidden_grad, gate_weight, up_weight, normed_both, context_both, rank_both, cot_both = (
        tie(
            ffn_in,
            hidden_grad,
            gate_weight,
            up_weight,
            normed_both,
            context_both,
            rank_both,
            cot_both,
        )
    )
    gate_values = matrix_product(ffn_in, gate_weight)
    up_values = matrix_product(ffn_in, up_weight)
    hidden_activated = convert_half(jax.nn.gelu(gate_values, approximate=True) * up_values)
    gelu_out, gelu_pull = jax.vjp(partial(jax.nn.gelu, approximate=True), gate_values)
    gate_grad = convert_half(gelu_pull(hidden_grad * up_values)[0])
    up_grad = convert_half(hidden_grad * gelu_out)

    def blocks_of(values):
        size = values.shape[0] // row_size
        return [values[size * step : size * (step + 1)] for step in range(row_size)]

    grad_down = convert_half(product(cot_rows, hidden_activated, contract_first))
    grad_down, gate_grad, up_grad = tie(grad_down, gate_grad, up_grad)
    down_blocks = [
        jnp.concatenate([one, two], axis=0)
        for one, two in zip(blocks_of(grad_down[:width]), blocks_of(grad_down[width:]))
    ]
    half_width = width // 2

    def normed_part(start, left_gate, left_up):
        stop = start + half_width
        return convert_half(
            product(left_gate, gate_weight[start:stop], contract_last)
            + product(left_up, up_weight[start:stop], contract_last)
        )

    def col_sum(values):
        return lax.psum_scatter(values, "col", scatter_dimension=0, tiled=True)

    def down_product(start, stop):
        return convert_half(product(hidden_activated, down_weight[start:stop], contract_last))

    if row_size == 4:
        own_down, far, free, last = split_blocks(down_blocks)
        far = send_pair(far)
        first_part = normed_part(0, gate_grad, up_grad)
        *far, first_part, gate_grad, up_grad, free_x, free_y = tie(
            *far, first_part, gate_grad, up_grad, *free
        )
        first_sum = col_sum(first_part)
        last = add_pair(last, far)
        down_free = send_pair((free_x, free_y))
        down_last = send_pair(last)
        second_part = normed_part(half_width, gate_grad, up_grad)
        rank_partial = down_product(width, width + rank_width)
        *down_free, second_part, gate_grad, up_grad, rank_partial, hidden_activated = tie(
            *down_free, second_part, gate_grad, up_grad, rank_partial, hidden_activated
        )
        second_sum = col_sum(second_part)
        grad_gate = convert_half(product(ffn_in, gate_grad, contract_first))
        *down_last, grad_gate, up_grad = tie(*down_last, grad_gate, up_grad)
        own_gate, far, free, gate_last = split_blocks(blocks_of(grad_gate))
        far = send_pair(far)
        gate_free = send_pair(free)
        grad_up = convert_half(product(ffn_in, up_grad, contract_first))
        *far, grad_up = tie(*far, grad_up)
        gate_last = add_pair(gate_last, far)
        own_up, up_far, up_free, up_last = split_blocks(blocks_of(grad_up))
        gate_last = send_pair(gate_last)
        up_far = send_pair(up_far)
    else:
        first_sum = col_sum(normed_part(0, gate_grad, up_grad))
        second_sum = col_sum(normed_part(half_width, gate_grad, up_grad))
        rank_partial = down_product(width, width + rank_width)
        grad_gate = convert_half(product(ffn_in, gate_grad, contract_first))
        grad_up = convert_half(product(ffn_in, up_grad, contract_first))
        down_total = row_sum(down_blocks, row_size)
        gate_sum = row_sum(blocks_of(grad_gate), row_size)
        up_sum = row_sum(blocks_of(grad_up), row_size)
    rank_sums = col_sum(rank_partial)
    normed_grad = jnp.concatenate([first_sum, second_sum], axis=1)

    normed_grad = reorder(normed_grad, order).astype(jnp.float32)
    state_out, norm_pull = jax.vjp(rms_scale, layer_state, gain_mlp)
    state_part, grad_gain_mlp = norm_pull(normed_grad)
    state_grad = cot_grad + state_part
    attn_grad = convert_half(state_grad)
    rank_out_grad = convert_half(product(attn_grad, out_upper, contract_last))
    out_grad = jnp.concatenate([attn_grad, rank_out_grad], axis=1)
    context_grad = product(out_grad, out_weight, contract_last)
    grad_rows = convert_half(context_grad).reshape(row_total, HD)
    down_partial = down_product(0, width)
    if row_size == 4:
        *sums, far_x, far_y, grad_rows, free_x, free_y, down_partial = tie(
            *gate_free, *gate_last, *up_far, grad_rows, *up_free, down_partial
        )
        gate_free, gate_last = sums[:2], sums[2:]
        up_last = add_pair(up_last, (far_x, far_y))
        up_free = send_pair((free_x, free_y))
    delta = jnp.sum(grad_rows.astype(jnp.float32) * mixed_rows, axis=1)
    weight_grad = product(grad_rows, value_rows, contract_last)
    score_grad = convert_half(probs.astype(jnp.float32) * (weight_grad - delta[:, None]))
    query_acc = matrix_product(score_grad, key_rows)
    query_grad = convert_half(
        unrotate(
            query_acc.reshape(tok_dev, NH, HD) * scale, cosine[:, None, :], sine_part[:, None, :]
        ).reshape(tok_dev, NH * HD)
    )
    query_grad, score_grad = tie(query_grad, score_grad)
    key_acc = product(score_grad, query_rows, contract_first)
    value_acc = product(probs, grad_rows, contract_first)
    keyval_part = jnp.concatenate([convert_half(key_acc), convert_half(value_acc)], axis=1)
    keyval_part, rank_sums = tie(keyval_part, rank_sums)
    keyval_sum = col_sum(keyval_part)
    if row_size == 4:
        *up_free, down_partial, normed_both, context_both, last_x, last_y = tie(
            *up_free, down_partial, normed_both, context_both, *up_last
        )
        up_last = send_pair((last_x, last_y))
    core = lax.axis_index("col") % 2
    query_right = halves_with_partner(query_grad, col_size)
    grad_query = convert_half(product(normed_both, query_right, contract_first))
    chips = devices // 2

    def shared(values):
        return convert_half(values).reshape(chips, 2 * gain_len, -1)

    out_right = halves_with_partner(out_grad[:, :width], col_size)
    rank_right = halves_with_partner(out_grad[:, width:], col_size)
    grad_out = product(
        context_both, jnp.concatenate([out_right, rank_right], axis=1), contract_first
    )
    grad_out_upper = product(rank_both, out_right, contract_first)
    out_group = jnp.concatenate([shared(grad_out), shared(grad_out_upper)], axis=2)
    query_group = shared(grad_query)
    *up_last, keyval_sum, down_partial, out_group, query_group = tie(
        *(up_last if row_size == 4 else ()), keyval_sum, down_partial, out_group, query_group
    )
    query_parts = row_first(query_group, row_size, col_size)
    out_parts = row_first(out_group, row_size, col_size)
    down_rank_rows = reorder(rank_sums, order)
    summed = col_sum(down_partial)
    layer_out = convert_half(
        layer_state
        + reorder(summed, order).astype(jnp.float32)
        + matrix_product(down_rank_rows, down_upper)
    )
    keyval_sum = keyval_sum.astype(jnp.float32)
    keyval_grad = jnp.concatenate(
        [convert_half(unrotate(keyval_sum[:, :HD], cosine, sine_part)), convert_half(keyval_sum[:, HD:])],
        axis=1,
    )
    in_grad = jnp.concatenate([query_grad, keyval_grad], axis=1)
    grad_keyval = product(
        normed_both, halves_with_partner(keyval_grad, col_size), contract_first
    )
    in_grad, grad_keyval, *parts = tie(in_grad, grad_keyval, *query_parts, *out_parts)
    lines = jnp.concatenate([row_rest(parts[:2], row_size), row_rest(parts[2:], row_size)], axis=2)
    normed_back = product(in_grad, in_weight, contract_last)
    normed_out, first_pull = jax.vjp(rms_scale, inputs, gain_attn)
    input_part, grad_gain_attn = first_pull(normed_back)
    input_grad = convert_half(state_grad + input_part)

    grad_down_upper = product(
        with_partner(down_rank_rows, col_size), cot_both, contract_first
    )
    gains = jnp.stack([grad_gain_attn, grad_gain_mlp])
    gain = lax.dynamic_index_in_dim(gains, core, 0, keepdims=False) + swap(
        lax.dynamic_index_in_dim(gains, 1 - core, 0, keepdims=False), "col", col_size, 1
    )
    keyval_group = jnp.concatenate(
        [
            shared(grad_keyval),
            shared(grad_down_upper),
            jnp.pad(shared(gain), ((0, 0), (0, 0), (0, 127))),
        ],
        axis=2,
    )
    lines, keyval_group = tie(lines, keyval_group)
    if row_size == 4:
        lines, own_down, own_gate, own_up = tie(lines, own_down, own_gate, own_up)
        down_total = finish_sum(own_down, down_free, down_last)
        gate_sum = finish_sum(own_gate, gate_free, gate_last)
        up_sum = finish_sum(own_up, up_free, up_last)
    down_sum, rank_sum = down_total[:model_rows], down_total[model_rows:]
    first, second = share_cores(line_stage(lines, col_size), col_size)
    keyval_first, keyval_second = share_cores(
        line_stage(row_rest(row_first(keyval_group, row_size, col_size, parts=1), row_size), col_size), col_size
    )
    half_query = query_width // 2
    query_first, query_second = first[:, :half_query], second[:, :half_query]
    out_first, out_second = first[:, half_query:], second[:, half_query:]

    def joined(first, second, start, size):
        return jnp.concatenate([first[:, start : start + size], second[:, start : start + size]], axis=1)

    def joined_rows(first, second, start, size):
        return jnp.concatenate(
            [
                half[:, start : start + size].reshape(adapter_rows, -1)
                for half in (first, second)
            ],
            axis=1,
        )

    half_rank = rank_width // 2
    half_keyval = key_value_matrix.shape[1] // 2
    half_upper = upper_width // 2
    return (
        layer_out,
        input_grad,
        keyval_first[:, half_keyval + half_upper],
        joined(query_first, query_second, 0, query_width // 2),
        joined(keyval_first, keyval_second, 0, half_keyval),
        joined(out_first, out_second, 0, half_width),
        joined(out_first, out_second, half_width, half_rank),
        joined_rows(out_first, out_second, half_width + half_rank, half_upper),
        keyval_second[:, half_keyval + half_upper],
        gate_sum,
        up_sum,
        down_sum,
        rank_sum,
        joined_rows(keyval_first, keyval_second, half_keyval, half_upper),
    )


def solution(mesh):
    return jax.shard_map(
        per_device,
        mesh=mesh,
        in_specs=(
            P(("row", "col"), None),
            P(("row", "col"), None),
            P("row"),
            P("row"),
            P(("row", "col")),
            P(("row", "col"), None),
            P(("row", "col"), None),
            P(("row", "col"), None),
            P(("row", "col"), None),
            P(("row", "col"), None),
            P(("row", "col")),
            P("row", "col"),
            P("row", "col"),
            P("row", "col"),
            P("row", "col"),
            P(("row", "col"), None),
        ),
        out_specs=(
            P(("row", "col"), None),
            P(("row", "col"), None),
            P(("row", "col")),
            P(("row", "col"), None),
            P(("row", "col"), None),
            P(("row", "col"), None),
            P(("row", "col"), None),
            P(("row", "col"), None),
            P(("row", "col")),
            P("row", "col"),
            P("row", "col"),
            P("row", "col"),
            P("row", "col"),
            P(("row", "col"), None),
        ),
        check_vma=False,
    )
```
